256 devices in a mesh: rec: 16 (over z, core), tm: 16 (over y, x).
Axes of the slice: x: 4, y: 4, z: 8, core: 2. Of those that a mesh axis runs over, the one named last changes fastest.
Arguments:
- frames: bfloat16 [65536, 1280], P(('rec', 'tm')), parts along dimension 0, may hold values from -50 to 50
- w_query: bfloat16 [1280, 1280], replicated, may hold values from -1 to 1
- w_kv: bfloat16 [1280, 2560], replicated, may hold values from -1 to 1
- w_out: bfloat16 [1280, 1280], replicated, may hold values from -0.15625 to 0.15625
- norm_gain: float32 [1280], replicated, may hold values from 0.5 to 1.5
- rand_owner: int32 [512, 3], P(('rec', 'tm')), parts along dimension 0, may hold values from 0 to 15, all different within a row; in each aligned block of 2 rows (0 to 1, 2 to 3, ...) at most 2 rows name the same one
- rand_slot: int32 [512, 3], P(('rec', 'tm')), parts along dimension 0, may hold values from 0 to 1
- global_pos: int32 [2048], P('rec'), parts along dimension 0, may hold values from 0 to 4095
- length: int32 [16], P('rec'), parts along dimension 0, may hold values from 16 to 32
Outputs:
- pooled_out: bfloat16 [16384, 1280], P(('rec', 'tm')), parts along dimension 0
The draws below stay inside these ranges and needn't reach their ends.
There are 16 independent parts, one for each index of `rec`. The reference program is written for one: setup_inputs(seed, part) draws one part's arguments, and reference() takes and returns one part's arrays. A program takes and returns all parts, laid end to end along the dimension named above; an argument that names none is the same for every part. Nothing has to cross between parts.
Inputs may be any that keep to these rules, and one draw needn't show every extreme that they name: `rand_owner`: the 3 owners of one query block differ; over the query blocks of one time shard no owner is named more than 2 times, a bound that some block reaches.
All inputs are finite; a program needn't handle non-finite values.
Results may differ from the reference program's by a relative error of at most 0.012.
The reference program's roundings to bfloat16 on the way count: a program that leaves them out, or rounds other values in their place, can miss the bound.
Values may be sent and summed in bfloat16 or wider, within the bound.
No kernel may reach another device: no remote copies, remote signals or barrier semaphores. Data moves between devices by JAX's collectives and lax.ppermute only.
A program may use at most 128 MiB of HBM per device.

```python
import math
import jax
import jax.numpy as jnp
import numpy as np
from jax import lax

D = 1280
HEADS = 20
BLOCK = 128
PICKS = 3
POOL = 4
GLOBALS = 128
QB_DEV = 2
SHARDS = 16
QBLOCKS = 32
FRAMES = 4096
CAP = 2


def draw_frames(key, part):
    normal_draw = jnp.clip(jax.random.normal(jax.random.fold_in(key, 31), (FRAMES, D), jnp.float32), -4.0, 4.0)
    return normal_draw.astype(jnp.bfloat16)


def query_base(key):
    return jnp.clip(jax.random.normal(jax.random.fold_in(key, 41), (D, D), jnp.float32), -4.0, 4.0) / jnp.sqrt(jnp.float32(D))


def draw_w_query(key, part):
    return query_base(key).astype(jnp.bfloat16)


def draw_w_kv(key, part):
    fresh_draw = jnp.clip(jax.random.normal(jax.random.fold_in(key, 42), (D, 2 * D), jnp.float32), -4.0, 4.0) / jnp.sqrt(jnp.float32(D))
    return fresh_draw.astype(jnp.bfloat16)


def draw_global_pos(key, part):
    shard_rows = QB_DEV * BLOCK
    spread_pos = jax.random.randint(jax.random.fold_in(key, 51), (GLOBALS,), 0, FRAMES, jnp.int32)
    home_shard = jax.random.randint(jax.random.fold_in(key, 52), (), 0, max(1, SHARDS // 2), jnp.int32)
    packed_pos = home_shard * shard_rows + jax.random.randint(jax.random.fold_in(key, 53), (GLOBALS,), 0, shard_rows, jnp.int32)
    return jnp.where(part % 4 == 0, packed_pos, spread_pos).astype(jnp.int32)


def set_ends(values, rng, smallest, high):
    shape = values.shape
    index_at = [jax.random.randint(jax.random.fold_in(rng, axis), (), 0, shape[axis]) for axis in range(len(shape))]
    values = values.at[tuple(index_at)].set(smallest)
    longest = shape.index(max(shape))
    index_at[longest] = (index_at[longest] + 1) % shape[longest]
    return values.at[tuple(index_at)].set(high)


def routed_block(stream_key, own, number, rows, number_of, top, bound, slope):
    ranking = jax.random.permutation(stream_key, number_of)
    heavy_load, ordinary = shares(number_of, rows * top, bound, slope, True), shares(number_of, rows * top, bound, slope, False)
    places = jnp.arange(number_of)

    def named(lengths, turn):
        used = int((lengths > 0).sum())
        fixed = max(1, used // 4)
        moved = fixed + (places - fixed + turn * (used - fixed)) % max(1, number_of - fixed)
        return jnp.zeros((number_of,), jnp.int32).at[ranking[jnp.where(places < fixed, places, moved)]].set(jnp.asarray(lengths, jnp.int32))

    lengths = jnp.where(number % 4 == 0, named(heavy_load, number // 4), named(ordinary, number - number // 4 - 1))
    mixed = jax.random.permutation(jax.random.fold_in(own, 3), number_of)
    giver, sink = mixed[0:number_of // 2 * 2:2], mixed[1:number_of // 2 * 2:2]
    room = jnp.minimum(lengths[giver] - 1, bound - lengths[sink]) // 2
    room = jnp.where((giver == ranking[0]) | (sink == ranking[0]) | (lengths[sink] == 0), 0, jnp.maximum(room, 0))
    moved = jax.random.randint(jax.random.fold_in(own, 4), (number_of // 2,), 0, 1 << 20) % (room + 1)
    lengths = lengths.at[giver].add(-moved).at[sink].add(moved)
    items = jnp.searchsorted(jnp.cumsum(lengths), jnp.arange(rows * top), side="right").astype(jnp.int32)
    table = items.reshape(top, rows).T
    table = table[jax.random.permutation(jax.random.fold_in(own, 1), rows)]
    turn = jax.random.randint(jax.random.fold_in(own, 2), (rows, 1), 0, top)
    return jnp.take_along_axis(table, (jnp.arange(top)[None, :] + turn) % top, axis=1)


def shares(count, total, bound, skew, full):
    loads = [(1 << 20) // math.isqrt(rank ** skew) + 1 for rank in range(1, count + 1)]
    largest = bound if full else min(bound, max(-(-total // count), total * loads[0] // sum(loads)))
    least = 1 if total - largest >= count - 1 else 0
    given, spare = [largest] + [least] * (count - 1), total - largest - least * (count - 1)
    while spare > 0:
        movable = [i for i in range(1, count) if given[i] < largest] or [i for i in range(1, count) if given[i] < bound]
        mass, left = sum([loads[i] for i in movable]), spare
        for i in movable:
            more = min(bound - given[i], max(1, left * loads[i] // mass), spare)
            given[i] = given[i] + more
            spare = spare - more
    return np.array(given)


def scatter_about(own_key, dims, width, most, held_as=jnp.bfloat16):
    values = width * jax.random.normal(own_key, dims, jnp.float32)
    return jnp.clip(values, min=-most, max=most).astype(held_as)


def setup_inputs(seed: int = 0, part: int = 0) -> dict:
    splits = jax.random.split(jax.random.key(seed), 10)
    own_keys = jax.random.split(jax.random.fold_in(splits[9], part), 10)
    frames = draw_frames(jax.random.fold_in(jax.random.fold_in(splits[9], part), 71), part)
    w_query = draw_w_query(jax.random.fold_in(splits[9], 71), part)
    w_kv = draw_w_kv(jax.random.fold_in(splits[9], 71), part)
    w_out = scatter_about(splits[3], (D, D), D ** -0.5, 0.15625)
    norm_gain = jnp.clip(1.0 + 0.1 * jax.random.normal(splits[4], (D,), jnp.float32), 0.5, 1.5)
    rand_owner_keys = jax.random.split(jax.random.fold_in(own_keys[5], 1), QBLOCKS // QB_DEV)
    rand_owner_turns = jax.random.permutation(jax.random.fold_in(own_keys[5], 3), QBLOCKS // QB_DEV)
    rand_owner = jax.vmap(lambda own, number: routed_block(jax.random.fold_in(own_keys[5], 2), own, number, QB_DEV, SHARDS, PICKS, CAP, 2))(rand_owner_keys, rand_owner_turns).reshape((QBLOCKS, PICKS))
    rand_slot = set_ends(jax.random.randint(own_keys[6], (QBLOCKS, PICKS), 0, QB_DEV), jax.random.fold_in(own_keys[6], 1), 0, QB_DEV - 1).astype(jnp.int32)
    global_pos = draw_global_pos(jax.random.fold_in(jax.random.fold_in(splits[9], part), 71), part)
    length = jax.random.randint(own_keys[8], (1,), QBLOCKS // 2, QBLOCKS + 1).astype(jnp.int32)
    return {"frames": frames, "w_query": w_query, "w_kv": w_kv, "w_out": w_out, "norm_gain": norm_gain, "rand_owner": rand_owner, "rand_slot": rand_slot, "global_pos": global_pos, "length": length}


def attend(query_rows, key_rows, key_live, global_keys, global_live, head_count):
    group_size, block_rows, model_width = query_rows.shape
    head_size = model_width // head_count
    score_scale = head_size ** (-0.5)
    query_h = query_rows.astype(jnp.float32).reshape(group_size, block_rows, head_count, head_size)
    key_h = key_rows[..., :model_width].astype(jnp.float32).reshape(group_size, -1, head_count, head_size)
    value_h = key_rows[..., model_width:].astype(jnp.float32).reshape(group_size, -1, head_count, head_size)
    global_key_h = global_keys[:, :model_width].astype(jnp.float32).reshape(-1, head_count, head_size)
    global_value_h = global_keys[:, model_width:].astype(jnp.float32).reshape(-1, head_count, head_size)
    near_scores = jnp.einsum('bihd,bjhd->bhij', query_h, key_h) * score_scale
    far_scores = jnp.einsum('bihd,jhd->bhij', query_h, global_key_h) * score_scale
    near_scores = jnp.where(key_live[:, None, None, :], near_scores, -1e+30)
    far_scores = jnp.where(global_live[None, None, None, :], far_scores, -1e+30)
    row_max = jnp.maximum(lax.optimization_barrier(jnp.max(near_scores, axis=-1)), lax.optimization_barrier(jnp.max(far_scores, axis=-1)))[..., None]
    near_exp = jnp.exp(near_scores - row_max)
    far_exp = jnp.exp(far_scores - row_max)
    row_total = lax.optimization_barrier(jnp.sum(near_exp, axis=-1, keepdims=True)) + lax.optimization_barrier(jnp.sum(far_exp, axis=-1, keepdims=True))
    near_weight = (near_exp / row_total).astype(jnp.bfloat16).astype(jnp.float32)
    far_weight = (far_exp / row_total).astype(jnp.bfloat16).astype(jnp.float32)
    context = jnp.einsum('bhij,bjhd->bihd', near_weight, value_h)
    context = context + jnp.einsum('bhij,jhd->bihd', far_weight, global_value_h)
    return context.reshape(group_size, block_rows, model_width).astype(jnp.bfloat16)

def reference(frames, w_query, w_kv, w_out, norm_gain, rand_owner, rand_slot, global_pos, length):
    model_width = frames.shape[1]
    query_rows = jnp.dot(frames, w_query, preferred_element_type=jnp.float32).astype(jnp.bfloat16)
    keyval = jnp.dot(frames, w_kv, preferred_element_type=jnp.float32).astype(jnp.bfloat16)
    live_blocks = length[0]
    zero_rim = jnp.zeros((BLOCK, 2 * model_width), jnp.bfloat16)
    padded = jnp.concatenate([zero_rim, keyval, zero_rim], axis=0)
    kv_blocks = keyval.reshape(QBLOCKS, BLOCK, 2 * model_width)
    global_keys = jnp.take(keyval, global_pos, axis=0)
    global_live = global_pos < live_blocks * BLOCK
    random_ids = (rand_owner * QB_DEV + rand_slot).astype(jnp.int32)

    def one_block(index):
        window = lax.dynamic_slice_in_dim(padded, index * BLOCK, 3 * BLOCK, 0)
        picked = jnp.take(kv_blocks, random_ids[index], axis=0).reshape(PICKS * BLOCK, 2 * model_width)
        key_rows = jnp.concatenate([window, picked], axis=0)[None]
        block_ids = jnp.concatenate([index - 1 + jnp.arange(3, dtype=jnp.int32), random_ids[index]])
        key_live = jnp.repeat((block_ids >= 0) & (block_ids < live_blocks), BLOCK)[None]
        rows_here = lax.dynamic_slice_in_dim(query_rows, index * BLOCK, BLOCK, 0)[None]
        return attend(rows_here, key_rows, key_live, global_keys, global_live, HEADS)[0]
    context = lax.map(one_block, jnp.arange(QBLOCKS, dtype=jnp.int32)).reshape(FRAMES, model_width)
    projected = jnp.dot(context, w_out, preferred_element_type=jnp.float32)
    pooled = lax.optimization_barrier(jnp.mean(projected.reshape(FRAMES // POOL, POOL, model_width), axis=1))
    feature_mean = lax.optimization_barrier(jnp.mean(pooled, axis=1, keepdims=True))
    centered = pooled - feature_mean
    feature_var = lax.optimization_barrier(jnp.mean(centered * centered, axis=1, keepdims=True))
    normed = centered * lax.rsqrt(feature_var + 1e-05) * norm_gain
    row_block = jnp.arange(FRAMES // POOL, dtype=jnp.int32) * POOL // BLOCK
    return jnp.where((row_block < live_blocks)[:, None], normed, 0.0).astype(jnp.bfloat16)
```

```python
import functools

import jax
import jax.numpy as jnp
from jax import lax
from jax.experimental import pallas as pl
from jax.experimental.pallas import tpu as pltpu
from jax.sharding import PartitionSpec as P

HEADS = 20
BLOCK = 128
POOL = 4
PICKS = 3
D = 1280
HD = 64
TILE = 256
STEPS = D // TILE
SHARDS = 16
SUB = BLOCK // SHARDS
ROWS = 256
NEG = -1e30

VM = pltpu.VMEM
SM = pltpu.SMEM


def _pack_kernel(first_ref, frames_ref, gpos_ref, out_ref):
    frames = frames_ref[...]
    for blk in range(2):
        out_ref[:, blk] = frames[blk * BLOCK : (blk + 1) * BLOCK].reshape(SHARDS, SUB, D)
    local = gpos_ref[...] - first_ref[0] * BLOCK
    rows = lax.broadcasted_iota(jnp.int32, (ROWS, BLOCK), 0)
    onehot = jnp.where(rows == local, 1.0, 0.0).T.astype(jnp.bfloat16)
    picked = jnp.dot(onehot, frames, preferred_element_type=jnp.float32)
    out_ref[:, 2] = picked.reshape(SHARDS, SUB, D).astype(jnp.bfloat16)


def pack(first, frames, gpos):
    return pl.pallas_call(
        _pack_kernel,
        out_shape=jax.ShapeDtypeStruct((SHARDS, 3, SUB, D), jnp.bfloat16),
        in_specs=[
            pl.BlockSpec(memory_space=SM),
            pl.BlockSpec(memory_space=VM),
            pl.BlockSpec(memory_space=VM),
        ],
        out_specs=pl.BlockSpec(memory_space=VM),
        name="pack",
    )(first, frames, gpos)


def _select_kernel(ids_ref, rows_ref, a_ref, b_ref):
    total = rows_ref[0, 2].astype(jnp.float32)
    for i in range(1, SHARDS):
        total = total + rows_ref[i, 2].astype(jnp.float32)
    total = total.astype(jnp.bfloat16)
    for r in range(SHARDS):
        for j in range(PICKS):
            c = ids_ref[r, j]
            a_ref[r, j] = rows_ref[c // 2, c % 2]
        a_ref[r, PICKS] = total
        for j in range(PICKS):
            c = ids_ref[r, PICKS + j]
            b_ref[r, j] = rows_ref[c // 2, c % 2]


def select(ids, rows):
    return pl.pallas_call(
        _select_kernel,
        out_shape=(
            jax.ShapeDtypeStruct((SHARDS, PICKS + 1, SUB, D), jnp.bfloat16),
            jax.ShapeDtypeStruct((SHARDS, PICKS, SUB, D), jnp.bfloat16),
        ),
        in_specs=[pl.BlockSpec(memory_space=SM), pl.BlockSpec(memory_space=VM)],
        out_specs=(pl.BlockSpec(memory_space=VM), pl.BlockSpec(memory_space=VM)),
        name="select",
    )(ids, rows)


def _dot(a, b):
    return jnp.dot(a, b, preferred_element_type=jnp.float32)


def _attend(query, keys, values, bias):
    lanes = lax.broadcasted_iota(jnp.int32, (BLOCK, TILE), 1) // HD
    zero = jnp.zeros_like(query)
    stacked = jnp.concatenate([jnp.where(lanes == i, query, zero) for i in range(4)], axis=0)
    scores = lax.dot_general(
        stacked, keys, (((1,), (1,)), ((), ())), preferred_element_type=jnp.float32
    )
    scores = scores + bias
    top = jnp.max(scores, axis=1, keepdims=True)
    weight = jnp.exp(scores - top).astype(jnp.bfloat16)
    ones = jnp.ones((keys.shape[0], 128), jnp.bfloat16)
    low = lax.broadcasted_iota(jnp.int32, (BLOCK, 128), 1) < HD
    outs, sums, tops = [], [], []
    for pair in range(2):
        ext = jnp.concatenate([values[:, pair * 128 : (pair + 1) * 128], ones], axis=1)
        res = _dot(weight[pair * 256 : (pair + 1) * 256], ext)
        outs.append(jnp.where(low, res[:BLOCK, :128], res[BLOCK:, :128]))
        sums.append(jnp.where(low, res[:BLOCK, 128:], res[BLOCK:, 128:]))
        tops.append(
            jnp.where(
                low,
                top[pair * 256 : pair * 256 + BLOCK],
                top[pair * 256 + BLOCK : (pair + 1) * 256],
            )
        )
    return (
        jnp.concatenate(outs, axis=1),
        jnp.concatenate(sums, axis=1),
        jnp.concatenate(tops, axis=1),
    )


def _window_kernel(lo_ref, own_ref, hi_ref, bias_ref, wq_ref, wk_ref, wv_ref, q_ref, o_ref, l_ref, m_ref):
    own = own_ref[...]
    rows = jnp.concatenate([lo_ref[...], own, hi_ref[...]], axis=0)
    query = _dot(own, wq_ref[...]).astype(jnp.bfloat16) * jnp.bfloat16(0.125)
    q_ref[...] = query
    keys = _dot(rows, wk_ref[...]).astype(jnp.bfloat16)
    values = _dot(rows, wv_ref[...]).astype(jnp.bfloat16)
    for b in range(2):
        at = slice(b * BLOCK, b * BLOCK + 3 * BLOCK)
        res = _attend(
            query[b * BLOCK : (b + 1) * BLOCK], keys[at], values[at], bias_ref[b : b + 1, :]
        )
        for ref, val in zip((o_ref, l_ref, m_ref), res):
            ref[b * BLOCK : (b + 1) * BLOCK, :] = val


def _whole(shape):
    return pl.BlockSpec(shape, lambda p: (0,) * len(shape))


def _cols(rows, shift=0):
    return pl.BlockSpec((rows, TILE), lambda p: (0, p + shift))


def window(lo, own, hi, bias, w_query, w_kv):
    f32 = jax.ShapeDtypeStruct((ROWS, D), jnp.float32)
    return pl.pallas_call(
        _window_kernel,
        grid=(STEPS,),
        out_shape=(jax.ShapeDtypeStruct((ROWS, D), jnp.bfloat16), f32, f32, f32),
        in_specs=[
            _whole((BLOCK, D)),
            _whole((ROWS, D)),
            _whole((BLOCK, D)),
            _whole((2, 3 * BLOCK)),
            _cols(D),
            _cols(D),
            _cols(D, STEPS),
        ],
        out_specs=(_cols(ROWS),) * 4,
        name="window",
    )(lo, own, hi, bias, w_query, w_kv, w_kv)


def _finish(acc, out_ref, gain_ref, live):
    tiles = []
    for c in range(D // 128):
        total = acc[c, pl.ds(0, 32, stride=POOL), :]
        for i in range(1, POOL):
            total = total + acc[c, pl.ds(i, 32, stride=POOL), :]
        tiles.append(total)
    pooled = jnp.concatenate(tiles, axis=1) * (1.0 / POOL)
    mean = jnp.mean(pooled, axis=1, keepdims=True)
    centered = pooled - mean
    var = jnp.mean(centered * centered, axis=1, keepdims=True)
    normed = centered * lax.rsqrt(var + 1e-05) * gain_ref[...]
    out_ref[...] = jnp.where(live, normed, 0.0).astype(jnp.bfloat16)


def _merge(query, keys, values, bias, o_ref, l_ref, m_ref):
    out, total, top = _attend(query, keys, values, bias)
    near = m_ref[...]
    both = jnp.maximum(near, top)
    a = jnp.exp(near - both)
    b = jnp.exp(top - both)
    return ((a * o_ref[...] + b * out) / (a * l_ref[...] + b * total)).astype(jnp.bfloat16)


def _accumulate(step, context, wo_ref, acc):
    part = _dot(context, wo_ref[...])
    for c in range(D // 128):
        piece = part[:, c * 128 : (c + 1) * 128]
        acc[c] = jnp.where(step == 0, piece, acc[c] + piece)


def _first_kernel(
    meta_ref, rows_ref, bias_ref, q_ref, o_ref, l_ref, m_ref, wk_ref, wv_ref, wo_ref, gain_ref,
    out_ref, gk_ref, gv_ref, acc,
):
    step = pl.program_id(0)
    rows = rows_ref[...]
    keys = _dot(rows, wk_ref[...])
    gk_ref[...] = keys.reshape(SHARDS, 4, SUB, TILE)[:, 3].reshape(BLOCK, TILE).astype(jnp.bfloat16)
    values = _dot(rows, wv_ref[...])
    gv_ref[...] = values.reshape(SHARDS, 4, SUB, TILE)[:, 3].reshape(BLOCK, TILE).astype(jnp.bfloat16)
    context = _merge(
        q_ref[...], keys.astype(jnp.bfloat16), values.astype(jnp.bfloat16), bias_ref[...], o_ref, l_ref, m_ref
    )
    _accumulate(step, context, wo_ref, acc)

    @pl.when(step == STEPS - 1)
    def _():
        _finish(acc, out_ref, gain_ref, meta_ref[0] < meta_ref[1])


def _second_kernel(
    meta_ref, rows_ref, bias_ref, q_ref, o_ref, l_ref, m_ref, wk_ref, wv_ref, wo_ref, gain_ref, gk_ref, gv_ref,
    prev_ref, out_ref, acc,
):
    step = pl.program_id(0)
    rows = rows_ref[...]
    keys = jnp.concatenate([_dot(rows, wk_ref[...]).astype(jnp.bfloat16), gk_ref[...]], axis=0)
    values = jnp.concatenate([_dot(rows, wv_ref[...]).astype(jnp.bfloat16), gv_ref[...]], axis=0)
    context = _merge(q_ref[...], keys, values, bias_ref[...], o_ref, l_ref, m_ref)
    _accumulate(step, context, wo_ref, acc)

    @pl.when(step == STEPS - 1)
    def _():
        _finish(acc, out_ref, gain_ref, meta_ref[0] + 1 < meta_ref[1])


def _half(b):
    return pl.BlockSpec((BLOCK, TILE), lambda p: (b, p))


def first(meta, rows, bias, q, o, l, m, w_kv, w_out, gain):
    glob = jax.ShapeDtypeStruct((BLOCK, D), jnp.bfloat16)
    return pl.pallas_call(
        _first_kernel,
        grid=(STEPS,),
        out_shape=(jax.ShapeDtypeStruct((64, D), jnp.bfloat16), glob, glob),
        in_specs=[
            pl.BlockSpec(memory_space=SM),
            _whole((4 * BLOCK, D)),
            _whole((1, 4 * BLOCK)),
            *[_half(0)] * 4,
            _cols(D),
            _cols(D, STEPS),
            pl.BlockSpec((TILE, D), lambda p: (p, 0)),
            _whole((1, D)),
        ],
        out_specs=(
            pl.BlockSpec((32, D), lambda p: (0, 0)),
            pl.BlockSpec((BLOCK, TILE), lambda p: (0, p)),
            pl.BlockSpec((BLOCK, TILE), lambda p: (0, p)),
        ),
        scratch_shapes=[pltpu.VMEM((D // 128, BLOCK, 128), jnp.float32)],
        name="first",
    )(meta, rows, bias, q, o, l, m, w_kv, w_kv, w_out, gain)


def second(meta, rows, bias, q, o, l, m, w_kv, w_out, gain, gk, gv, prev):
    return pl.pallas_call(
        _second_kernel,
        grid=(STEPS,),
        out_shape=jax.ShapeDtypeStruct((64, D), jnp.bfloat16),
        in_specs=[
            pl.BlockSpec(memory_space=SM),
            _whole((3 * BLOCK, D)),
            _whole((1, 4 * BLOCK)),
            *[_half(1)] * 4,
            _cols(D),
            _cols(D, STEPS),
            pl.BlockSpec((TILE, D), lambda p: (p, 0)),
            _whole((1, D)),
            pl.BlockSpec((BLOCK, TILE), lambda p: (0, p)),
            pl.BlockSpec((BLOCK, TILE), lambda p: (0, p)),
            pl.BlockSpec(memory_space=pl.ANY),
        ],
        out_specs=pl.BlockSpec((32, D), lambda p: (1, 0)),
        scratch_shapes=[pltpu.VMEM((D // 128, BLOCK, 128), jnp.float32)],
        input_output_aliases={13: 0},
        name="second",
    )(meta, rows, bias, q, o, l, m, w_kv, w_kv, w_out, gain, gk, gv, prev)


def exchange(value):
    return lax.all_to_all(value, "tm", split_axis=0, concat_axis=0, tiled=True)


def body(frames, w_query, w_kv, w_out, norm_gain, rand_owner, rand_slot, global_pos, length):
    shards = lax.axis_size("tm")
    rank = lax.axis_index("tm").astype(jnp.int32)
    first_block = rank * 2
    live = length[0]
    ids = (rand_owner * 2 + rand_slot).astype(jnp.int32)
    meta = jnp.stack([first_block, live])
    asked = exchange(jnp.broadcast_to(jnp.pad(ids.reshape(1, 6), ((0, 0), (0, 2))), (shards, 8)))
    up = [(i, i + 1) for i in range(shards - 1)]
    down = [(j, i) for i, j in up]
    packed = pack(meta, frames, global_pos.reshape(1, BLOCK))
    held = exchange(packed)
    lo = lax.ppermute(frames[BLOCK:], "tm", up)
    hi = lax.ppermute(frames[:BLOCK], "tm", down)
    send_a, send_b = select(asked, held)
    got_a = exchange(send_a).reshape(4 * BLOCK, D)
    got_b = exchange(send_b).reshape(3 * BLOCK, D)

    window_ids = first_block + jnp.arange(2, dtype=jnp.int32)[:, None] - 1 + jnp.arange(3, dtype=jnp.int32)[None, :]
    window_live = (window_ids >= 0) & (window_ids < live)
    window_bias = jnp.where(jnp.repeat(window_live, BLOCK, axis=1), 0.0, NEG)
    rand_bias = jnp.where(ids < live, 0.0, NEG)
    glob_bias = jnp.where(global_pos < live * BLOCK, 0.0, NEG)
    spread = jnp.broadcast_to(rand_bias[:, None, :, None], (2, SHARDS, PICKS, SUB))
    bias_a = jnp.concatenate([spread[0], glob_bias.reshape(SHARDS, 1, SUB)], axis=1).reshape(1, 4 * BLOCK)
    bias_b = jnp.concatenate([spread[1].reshape(-1), glob_bias]).reshape(1, 4 * BLOCK)
    gain = norm_gain.reshape(1, D)

    q, o, l, m = window(lo, frames, hi, window_bias, w_query, w_kv)
    half, gk, gv = first(meta, got_a, bias_a, q, o, l, m, w_kv, w_out, gain)
    return second(meta, got_b, bias_b, q, o, l, m, w_kv, w_out, gain, gk, gv, half)


def solution(mesh):
    placed = (
        P(("rec", "tm"), None),
        P(),
        P(),
        P(),
        P(),
        P(("rec", "tm"), None),
        P(("rec", "tm"), None),
        P("rec"),
        P("rec"),
    )
    return jax.shard_map(
        body, mesh=mesh, in_specs=placed, out_specs=P(("rec", "tm"), None), check_vma=False
    )
```

```python
import jax
import jax.numpy as jnp
from jax import lax
from jax.experimental import pallas as pl
from jax.experimental.pallas import tpu as pltpu
from jax.sharding import PartitionSpec as P


BLOCK = 128
POOL = 4
PICKS = 3
D = 1280
HD = 64
TILE = 256
STEPS = D // TILE
SHARDS = 16
SUB = BLOCK // SHARDS
ROWS = 256
LT = D // 128
NEG = -1e30

VM = pltpu.VMEM
SM = pltpu.SMEM


def _pack_kernel(meta_ref, owner_ref, slot_ref, frames_ref, gpos_ref, out_ref):
    frames = frames_ref[...]
    for blk in range(2):
        for c in range(LT):
            piece = frames_ref[blk * BLOCK : (blk + 1) * BLOCK, c * 128 : (c + 1) * 128]
            out_ref[:, blk * LT + c] = piece.reshape(SHARDS, SUB, 128)
    local = (gpos_ref[...] - meta_ref[0] * BLOCK).astype(jnp.float32)
    local = jnp.broadcast_to(local, (8, BLOCK)).T[:, :1]
    cols = lax.broadcasted_iota(jnp.int32, (BLOCK, ROWS), 1).astype(jnp.float32)
    onehot = jnp.where(cols == local, 1.0, 0.0).astype(jnp.bfloat16)
    picked = jnp.dot(onehot, frames, preferred_element_type=jnp.float32)
    for c in range(LT):
        piece = picked[:, c * 128 : (c + 1) * 128].reshape(SHARDS, SUB, 128)
        out_ref[:, 2 * LT + c] = piece.astype(jnp.bfloat16)
    lane = lax.broadcasted_iota(jnp.int32, (SUB, 128), 1)
    codes = jnp.zeros((SUB, 128), jnp.int32)
    for q in range(2):
        for j in range(PICKS):
            code = (slot_ref[q, j] * SHARDS + owner_ref[q, j]) * SUB
            codes = jnp.where(lane == q * PICKS + j, code, codes)
    codes = codes + lax.broadcasted_iota(jnp.int32, (SUB, 128), 0)
    codes = codes.astype(jnp.float32).astype(jnp.bfloat16)
    for s in range(SHARDS):
        out_ref[s, 3 * LT] = codes


def pack(meta, owner, slot, frames, gpos):
    return pl.pallas_call(
        _pack_kernel,
        out_shape=jax.ShapeDtypeStruct((SHARDS, 3 * LT + 1, SUB, 128), jnp.bfloat16),
        in_specs=[pl.BlockSpec(memory_space=SM)] * 3 + [pl.BlockSpec(memory_space=VM)] * 2,
        out_specs=pl.BlockSpec(memory_space=VM),
        name="pack",
    )(meta, owner, slot, frames, gpos)


def _select_kernel(held_ref, a_ref, b_ref, buf, sem):
    codes = held_ref[:, 3 * LT].astype(jnp.float32).reshape(BLOCK, 128)
    blocks = []
    for slot in range(2):
        tiles = [
            held_ref[:, slot * LT + c].astype(jnp.float32).reshape(BLOCK, 128).astype(jnp.bfloat16)
            for c in range(LT)
        ]
        blocks.append(jnp.concatenate(tiles, axis=1))
    rows = jnp.concatenate(blocks, axis=0)
    cols = lax.broadcasted_iota(jnp.int32, (BLOCK, ROWS), 1).astype(jnp.float32)
    copies = []

    def send(k, dest):
        copy = pltpu.make_async_copy(buf.at[k], dest, sem.at[k])
        copy.start()
        copies.append(copy)

    for c in range(LT):
        total = held_ref[0, 2 * LT + c].astype(jnp.float32)
        for i in range(1, SHARDS):
            total = total + held_ref[i, 2 * LT + c].astype(jnp.float32)
        total = total.astype(jnp.bfloat16)
        for r in range(SHARDS):
            buf[6, r, :, c * 128 : (c + 1) * 128] = total
    send(6, a_ref.at[:, PICKS])
    for k in range(2 * PICKS):
        onehot = jnp.where(cols == codes[:, k : k + 1], 1.0, 0.0).astype(jnp.bfloat16)
        got = jnp.dot(onehot, rows, preferred_element_type=jnp.float32)
        buf[k] = got.reshape(SHARDS, SUB, D).astype(jnp.bfloat16)
        send(k, a_ref.at[:, k] if k < PICKS else b_ref.at[:, k - PICKS])
    for copy in copies:
        copy.wait()


def select(held):
    return pl.pallas_call(
        _select_kernel,
        out_shape=(
            jax.ShapeDtypeStruct((SHARDS, PICKS + 1, SUB, D), jnp.bfloat16),
            jax.ShapeDtypeStruct((SHARDS, PICKS, SUB, D), jnp.bfloat16),
        ),
        in_specs=[pl.BlockSpec(memory_space=VM)],
        out_specs=(pl.BlockSpec(memory_space=pl.ANY), pl.BlockSpec(memory_space=pl.ANY)),
        scratch_shapes=[
            pltpu.VMEM((2 * PICKS + 1, SHARDS, SUB, D), jnp.bfloat16),
            pltpu.SemaphoreType.DMA((2 * PICKS + 1,)),
        ],
        name="select",
    )(held)


def _dot(a, b):
    return jnp.dot(a, b, preferred_element_type=jnp.float32)


def _attend(query, keys, values, bias):
    lanes = lax.broadcasted_iota(jnp.int32, (BLOCK, TILE), 1) // HD
    zero = jnp.zeros_like(query)
    stacked = jnp.concatenate([jnp.where(lanes == i, query, zero) for i in range(4)], axis=0)
    scores = lax.dot_general(
        stacked, keys, (((1,), (1,)), ((), ())), preferred_element_type=jnp.float32
    )
    scores = scores + bias
    top = jnp.max(scores, axis=1, keepdims=True)
    weight = jnp.exp(scores - top).astype(jnp.bfloat16)
    ones = jnp.ones((keys.shape[0], 128), jnp.bfloat16)
    low = lax.broadcasted_iota(jnp.int32, (BLOCK, 128), 1) < HD
    outs, sums, tops = [], [], []
    for pair in range(2):
        ext = jnp.concatenate([values[:, pair * 128 : (pair + 1) * 128], ones], axis=1)
        res = _dot(weight[pair * 256 : (pair + 1) * 256], ext)
        outs.append(jnp.where(low, res[:BLOCK, :128], res[BLOCK:, :128]))
        sums.append(jnp.where(low, res[:BLOCK, 128:], res[BLOCK:, 128:]))
        tops.append(
            jnp.where(
                low,
                top[pair * 256 : pair * 256 + BLOCK],
                top[pair * 256 + BLOCK : (pair + 1) * 256],
            )
        )
    return (
        jnp.concatenate(outs, axis=1),
        jnp.concatenate(sums, axis=1),
        jnp.concatenate(tops, axis=1),
    )


def _window_kernel(lo_ref, own_ref, hi_ref, bias_ref, wq_ref, wk_ref, wv_ref, q_ref, o_ref, l_ref, m_ref):
    own = own_ref[...]
    rows = jnp.concatenate([lo_ref[...], own, hi_ref[...]], axis=0)
    query = _dot(own, wq_ref[...]).astype(jnp.bfloat16) * jnp.bfloat16(0.125)
    q_ref[...] = query
    keys = _dot(rows, wk_ref[...]).astype(jnp.bfloat16)
    values = _dot(rows, wv_ref[...]).astype(jnp.bfloat16)
    for b in range(2):
        at = slice(b * BLOCK, b * BLOCK + 3 * BLOCK)
        res = _attend(
            query[b * BLOCK : (b + 1) * BLOCK], keys[at], values[at], bias_ref[b : b + 1, :]
        )
        for ref, val in zip((o_ref, l_ref, m_ref), res):
            ref[b * BLOCK : (b + 1) * BLOCK, :] = val


def _whole(shape):
    return pl.BlockSpec(shape, lambda p: (0,) * len(shape))


def _cols(rows, shift=0):
    return pl.BlockSpec((rows, TILE), lambda p: (0, p + shift))


def window(lo, own, hi, bias, w_query, w_kv):
    f32 = jax.ShapeDtypeStruct((ROWS, D), jnp.float32)
    return pl.pallas_call(
        _window_kernel,
        grid=(STEPS,),
        out_shape=(jax.ShapeDtypeStruct((ROWS, D), jnp.bfloat16), f32, f32, f32),
        in_specs=[
            _whole((BLOCK, D)),
            _whole((ROWS, D)),
            _whole((BLOCK, D)),
            _whole((2, 3 * BLOCK)),
            _cols(D),
            _cols(D),
            _cols(D, STEPS),
        ],
        out_specs=(_cols(ROWS),) * 4,
        name="window",
    )(lo, own, hi, bias, w_query, w_kv, w_kv)


def _finish(acc, out_ref, gain_ref, live):
    tiles = []
    for c in range(D // 128):
        total = acc[c, pl.ds(0, 32, stride=POOL), :]
        for i in range(1, POOL):
            total = total + acc[c, pl.ds(i, 32, stride=POOL), :]
        tiles.append(total)
    pooled = jnp.concatenate(tiles, axis=1) * (1.0 / POOL)
    mean = jnp.mean(pooled, axis=1, keepdims=True)
    centered = pooled - mean
    var = jnp.mean(centered * centered, axis=1, keepdims=True)
    normed = centered * lax.rsqrt(var + 1e-05) * gain_ref[...]
    out_ref[...] = jnp.where(live, normed, 0.0).astype(jnp.bfloat16)


def _merge(query, keys, values, bias, o_ref, l_ref, m_ref):
    out, total, top = _attend(query, keys, values, bias)
    near = m_ref[...]
    both = jnp.maximum(near, top)
    a = jnp.exp(near - both)
    b = jnp.exp(top - both)
    return ((a * o_ref[...] + b * out) / (a * l_ref[...] + b * total)).astype(jnp.bfloat16)


def _accumulate(step, context, wo_ref, acc):
    part = _dot(context, wo_ref[...])
    for c in range(D // 128):
        piece = part[:, c * 128 : (c + 1) * 128]
        acc[c] = jnp.where(step == 0, piece, acc[c] + piece)


def _first_kernel(
    meta_ref, rows_ref, bias_ref, q_ref, o_ref, l_ref, m_ref, wk_ref, wv_ref, wo_ref, gain_ref,
    out_ref, gk_ref, gv_ref, acc,
):
    step = pl.program_id(0)
    rows = rows_ref[...]
    keys = _dot(rows, wk_ref[...])
    gk_ref[...] = keys.reshape(SHARDS, 4, SUB, TILE)[:, 3].reshape(BLOCK, TILE).astype(jnp.bfloat16)
    values = _dot(rows, wv_ref[...])
    gv_ref[...] = values.reshape(SHARDS, 4, SUB, TILE)[:, 3].reshape(BLOCK, TILE).astype(jnp.bfloat16)
    context = _merge(
        q_ref[...], keys.astype(jnp.bfloat16), values.astype(jnp.bfloat16), bias_ref[...], o_ref, l_ref, m_ref
    )
    _accumulate(step, context, wo_ref, acc)

    @pl.when(step == STEPS - 1)
    def _():
        _finish(acc, out_ref, gain_ref, meta_ref[0] < meta_ref[1])


def _second_kernel(
    meta_ref, rows_ref, bias_ref, q_ref, o_ref, l_ref, m_ref, wk_ref, wv_ref, wo_ref, gain_ref, gk_ref, gv_ref,
    prev_ref, out_ref, acc,
):
    step = pl.program_id(0)
    rows = rows_ref[...]
    keys = jnp.concatenate([_dot(rows, wk_ref[...]).astype(jnp.bfloat16), gk_ref[...]], axis=0)
    values = jnp.concatenate([_dot(rows, wv_ref[...]).astype(jnp.bfloat16), gv_ref[...]], axis=0)
    context = _merge(q_ref[...], keys, values, bias_ref[...], o_ref, l_ref, m_ref)
    _accumulate(step, context, wo_ref, acc)

    @pl.when(step == STEPS - 1)
    def _():
        _finish(acc, out_ref, gain_ref, meta_ref[0] + 1 < meta_ref[1])


def _half(b):
    return pl.BlockSpec((BLOCK, TILE), lambda p: (b, p))


def first(meta, rows, bias, q, o, l, m, w_kv, w_out, gain):
    glob = jax.ShapeDtypeStruct((BLOCK, D), jnp.bfloat16)
    return pl.pallas_call(
        _first_kernel,
        grid=(STEPS,),
        out_shape=(jax.ShapeDtypeStruct((64, D), jnp.bfloat16), glob, glob),
        in_specs=[
            pl.BlockSpec(memory_space=SM),
            _whole((4 * BLOCK, D)),
            _whole((1, 4 * BLOCK)),
            *[_half(0)] * 4,
            _cols(D),
            _cols(D, STEPS),
            pl.BlockSpec((TILE, D), lambda p: (p, 0)),
            _whole((1, D)),
        ],
        out_specs=(
            pl.BlockSpec((32, D), lambda p: (0, 0)),
            pl.BlockSpec((BLOCK, TILE), lambda p: (0, p)),
            pl.BlockSpec((BLOCK, TILE), lambda p: (0, p)),
        ),
        scratch_shapes=[pltpu.VMEM((D // 128, BLOCK, 128), jnp.float32)],
        name="first",
    )(meta, rows, bias, q, o, l, m, w_kv, w_kv, w_out, gain)


def second(meta, rows, bias, q, o, l, m, w_kv, w_out, gain, gk, gv, prev):
    return pl.pallas_call(
        _second_kernel,
        grid=(STEPS,),
        out_shape=jax.ShapeDtypeStruct((64, D), jnp.bfloat16),
        in_specs=[
            pl.BlockSpec(memory_space=SM),
            _whole((3 * BLOCK, D)),
            _whole((1, 4 * BLOCK)),
            *[_half(1)] * 4,
            _cols(D),
            _cols(D, STEPS),
            pl.BlockSpec((TILE, D), lambda p: (p, 0)),
            _whole((1, D)),
            pl.BlockSpec((BLOCK, TILE), lambda p: (0, p)),
            pl.BlockSpec((BLOCK, TILE), lambda p: (0, p)),
            pl.BlockSpec(memory_space=pl.ANY),
        ],
        out_specs=pl.BlockSpec((32, D), lambda p: (1, 0)),
        scratch_shapes=[pltpu.VMEM((D // 128, BLOCK, 128), jnp.float32)],
        input_output_aliases={13: 0},
        name="second",
    )(meta, rows, bias, q, o, l, m, w_kv, w_kv, w_out, gain, gk, gv, prev)


def exchange(value):
    return lax.all_to_all(value, "tm", split_axis=0, concat_axis=0, tiled=True)


def program(frames, w_query, w_kv, w_out, norm_gain, rand_owner, rand_slot, global_pos, length):
    shards = lax.axis_size("tm")
    rank = lax.axis_index("tm").astype(jnp.int32)
    first_block = rank * 2
    live = length[0]
    meta = jnp.stack([first_block, live])
    up = [(i, i + 1) for i in range(shards - 1)]
    down = [(j, i) for i, j in up]
    packed = pack(meta, rand_owner, rand_slot, frames, global_pos.reshape(1, BLOCK))
    held = exchange(packed)
    lo = lax.ppermute(frames[BLOCK:], "tm", up)
    hi = lax.ppermute(frames[:BLOCK], "tm", down)
    send_a, send_b = select(held)
    got_a = exchange(send_a).reshape(4 * BLOCK, D)
    got_b = exchange(send_b).reshape(3 * BLOCK, D)

    ids = rand_owner * 2 + rand_slot
    window_ids = first_block + jnp.arange(2, dtype=jnp.int32)[:, None] - 1 + jnp.arange(3, dtype=jnp.int32)[None, :]
    window_live = (window_ids >= 0) & (window_ids < live)
    window_bias = jnp.where(jnp.repeat(window_live, BLOCK, axis=1), 0.0, NEG)
    rand_bias = jnp.where(ids < live, 0.0, NEG)
    glob_bias = jnp.where(global_pos < live * BLOCK, 0.0, NEG)
    spread = jnp.broadcast_to(rand_bias[:, None, :, None], (2, SHARDS, PICKS, SUB))
    bias_a = jnp.concatenate([spread[0], glob_bias.reshape(SHARDS, 1, SUB)], axis=1).reshape(1, 4 * BLOCK)
    bias_b = jnp.concatenate([spread[1].reshape(-1), glob_bias]).reshape(1, 4 * BLOCK)
    gain = norm_gain.reshape(1, D)

    q, o, l, m = window(lo, frames, hi, window_bias, w_query, w_kv)
    half, gk, gv = first(meta, got_a, bias_a, q, o, l, m, w_kv, w_out, gain)
    return second(meta, got_b, bias_b, q, o, l, m, w_kv, w_out, gain, gk, gv, half)


def solution(mesh):
    placed = (
        P(("rec", "tm"), None),
        P(),
        P(),
        P(),
        P(),
        P(("rec", "tm"), None),
        P(("rec", "tm"), None),
        P("rec"),
        P("rec"),
    )
    return jax.shard_map(
        program, mesh=mesh, in_specs=placed, out_specs=P(("rec", "tm"), None), check_vma=False
    )
```

```python
import jax
import jax.numpy as jnp
from jax import lax
from jax.experimental import pallas as pl
from jax.experimental.pallas import tpu as pltpu
from jax.sharding import PartitionSpec as P


BLOCK = 128
POOL = 4
PICKS = 3
D = 1280
HD = 64
TILE = 256
STEPS = D // TILE
SHARDS = 16
SUB = BLOCK // SHARDS
ROWS = 256
SUBS_A = 5
SUBS_B = 2
LT = D // 128
NEG = -1e30

VM = pltpu.VMEM
SM = pltpu.SMEM


def _pack_kernel(rank_ref, owner_ref, slot_ref, frames_ref, gpos_ref, out_ref):
    frames = frames_ref[...]
    for blk in range(2):
        for c in range(LT):
            piece = frames_ref[blk * BLOCK : (blk + 1) * BLOCK, c * 128 : (c + 1) * 128]
            out_ref[:, blk * LT + c] = piece.reshape(SHARDS, SUB, 128)
    local = (gpos_ref[...] - rank_ref[0] * ROWS).astype(jnp.float32)
    local = jnp.broadcast_to(local, (8, BLOCK)).T[:, :1]
    cols = lax.broadcasted_iota(jnp.int32, (BLOCK, ROWS), 1).astype(jnp.float32)
    onehot = jnp.where(cols == local, 1.0, 0.0).astype(jnp.bfloat16)
    picked = jnp.dot(onehot, frames, preferred_element_type=jnp.float32)
    for c in range(LT):
        piece = picked[:, c * 128 : (c + 1) * 128].reshape(SHARDS, SUB, 128)
        out_ref[:, 2 * LT + c] = piece.astype(jnp.bfloat16)
    lane = lax.broadcasted_iota(jnp.int32, (SUB, 128), 1)
    codes = jnp.zeros((SUB, 128), jnp.int32)
    for q in range(2):
        for j in range(PICKS):
            code = (slot_ref[q, j] * SHARDS + owner_ref[q, j]) * SUB
            codes = jnp.where(lane == q * PICKS + j, code, codes)
    codes = codes + lax.broadcasted_iota(jnp.int32, (SUB, 128), 0)
    codes = codes.astype(jnp.float32).astype(jnp.bfloat16)
    for s in range(SHARDS):
        out_ref[s, 3 * LT] = codes


def pack(rank, owner, slot, frames, gpos):
    return pl.pallas_call(
        _pack_kernel,
        out_shape=VM((SHARDS, 3 * LT + 1, SUB, 128), jnp.bfloat16),
        in_specs=[pl.BlockSpec(memory_space=SM)] * 3 + [pl.BlockSpec(memory_space=VM)] * 2,
        out_specs=pl.BlockSpec(memory_space=VM),
        name="pack",
    )(rank, owner, slot, frames, gpos)


def _select_kernel(held_ref, a_ref, b_ref, buf, sem):
    copies = []

    def send(k, dest):
        copy = pltpu.make_async_copy(buf.at[k], dest, sem.at[k])
        copy.start()
        copies.append(copy)

    codes = held_ref[:, 3 * LT].astype(jnp.float32).reshape(BLOCK, 128)
    blocks = []
    for slot in range(2):
        tiles = [
            held_ref[:, slot * LT + c].astype(jnp.float32).reshape(BLOCK, 128).astype(jnp.bfloat16)
            for c in range(LT)
        ]
        blocks.append(jnp.concatenate(tiles, axis=1))
    rows = jnp.concatenate(blocks, axis=0)
    cols = lax.broadcasted_iota(jnp.int32, (BLOCK, ROWS), 1).astype(jnp.float32)
    for c in range(LT):
        total = held_ref[0, 2 * LT + c].astype(jnp.float32)
        for i in range(1, SHARDS):
            total = total + held_ref[i, 2 * LT + c].astype(jnp.float32)
        total = total.astype(jnp.bfloat16)
        for r in range(SHARDS):
            buf[2 * PICKS, r, :, c * 128 : (c + 1) * 128] = total
    send(2 * PICKS, a_ref.at[:, SUBS_A - 1])
    for k in range(2 * PICKS):
        onehot = jnp.where(cols == codes[:, k : k + 1], 1.0, 0.0).astype(jnp.bfloat16)
        got = jnp.dot(onehot, rows, preferred_element_type=jnp.float32)
        buf[k] = got.reshape(SHARDS, SUB, D).astype(jnp.bfloat16)
        send(k, a_ref.at[:, k] if k < SUBS_A - 1 else b_ref.at[:, k - SUBS_A + 1])
    for copy in copies:
        copy.wait()


def select(held):
    return pl.pallas_call(
        _select_kernel,
        out_shape=(
            jax.ShapeDtypeStruct((SHARDS, SUBS_A, SUB, D), jnp.bfloat16),
            jax.ShapeDtypeStruct((SHARDS, SUBS_B, SUB, D), jnp.bfloat16),
        ),
        in_specs=[pl.BlockSpec(memory_space=VM)],
        out_specs=(pl.BlockSpec(memory_space=pl.ANY), pl.BlockSpec(memory_space=pl.ANY)),
        scratch_shapes=[
            pltpu.VMEM((2 * PICKS + 1, SHARDS, SUB, D), jnp.bfloat16),
            pltpu.SemaphoreType.DMA((2 * PICKS + 1,)),
        ],
        name="select",
    )(pltpu.with_memory_space_constraint(held, VM))


def _dot(a, b):
    return jnp.dot(a, b, preferred_element_type=jnp.float32)


def _attend(query, keys, values, bias):
    lanes = lax.broadcasted_iota(jnp.int32, (BLOCK, TILE), 1) // HD
    zero = jnp.zeros_like(query)
    stacked = jnp.concatenate([jnp.where(lanes == i, query, zero) for i in range(4)], axis=0)
    scores = lax.dot_general(
        stacked, keys, (((1,), (1,)), ((), ())), preferred_element_type=jnp.float32
    )
    scores = scores + bias
    top = jnp.max(scores, axis=1, keepdims=True)
    weight = jnp.exp(scores - top).astype(jnp.bfloat16)
    ones = jnp.ones((keys.shape[0], 128), jnp.bfloat16)
    low = lax.broadcasted_iota(jnp.int32, (BLOCK, 128), 1) < HD
    outs, sums, tops = [], [], []
    for pair in range(2):
        ext = jnp.concatenate([values[:, pair * 128 : (pair + 1) * 128], ones], axis=1)
        res = _dot(weight[pair * 256 : (pair + 1) * 256], ext)
        outs.append(jnp.where(low, res[:BLOCK, :128], res[BLOCK:, :128]))
        sums.append(jnp.where(low, res[:BLOCK, 128:], res[BLOCK:, 128:]))
        tops.append(
            jnp.where(
                low,
                top[pair * 256 : pair * 256 + BLOCK],
                top[pair * 256 + BLOCK : (pair + 1) * 256],
            )
        )
    return (
        jnp.concatenate(outs, axis=1),
        jnp.concatenate(sums, axis=1),
        jnp.concatenate(tops, axis=1),
    )


def _own_kernel(
    rank_ref, len_ref, owner_ref, slot_ref, gpos_ref, own_ref, wq_ref, wk_ref, wv_ref,
    q_ref, k_ref, v_ref, bias_ref,
):
    own = own_ref[...]
    q_ref[...] = _dot(own, wq_ref[...]).astype(jnp.bfloat16) * jnp.bfloat16(0.125)
    k_ref[...] = _dot(own, wk_ref[...]).astype(jnp.bfloat16)
    v_ref[...] = _dot(own, wv_ref[...]).astype(jnp.bfloat16)

    @pl.when(pl.program_id(0) == 0)
    def _():
        live = len_ref[0]
        lane = lax.broadcasted_iota(jnp.int32, (1, 4 * BLOCK), 1)

        def row(parts):
            dead = lane < 0
            for at, block in parts:
                dead = dead | (at & ((block < 0) | (block >= live)))
            return jnp.where(dead, NEG, 0.0)

        def picked(q, j):
            return owner_ref[q, j] * 2 + slot_ref[q, j]

        for q in range(2):
            near = [(lane // BLOCK == i, rank_ref[0] * 2 + q - 1 + i) for i in range(3)]
            bias_ref[q : q + 1, :] = row(near)
        glob = jnp.where(gpos_ref[...] < live * BLOCK, 0.0, NEG)
        rows = lane // SUB
        far = row([((rows % 3 == j), picked(0, j)) for j in range(3)])
        bias_ref[2:3, :] = jnp.concatenate([far[:, : 3 * BLOCK], glob], axis=1)
        far = row([((rows % 2 == j), picked(1, j + 1)) for j in range(2)])
        more = row([(lane >= 0, picked(1, 0))])
        bias_ref[3:4, :] = jnp.concatenate([far[:, : 2 * BLOCK], glob, more[:, :BLOCK]], axis=1)
        bias_ref[4:8, :] = jnp.zeros((4, 4 * BLOCK), jnp.float32)


def _halo_kernel(lo_ref, hi_ref, bias_ref, q_ref, k_ref, v_ref, wk_ref, wv_ref, o_ref, l_ref, m_ref):
    rim = jnp.concatenate([lo_ref[...], hi_ref[...]], axis=0)

    def widen(own_ref, w_ref):
        far = _dot(rim, w_ref[...]).astype(jnp.bfloat16)
        return jnp.concatenate([far[:BLOCK], own_ref[...], far[BLOCK:]], axis=0)

    keys = widen(k_ref, wk_ref)
    values = widen(v_ref, wv_ref)
    for b in range(2):
        at = slice(b * BLOCK, b * BLOCK + 3 * BLOCK)
        res = _attend(
            q_ref[b * BLOCK : (b + 1) * BLOCK], keys[at], values[at], bias_ref[b : b + 1, : 3 * BLOCK]
        )
        for ref, val in zip((o_ref, l_ref, m_ref), res):
            ref[b * BLOCK : (b + 1) * BLOCK, :] = val


def _whole(shape):
    return pl.BlockSpec(shape, lambda p: (0,) * len(shape))


def _cols(rows, shift=0):
    return pl.BlockSpec((rows, TILE), lambda p: (0, p + shift))


def own_part(rank, length, owner, slot, gpos, own, w_query, w_kv):
    half = jax.ShapeDtypeStruct((ROWS, D), jnp.bfloat16)
    return pl.pallas_call(
        _own_kernel,
        grid=(STEPS,),
        out_shape=(half, half, half, jax.ShapeDtypeStruct((8, 4 * BLOCK), jnp.float32)),
        in_specs=[pl.BlockSpec(memory_space=SM)] * 4
        + [_whole((1, BLOCK)), _whole((ROWS, D)), _cols(D), _cols(D), _cols(D, STEPS)],
        out_specs=(_cols(ROWS),) * 3 + (_whole((8, 4 * BLOCK)),),
        name="own",
    )(rank, length, owner, slot, gpos, own, w_query, w_kv, w_kv)


def halo_part(lo, hi, bias, q, k, v, w_kv):
    f32 = jax.ShapeDtypeStruct((ROWS, D), jnp.float32)
    lo = pltpu.with_memory_space_constraint(lo, VM)
    hi = pltpu.with_memory_space_constraint(hi, VM)
    return pl.pallas_call(
        _halo_kernel,
        grid=(STEPS,),
        out_shape=(f32, f32, f32),
        in_specs=[
            pl.BlockSpec(memory_space=VM),
            pl.BlockSpec(memory_space=VM),
            _whole((8, 4 * BLOCK)),
            *[_cols(ROWS)] * 3,
            _cols(D),
            _cols(D, STEPS),
        ],
        out_specs=(_cols(ROWS),) * 3,
        name="halo",
    )(lo, hi, bias, q, k, v, w_kv, w_kv)


def _finish(acc, out_ref, gain_ref, live):
    tiles = []
    for c in range(D // 128):
        total = acc[c, pl.ds(0, 32, stride=POOL), :]
        for i in range(1, POOL):
            total = total + acc[c, pl.ds(i, 32, stride=POOL), :]
        tiles.append(total)
    pooled = jnp.concatenate(tiles, axis=1) * (1.0 / POOL)
    mean = jnp.mean(pooled, axis=1, keepdims=True)
    centered = pooled - mean
    var = jnp.mean(centered * centered, axis=1, keepdims=True)
    normed = centered * lax.rsqrt(var + 1e-05) * gain_ref[...]
    out_ref[...] = jnp.where(live, normed, 0.0).astype(jnp.bfloat16)


def _merge(query, keys, values, bias, o_ref, l_ref, m_ref):
    out, total, top = _attend(query, keys, values, bias)
    near = m_ref[...]
    both = jnp.maximum(near, top)
    a = jnp.exp(near - both)
    b = jnp.exp(top - both)
    return ((a * o_ref[...] + b * out) / (a * l_ref[...] + b * total)).astype(jnp.bfloat16)


def _accumulate(step, context, wo_ref, acc):
    part = _dot(context, wo_ref[...])
    for c in range(D // 128):
        piece = part[:, c * 128 : (c + 1) * 128]
        acc[c] = jnp.where(step == 0, piece, acc[c] + piece)


def _first_kernel(
    rank_ref, len_ref, rows_ref, bias_ref, q_ref, o_ref, l_ref, m_ref, wk_ref, wv_ref, wo_ref, gain_ref,
    out_ref, gk_ref, gv_ref, acc,
):
    step = pl.program_id(0)
    rows = rows_ref[...]

    def split(w_ref, keep_ref):
        full = _dot(rows, w_ref[...]).reshape(SHARDS, SUBS_A, SUB, TILE)
        near = full[:, :PICKS].reshape(PICKS * BLOCK, TILE).astype(jnp.bfloat16)
        more = full[:, PICKS].reshape(BLOCK, TILE).astype(jnp.bfloat16)
        glob = full[:, PICKS + 1].reshape(BLOCK, TILE).astype(jnp.bfloat16)
        keep_ref[:BLOCK, :] = glob
        keep_ref[BLOCK:, :] = more
        return jnp.concatenate([near, glob], axis=0)

    keys = split(wk_ref, gk_ref)
    values = split(wv_ref, gv_ref)
    context = _merge(q_ref[...], keys, values, bias_ref[2:3, :], o_ref, l_ref, m_ref)
    _accumulate(step, context, wo_ref, acc)

    @pl.when(step == STEPS - 1)
    def _():
        _finish(acc, out_ref, gain_ref, rank_ref[0] * 2 < len_ref[0])


def _second_kernel(
    rank_ref, len_ref, rows_ref, bias_ref, q_ref, o_ref, l_ref, m_ref, wk_ref, wv_ref, wo_ref, gain_ref,
    gk_ref, gv_ref, prev_ref, out_ref, acc,
):
    step = pl.program_id(0)
    rows = rows_ref[...]
    keys = jnp.concatenate([_dot(rows, wk_ref[...]).astype(jnp.bfloat16), gk_ref[...]], axis=0)
    values = jnp.concatenate([_dot(rows, wv_ref[...]).astype(jnp.bfloat16), gv_ref[...]], axis=0)
    context = _merge(q_ref[...], keys, values, bias_ref[3:4, :], o_ref, l_ref, m_ref)
    _accumulate(step, context, wo_ref, acc)

    @pl.when(step == STEPS - 1)
    def _():
        _finish(acc, out_ref, gain_ref, rank_ref[0] * 2 + 1 < len_ref[0])


def _half(b):
    return pl.BlockSpec((BLOCK, TILE), lambda p: (b, p))


def _late_specs(b):
    return [
        *[pl.BlockSpec(memory_space=SM)] * 2,
        pl.BlockSpec(memory_space=VM),
        _whole((8, 4 * BLOCK)),
        *[_half(b)] * 4,
        _cols(D),
        _cols(D, STEPS),
        pl.BlockSpec((TILE, D), lambda p: (p, 0)),
        _whole((1, D)),
    ]


def first(rank, length, rows, bias, q, o, l, m, w_kv, w_out, gain):
    kept = jax.ShapeDtypeStruct((2 * BLOCK, D), jnp.bfloat16)
    rows = pltpu.with_memory_space_constraint(rows, VM)
    return pl.pallas_call(
        _first_kernel,
        grid=(STEPS,),
        out_shape=(jax.ShapeDtypeStruct((64, D), jnp.bfloat16), kept, kept),
        in_specs=_late_specs(0),
        out_specs=(pl.BlockSpec((32, D), lambda p: (0, 0)), _cols(2 * BLOCK), _cols(2 * BLOCK)),
        scratch_shapes=[pltpu.VMEM((D // 128, BLOCK, 128), jnp.float32)],
        name="first",
    )(rank, length, rows, bias, q, o, l, m, w_kv, w_kv, w_out, gain)


def second(rank, length, rows, bias, q, o, l, m, w_kv, w_out, gain, gk, gv, prev):
    rows = pltpu.with_memory_space_constraint(rows, VM)
    return pl.pallas_call(
        _second_kernel,
        grid=(STEPS,),
        out_shape=jax.ShapeDtypeStruct((64, D), jnp.bfloat16),
        in_specs=[
            *_late_specs(1),
            _cols(2 * BLOCK),
            _cols(2 * BLOCK),
            pl.BlockSpec(memory_space=pl.ANY),
        ],
        out_specs=pl.BlockSpec((32, D), lambda p: (1, 0)),
        scratch_shapes=[pltpu.VMEM((D // 128, BLOCK, 128), jnp.float32)],
        input_output_aliases={14: 0},
        name="second",
    )(rank, length, rows, bias, q, o, l, m, w_kv, w_kv, w_out, gain, gk, gv, prev)


def exchange(value):
    return lax.all_to_all(value, "tm", split_axis=0, concat_axis=0, tiled=True)


def program(frames, w_query, w_kv, w_out, norm_gain, rand_owner, rand_slot, global_pos, length):
    shards = lax.axis_size("tm")
    rank = lax.axis_index("tm").astype(jnp.int32).reshape(1)
    gpos = global_pos.reshape(1, BLOCK)
    gain = norm_gain.reshape(1, D)
    up = [(i, i + 1) for i in range(shards - 1)]
    down = [(j, i) for i, j in up]
    packed = pack(rank, rand_owner, rand_slot, frames, gpos)
    held = exchange(packed)
    q, k, v, bias = own_part(rank, length, rand_owner, rand_slot, gpos, frames, w_query, w_kv)
    lo = lax.ppermute(frames[BLOCK:], "tm", up)
    hi = lax.ppermute(frames[:BLOCK], "tm", down)
    send_a, send_b = select(held)
    got_a = exchange(send_a).reshape(SUBS_A * BLOCK, D)
    got_b = exchange(send_b).reshape(SUBS_B * BLOCK, D)
    o, l, m = halo_part(lo, hi, bias, q, k, v, w_kv)
    half, gk, gv = first(rank, length, got_a, bias, q, o, l, m, w_kv, w_out, gain)
    return second(rank, length, got_b, bias, q, o, l, m, w_kv, w_out, gain, gk, gv, half)


def solution(mesh):
    placed = (
        P(("rec", "tm"), None),
        P(),
        P(),
        P(),
        P(),
        P(("rec", "tm"), None),
        P(("rec", "tm"), None),
        P("rec"),
        P("rec"),
    )
    return jax.shard_map(
        program, mesh=mesh, in_specs=placed, out_specs=P(("rec", "tm"), None), check_vma=False
    )
```

```python
import jax
import jax.numpy as jnp
from jax import lax
from jax.experimental import pallas as pl
from jax.experimental.pallas import tpu as pltpu
from jax.sharding import PartitionSpec as P


BLOCK = 128
POOL = 4
PICKS = 3
D = 1280
HD = 64
TILE = 256
STEPS = D // TILE
SHARDS = 16
SUB = BLOCK // SHARDS
ROWS = 256
SUBS_A = 4
SUBS_B = 3
LT = D // 128
NEG = -1e30

VM = pltpu.VMEM
SM = pltpu.SMEM


def _pack_kernel(rank_ref, owner_ref, slot_ref, frames_ref, gpos_ref, out_ref):
    frames = frames_ref[...]
    for blk in range(2):
        for c in range(LT):
            piece = frames_ref[blk * BLOCK : (blk + 1) * BLOCK, c * 128 : (c + 1) * 128]
            out_ref[:, blk * LT + c] = piece.reshape(SHARDS, SUB, 128)
    local = (gpos_ref[...] - rank_ref[0] * ROWS).astype(jnp.float32)
    local = jnp.broadcast_to(local, (8, BLOCK)).T[:, :1]
    cols = lax.broadcasted_iota(jnp.int32, (BLOCK, ROWS), 1).astype(jnp.float32)
    onehot = jnp.where(cols == local, 1.0, 0.0).astype(jnp.bfloat16)
    picked = jnp.dot(onehot, frames, preferred_element_type=jnp.float32)
    for c in range(LT):
        piece = picked[:, c * 128 : (c + 1) * 128].reshape(SHARDS, SUB, 128)
        out_ref[:, 2 * LT + c] = piece.astype(jnp.bfloat16)
    lane = lax.broadcasted_iota(jnp.int32, (SUB, 128), 1)
    codes = jnp.zeros((SUB, 128), jnp.int32)
    for q in range(2):
        for j in range(PICKS):
            code = (slot_ref[q, j] * SHARDS + owner_ref[q, j]) * SUB
            codes = jnp.where(lane == q * PICKS + j, code, codes)
    codes = codes + lax.broadcasted_iota(jnp.int32, (SUB, 128), 0)
    codes = codes.astype(jnp.float32).astype(jnp.bfloat16)
    for s in range(SHARDS):
        out_ref[s, 3 * LT] = codes


def pack(rank, owner, slot, frames, gpos):
    return pl.pallas_call(
        _pack_kernel,
        out_shape=VM((SHARDS, 3 * LT + 1, SUB, 128), jnp.bfloat16),
        in_specs=[pl.BlockSpec(memory_space=SM)] * 3 + [pl.BlockSpec(memory_space=VM)] * 2,
        out_specs=pl.BlockSpec(memory_space=VM),
        name="pack",
    )(rank, owner, slot, frames, gpos)


def _select_kernel(held_ref, a_ref, b_ref, buf, sem):
    copies = []

    def send(k, dest):
        copy = pltpu.make_async_copy(buf.at[k], dest, sem.at[k])
        copy.start()
        copies.append(copy)

    codes = held_ref[:, 3 * LT].astype(jnp.float32).reshape(BLOCK, 128)
    blocks = []
    for slot in range(2):
        tiles = [
            held_ref[:, slot * LT + c].astype(jnp.float32).reshape(BLOCK, 128).astype(jnp.bfloat16)
            for c in range(LT)
        ]
        blocks.append(jnp.concatenate(tiles, axis=1))
    rows = jnp.concatenate(blocks, axis=0)
    cols = lax.broadcasted_iota(jnp.int32, (BLOCK, ROWS), 1).astype(jnp.float32)
    for c in range(LT):
        total = held_ref[0, 2 * LT + c].astype(jnp.float32)
        for i in range(1, SHARDS):
            total = total + held_ref[i, 2 * LT + c].astype(jnp.float32)
        total = total.astype(jnp.bfloat16)
        for r in range(SHARDS):
            buf[2 * PICKS, r, :, c * 128 : (c + 1) * 128] = total
    send(2 * PICKS, a_ref.at[:, SUBS_A - 1])
    for k in range(2 * PICKS):
        onehot = jnp.where(cols == codes[:, k : k + 1], 1.0, 0.0).astype(jnp.bfloat16)
        got = jnp.dot(onehot, rows, preferred_element_type=jnp.float32)
        buf[k] = got.reshape(SHARDS, SUB, D).astype(jnp.bfloat16)
        send(k, a_ref.at[:, k] if k < SUBS_A - 1 else b_ref.at[:, k - SUBS_A + 1])
    for copy in copies:
        copy.wait()


def select(held):
    return pl.pallas_call(
        _select_kernel,
        out_shape=(
            jax.ShapeDtypeStruct((SHARDS, SUBS_A, SUB, D), jnp.bfloat16),
            jax.ShapeDtypeStruct((SHARDS, SUBS_B, SUB, D), jnp.bfloat16),
        ),
        in_specs=[pl.BlockSpec(memory_space=VM)],
        out_specs=(pl.BlockSpec(memory_space=pl.ANY), pl.BlockSpec(memory_space=pl.ANY)),
        scratch_shapes=[
            pltpu.VMEM((2 * PICKS + 1, SHARDS, SUB, D), jnp.bfloat16),
            pltpu.SemaphoreType.DMA((2 * PICKS + 1,)),
        ],
        name="select",
    )(pltpu.with_memory_space_constraint(held, VM))


def _dot(a, b):
    return jnp.dot(a, b, preferred_element_type=jnp.float32)


def _scores(query, keys):
    lanes = lax.broadcasted_iota(jnp.int32, (BLOCK, TILE), 1) // HD
    zero = jnp.zeros_like(query)
    stacked = jnp.concatenate([jnp.where(lanes == i, query, zero) for i in range(4)], axis=0)
    return lax.dot_general(
        stacked, keys, (((1,), (1,)), ((), ())), preferred_element_type=jnp.float32
    )


def _weigh(scores, values, bias):
    scores = scores + bias
    top = jnp.max(scores, axis=1, keepdims=True)
    weight = jnp.exp(scores - top).astype(jnp.bfloat16)
    ones = jnp.ones((values.shape[0], 128), jnp.bfloat16)
    low = lax.broadcasted_iota(jnp.int32, (BLOCK, 128), 1) < HD
    outs, sums, tops = [], [], []
    for pair in range(2):
        ext = jnp.concatenate([values[:, pair * 128 : (pair + 1) * 128], ones], axis=1)
        res = _dot(weight[pair * 256 : (pair + 1) * 256], ext)
        outs.append(jnp.where(low, res[:BLOCK, :128], res[BLOCK:, :128]))
        sums.append(jnp.where(low, res[:BLOCK, 128:], res[BLOCK:, 128:]))
        tops.append(
            jnp.where(
                low,
                top[pair * 256 : pair * 256 + BLOCK],
                top[pair * 256 + BLOCK : (pair + 1) * 256],
            )
        )
    return tuple(jnp.concatenate(x, axis=1) for x in (outs, sums, tops))


def _attend(query, keys, values, bias):
    return _weigh(_scores(query, keys), values, bias)


def _join(near, far):
    both = jnp.maximum(near[2], far[2])
    a = jnp.exp(near[2] - both)
    b = jnp.exp(far[2] - both)
    return a * near[0] + b * far[0], a * near[1] + b * far[1], both


def _own_kernel(
    rank_ref, len_ref, owner_ref, slot_ref, gpos_ref, own_ref, wq_ref, wk_ref, wv_ref,
    q_ref, k_ref, v_ref, bias_ref,
):
    own = own_ref[...]
    q_ref[...] = _dot(own, wq_ref[...]).astype(jnp.bfloat16) * jnp.bfloat16(0.125)
    k_ref[...] = _dot(own, wk_ref[...]).astype(jnp.bfloat16)
    v_ref[...] = _dot(own, wv_ref[...]).astype(jnp.bfloat16)

    @pl.when(pl.program_id(0) == 0)
    def _():
        live = len_ref[0]
        lane = lax.broadcasted_iota(jnp.int32, (1, 4 * BLOCK), 1)

        def row(parts):
            dead = lane < 0
            for at, block in parts:
                dead = dead | (at & ((block < 0) | (block >= live)))
            return jnp.where(dead, NEG, 0.0)

        def picked(q, j):
            return owner_ref[q, j] * 2 + slot_ref[q, j]

        for q in range(2):
            near = [(lane // BLOCK == i, rank_ref[0] * 2 + q - 1 + i) for i in range(3)]
            bias_ref[q : q + 1, :] = row(near)
        glob = jnp.where(gpos_ref[...] < live * BLOCK, 0.0, NEG)
        rows = lane // SUB
        for q in range(2):
            far = row([((rows % PICKS == j), picked(q, j)) for j in range(PICKS)])
            bias_ref[2 + q : 3 + q, :] = jnp.concatenate([far[:, : PICKS * BLOCK], glob], axis=1)
        bias_ref[4:8, :] = jnp.zeros((4, 4 * BLOCK), jnp.float32)


def _halo_kernel(lo_ref, hi_ref, bias_ref, q_ref, k_ref, v_ref, wk_ref, wv_ref, o_ref, l_ref, m_ref):
    rim = jnp.concatenate([lo_ref[...], hi_ref[...]], axis=0)

    def widen(own_ref, w_ref):
        far = _dot(rim, w_ref[...]).astype(jnp.bfloat16)
        return jnp.concatenate([far[:BLOCK], own_ref[...], far[BLOCK:]], axis=0)

    keys = widen(k_ref, wk_ref)
    values = widen(v_ref, wv_ref)
    for b in range(2):
        at = slice(b * BLOCK, b * BLOCK + 3 * BLOCK)
        res = _attend(
            q_ref[b * BLOCK : (b + 1) * BLOCK], keys[at], values[at], bias_ref[b : b + 1, : 3 * BLOCK]
        )
        for ref, val in zip((o_ref, l_ref, m_ref), res):
            ref[b * BLOCK : (b + 1) * BLOCK, :] = val


def _whole(shape):
    return pl.BlockSpec(shape, lambda p: (0,) * len(shape))


def _cols(rows, shift=0):
    return pl.BlockSpec((rows, TILE), lambda p: (0, p + shift))


def own_part(rank, length, owner, slot, gpos, own, w_query, w_kv):
    half = jax.ShapeDtypeStruct((ROWS, D), jnp.bfloat16)
    return pl.pallas_call(
        _own_kernel,
        grid=(STEPS,),
        out_shape=(half, half, half, jax.ShapeDtypeStruct((8, 4 * BLOCK), jnp.float32)),
        in_specs=[pl.BlockSpec(memory_space=SM)] * 4
        + [_whole((1, BLOCK)), _whole((ROWS, D)), _cols(D), _cols(D), _cols(D, STEPS)],
        out_specs=(_cols(ROWS),) * 3 + (_whole((8, 4 * BLOCK)),),
        name="own",
    )(rank, length, owner, slot, gpos, own, w_query, w_kv, w_kv)


def halo_part(lo, hi, bias, q, k, v, w_kv):
    f32 = jax.ShapeDtypeStruct((ROWS, D), jnp.float32)
    lo = pltpu.with_memory_space_constraint(lo, VM)
    hi = pltpu.with_memory_space_constraint(hi, VM)
    return pl.pallas_call(
        _halo_kernel,
        grid=(STEPS,),
        out_shape=(f32, f32, f32),
        in_specs=[
            pl.BlockSpec(memory_space=VM),
            pl.BlockSpec(memory_space=VM),
            _whole((8, 4 * BLOCK)),
            *[_cols(ROWS)] * 3,
            _cols(D),
            _cols(D, STEPS),
        ],
        out_specs=(_cols(ROWS),) * 3,
        name="halo",
    )(lo, hi, bias, q, k, v, w_kv, w_kv)


def _finish(context, wo_ref, acc, out_ref, gain_ref, live):
    projected = _dot(context, wo_ref[...])
    tiles = []
    for c in range(LT):
        acc[c] = projected[:, c * 128 : (c + 1) * 128]
    for c in range(LT):
        total = acc[c, pl.ds(0, 32, stride=POOL), :]
        for i in range(1, POOL):
            total = total + acc[c, pl.ds(i, 32, stride=POOL), :]
        tiles.append(total)
    pooled = jnp.concatenate(tiles, axis=1) * (1.0 / POOL)
    mean = jnp.mean(pooled, axis=1, keepdims=True)
    centered = pooled - mean
    var = jnp.mean(centered * centered, axis=1, keepdims=True)
    normed = centered * lax.rsqrt(var + 1e-05) * gain_ref[...]
    out_ref[...] = jnp.where(live, normed, 0.0).astype(jnp.bfloat16)


def _tile(p, base=0):
    return slice(base + p * TILE, base + (p + 1) * TILE)


def _stage(query, keys_ref, values_ref, scores_ref, weight_ref, bias):
    width = keys_ref.shape[0]
    scores_ref[:, :width] = _scores(query, keys_ref[...])
    tops = []
    for r in range(0, 4 * BLOCK, 64):
        piece = scores_ref[r : r + 64, :width] + bias
        top = jnp.max(piece, axis=1, keepdims=True)
        weight_ref[r : r + 64, :width] = jnp.exp(piece - top).astype(jnp.bfloat16)
        tops.append(top)
    top = jnp.concatenate(tops, axis=0)
    ones = jnp.ones((width, 128), jnp.bfloat16)
    low = lax.broadcasted_iota(jnp.int32, (BLOCK, 128), 1) < HD
    outs, sums, maxes = [], [], []
    for pair in range(2):
        base = pair * 256
        ext = jnp.concatenate([values_ref[:, pair * 128 : (pair + 1) * 128], ones], axis=1)
        res = _dot(weight_ref[base : base + 256, :width], ext)
        outs.append(jnp.where(low, res[:BLOCK, :128], res[BLOCK:, :128]))
        sums.append(jnp.where(low, res[:BLOCK, 128:], res[BLOCK:, 128:]))
        maxes.append(jnp.where(low, top[base : base + BLOCK], top[base + BLOCK : base + 256]))
    return tuple(jnp.concatenate(x, axis=1) for x in (outs, sums, maxes))


class _Fetch:
    def __init__(self, half, q_ref, o_ref, l_ref, m_ref, wkv_ref, wo_ref, bufs, sem):
        q, o, l, m, wkv, wo = bufs
        self.copies = {}
        count = 0

        def start(key, src, dst):
            nonlocal count
            copy = pltpu.make_async_copy(src, dst, sem.at[count])
            copy.start()
            self.copies[key] = copy
            count += 1

        def weights(p, base):
            at = _tile(p, base)
            start(("w", base, p), wkv_ref.at[:, at], wkv.at[:, at])

        weights(0, 0)
        start("q", q_ref.at[half], q)
        weights(0, D)
        weights(1, 0)
        for key, src, dst in (("o", o_ref, o), ("l", l_ref, l), ("m", m_ref, m)):
            start(key, src, dst)
        for p in range(1, STEPS):
            weights(p, D)
            if p + 1 < STEPS:
                weights(p + 1, 0)
        start("wo", wo_ref, wo)

    def wait(self, *keys):
        for key in keys:
            self.copies.pop(key).wait()


def _first_kernel(
    rank_ref, len_ref, rows_ref, bias_ref, q_hbm, o_hbm, l_hbm, m_hbm, wkv_hbm, wo_hbm, gain_ref,
    out_ref, o1_ref, l1_ref, m1_ref, acc, q_ref, o_ref, l_ref, m_ref, wkv_ref, wo_ref, sem,
    keys_ref, values_ref, scores_ref, weight_ref, context_ref, scores1_ref, weight1_ref,
):
    fetch = _Fetch(
        slice(0, ROWS), q_hbm, o_hbm, l_hbm, m_hbm, wkv_hbm, wo_hbm,
        (q_ref, o_ref, l_ref, m_ref, wkv_ref, wo_ref), sem,
    )
    far_rows = PICKS * BLOCK

    def project(p):
        fetch.wait(("w", 0, p), ("w", D, p))
        for base, ref in ((0, keys_ref), (D, values_ref)):
            full = _dot(rows_ref[...], wkv_ref[:, _tile(p, base)]).reshape(SHARDS, SUBS_A, SUB, TILE)
            ref[p % 2, :far_rows] = full[:, :PICKS].reshape(far_rows, TILE).astype(jnp.bfloat16)
            ref[p % 2, far_rows:] = full[:, PICKS].reshape(BLOCK, TILE).astype(jnp.bfloat16)

    bias = bias_ref[2:3, :]
    project(0)
    fetch.wait("q")
    for p in range(STEPS):
        at = _tile(p)
        if p + 1 < STEPS:
            project(p + 1)
        if p == 0:
            fetch.wait("o", "l", "m")
        rows = slice(0, BLOCK)
        far = _stage(
            q_ref[rows, at], keys_ref.at[p % 2], values_ref.at[p % 2], scores_ref.at[p % 2],
            weight_ref.at[p % 2], bias,
        )
        out, total, _ = _join((o_ref[rows, at], l_ref[rows, at], m_ref[rows, at]), far)
        context_ref[:, at] = (out / total).astype(jnp.bfloat16)
        rows = slice(BLOCK, ROWS)
        glob = pl.ds(far_rows, BLOCK)
        far = _stage(
            q_ref[rows, at], keys_ref.at[p % 2, glob], values_ref.at[p % 2, glob],
            scores1_ref.at[p % 2], weight1_ref.at[p % 2], bias[:, far_rows:],
        )
        joined = _join((o_ref[rows, at], l_ref[rows, at], m_ref[rows, at]), far)
        for ref, val in zip((o1_ref, l1_ref, m1_ref), joined):
            ref[:, at] = val
    fetch.wait("wo")
    _finish(context_ref[...], wo_ref, acc, out_ref, gain_ref, rank_ref[0] * 2 < len_ref[0])


def _second_kernel(
    rank_ref, len_ref, rows_ref, bias_ref, q_hbm, o_hbm, l_hbm, m_hbm, wkv_hbm, wo_hbm, gain_ref,
    prev_ref, out_ref, acc, q_ref, o_ref, l_ref, m_ref, wkv_ref, wo_ref, sem,
    keys_ref, values_ref, scores_ref, weight_ref, context_ref,
):
    fetch = _Fetch(
        slice(BLOCK, ROWS), q_hbm, o_hbm, l_hbm, m_hbm, wkv_hbm, wo_hbm,
        (q_ref, o_ref, l_ref, m_ref, wkv_ref, wo_ref), sem,
    )

    def project(p):
        fetch.wait(("w", 0, p), ("w", D, p))
        for base, ref in ((0, keys_ref), (D, values_ref)):
            ref[p % 2] = _dot(rows_ref[...], wkv_ref[:, _tile(p, base)]).astype(jnp.bfloat16)

    bias = bias_ref[3:4, : PICKS * BLOCK]
    project(0)
    fetch.wait("q")
    for p in range(STEPS):
        at = _tile(p)
        if p + 1 < STEPS:
            project(p + 1)
        if p == 0:
            fetch.wait("o", "l", "m")
        far = _stage(
            q_ref[:, at], keys_ref.at[p % 2], values_ref.at[p % 2], scores_ref.at[p % 2],
            weight_ref.at[p % 2], bias,
        )
        near = (o_ref[:, at], l_ref[:, at], m_ref[:, at])
        out, total, _ = _join(near, far)
        context_ref[:, at] = (out / total).astype(jnp.bfloat16)
    fetch.wait("wo")
    _finish(context_ref[...], wo_ref, acc, out_ref, gain_ref, rank_ref[0] * 2 + 1 < len_ref[0])


def _late(rows, *widths):
    wide = widths[0]
    scratch = [
        VM((LT, BLOCK, 128), jnp.float32),
        VM((rows, D), jnp.bfloat16),
        *[VM((rows, D), jnp.float32)] * 3,
        VM((D, 2 * D), jnp.bfloat16),
        VM((D, D), jnp.bfloat16),
        pltpu.SemaphoreType.DMA((2 * STEPS + 5,)),
        VM((2, wide, TILE), jnp.bfloat16),
        VM((2, wide, TILE), jnp.bfloat16),
        VM((2, 4 * BLOCK, wide), jnp.float32),
        VM((2, 4 * BLOCK, wide), jnp.bfloat16),
        VM((BLOCK, D), jnp.bfloat16),
    ]
    for width in widths[1:]:
        scratch += [VM((2, 4 * BLOCK, width), jnp.float32), VM((2, 4 * BLOCK, width), jnp.bfloat16)]
    return dict(grid=(1,), scratch_shapes=scratch)


LATE_SPECS = [
    *[pl.BlockSpec(memory_space=SM)] * 2,
    *[pl.BlockSpec(memory_space=VM)] * 2,
    *[pl.BlockSpec(memory_space=pl.ANY)] * 6,
    pl.BlockSpec(memory_space=VM),
]


def first(rank, length, rows, bias, q, o, l, m, w_kv, w_out, gain):
    f32 = jax.ShapeDtypeStruct((BLOCK, D), jnp.float32)
    rows = pltpu.with_memory_space_constraint(rows, VM)
    return pl.pallas_call(
        _first_kernel,
        out_shape=(jax.ShapeDtypeStruct((64, D), jnp.bfloat16), f32, f32, f32),
        in_specs=LATE_SPECS,
        out_specs=(pl.BlockSpec((32, D), lambda p: (0, 0)),) + (_whole((BLOCK, D)),) * 3,
        name="first",
        **_late(ROWS, SUBS_A * BLOCK, BLOCK),
    )(rank, length, rows, bias, q, o, l, m, w_kv, w_out, gain)


def second(rank, length, rows, bias, q, o, l, m, w_kv, w_out, gain, prev):
    rows = pltpu.with_memory_space_constraint(rows, VM)
    return pl.pallas_call(
        _second_kernel,
        out_shape=jax.ShapeDtypeStruct((64, D), jnp.bfloat16),
        in_specs=LATE_SPECS + [pl.BlockSpec(memory_space=pl.ANY)],
        out_specs=pl.BlockSpec((32, D), lambda p: (1, 0)),
        input_output_aliases={11: 0},
        name="second",
        **_late(BLOCK, SUBS_B * BLOCK),
    )(rank, length, rows, bias, q, o, l, m, w_kv, w_out, gain, prev)


def exchange(value):
    return lax.all_to_all(value, "tm", split_axis=0, concat_axis=0, tiled=True)


def program(frames, w_query, w_kv, w_out, norm_gain, rand_owner, rand_slot, global_pos, length):
    shards = lax.axis_size("tm")
    rank = lax.axis_index("tm").astype(jnp.int32).reshape(1)
    gpos = global_pos.reshape(1, BLOCK)
    gain = norm_gain.reshape(1, D)
    up = [(i, i + 1) for i in range(shards - 1)]
    down = [(j, i) for i, j in up]
    packed = pack(rank, rand_owner, rand_slot, frames, gpos)
    held = exchange(packed)
    q, k, v, bias = own_part(rank, length, rand_owner, rand_slot, gpos, frames, w_query, w_kv)
    lo = lax.ppermute(frames[BLOCK:], "tm", up)
    hi = lax.ppermute(frames[:BLOCK], "tm", down)
    send_a, send_b = select(held)
    got_a = exchange(send_a).reshape(SUBS_A * BLOCK, D)
    got_b = exchange(send_b).reshape(SUBS_B * BLOCK, D)
    o, l, m = halo_part(lo, hi, bias, q, k, v, w_kv)
    half, o1, l1, m1 = first(rank, length, got_a, bias, q, o, l, m, w_kv, w_out, gain)
    return second(rank, length, got_b, bias, q, o1, l1, m1, w_kv, w_out, gain, half)


def solution(mesh):
    placed = (
        P(("rec", "tm"), None),
        P(),
        P(),
        P(),
        P(),
        P(("rec", "tm"), None),
        P(("rec", "tm"), None),
        P("rec"),
        P("rec"),
    )
    return jax.shard_map(
        program, mesh=mesh, in_specs=placed, out_specs=P(("rec", "tm"), None), check_vma=False
    )
```

```python
import jax
import jax.numpy as jnp
from jax import lax
from jax.experimental import pallas as pl
from jax.experimental.pallas import tpu as pltpu
from jax.sharding import PartitionSpec as P


BLOCK = 128
POOL = 4
PICKS = 3
D = 1280
HD = 64
TILE = 256
STEPS = D // TILE
SHARDS = 16
SUB = BLOCK // SHARDS
ROWS = 256
SUBS = 2 * PICKS + 1
LT = D // 128
NEG = -1e30

VM = pltpu.VMEM
SM = pltpu.SMEM


def _pack_kernel(rank_ref, owner_ref, slot_ref, frames_ref, gpos_ref, out_ref):
    frames = frames_ref[...]
    for blk in range(2):
        for c in range(LT):
            piece = frames_ref[blk * BLOCK : (blk + 1) * BLOCK, c * 128 : (c + 1) * 128]
            out_ref[:, blk * LT + c] = piece.reshape(SHARDS, SUB, 128)
    local = (gpos_ref[...] - rank_ref[0] * ROWS).astype(jnp.float32)
    local = jnp.broadcast_to(local, (8, BLOCK)).T[:, :1]
    cols = lax.broadcasted_iota(jnp.int32, (BLOCK, ROWS), 1).astype(jnp.float32)
    onehot = jnp.where(cols == local, 1.0, 0.0).astype(jnp.bfloat16)
    picked = jnp.dot(onehot, frames, preferred_element_type=jnp.float32)
    for c in range(LT):
        piece = picked[:, c * 128 : (c + 1) * 128].reshape(SHARDS, SUB, 128)
        out_ref[:, 2 * LT + c] = piece.astype(jnp.bfloat16)
    lane = lax.broadcasted_iota(jnp.int32, (SUB, 128), 1)
    codes = jnp.zeros((SUB, 128), jnp.int32)
    for q in range(2):
        for j in range(PICKS):
            code = (slot_ref[q, j] * SHARDS + owner_ref[q, j]) * SUB
            codes = jnp.where(lane == q * PICKS + j, code, codes)
    codes = codes + lax.broadcasted_iota(jnp.int32, (SUB, 128), 0)
    codes = codes.astype(jnp.float32).astype(jnp.bfloat16)
    for s in range(SHARDS):
        out_ref[s, 3 * LT] = codes


def pack(rank, owner, slot, frames, gpos):
    return pl.pallas_call(
        _pack_kernel,
        out_shape=VM((SHARDS, 3 * LT + 1, SUB, 128), jnp.bfloat16),
        in_specs=[pl.BlockSpec(memory_space=SM)] * 3 + [pl.BlockSpec(memory_space=VM)] * 2,
        out_specs=pl.BlockSpec(memory_space=VM),
        name="pack",
    )(rank, owner, slot, frames, gpos)


def _select_kernel(held_ref, out_ref, buf, sem):
    copies = []

    def send(k, dest):
        copy = pltpu.make_async_copy(buf.at[k], dest, sem.at[k])
        copy.start()
        copies.append(copy)

    codes = held_ref[:, 3 * LT].astype(jnp.float32).reshape(BLOCK, 128)
    blocks = []
    for slot in range(2):
        tiles = [
            held_ref[:, slot * LT + c].astype(jnp.float32).reshape(BLOCK, 128).astype(jnp.bfloat16)
            for c in range(LT)
        ]
        blocks.append(jnp.concatenate(tiles, axis=1))
    rows = jnp.concatenate(blocks, axis=0)
    cols = lax.broadcasted_iota(jnp.int32, (BLOCK, ROWS), 1).astype(jnp.float32)
    for c in range(LT):
        total = held_ref[0, 2 * LT + c].astype(jnp.float32)
        for i in range(1, SHARDS):
            total = total + held_ref[i, 2 * LT + c].astype(jnp.float32)
        total = total.astype(jnp.bfloat16)
        for r in range(SHARDS):
            buf[2 * PICKS, r, :, c * 128 : (c + 1) * 128] = total
    send(2 * PICKS, out_ref.at[:, 2 * PICKS])
    for k in range(2 * PICKS):
        onehot = jnp.where(cols == codes[:, k : k + 1], 1.0, 0.0).astype(jnp.bfloat16)
        got = jnp.dot(onehot, rows, preferred_element_type=jnp.float32)
        buf[k] = got.reshape(SHARDS, SUB, D).astype(jnp.bfloat16)
        send(k, out_ref.at[:, k])
    for copy in copies:
        copy.wait()


def select(held):
    return pl.pallas_call(
        _select_kernel,
        out_shape=jax.ShapeDtypeStruct((SHARDS, SUBS, SUB, D), jnp.bfloat16),
        in_specs=[pl.BlockSpec(memory_space=VM)],
        out_specs=pl.BlockSpec(memory_space=pl.ANY),
        scratch_shapes=[
            pltpu.VMEM((2 * PICKS + 1, SHARDS, SUB, D), jnp.bfloat16),
            pltpu.SemaphoreType.DMA((2 * PICKS + 1,)),
        ],
        name="select",
    )(pltpu.with_memory_space_constraint(held, VM))


def _dot(a, b):
    return jnp.dot(a, b, preferred_element_type=jnp.float32)


def _scores(query, keys):
    lanes = lax.broadcasted_iota(jnp.int32, (BLOCK, TILE), 1) // HD
    zero = jnp.zeros_like(query)
    stacked = jnp.concatenate([jnp.where(lanes == i, query, zero) for i in range(4)], axis=0)
    return lax.dot_general(
        stacked, keys, (((1,), (1,)), ((), ())), preferred_element_type=jnp.float32
    )


def _weigh(scores, values, bias):
    scores = scores + bias
    top = jnp.max(scores, axis=1, keepdims=True)
    weight = jnp.exp(scores - top).astype(jnp.bfloat16)
    ones = jnp.ones((values.shape[0], 128), jnp.bfloat16)
    low = lax.broadcasted_iota(jnp.int32, (BLOCK, 128), 1) < HD
    outs, sums, tops = [], [], []
    for pair in range(2):
        ext = jnp.concatenate([values[:, pair * 128 : (pair + 1) * 128], ones], axis=1)
        res = _dot(weight[pair * 256 : (pair + 1) * 256], ext)
        outs.append(jnp.where(low, res[:BLOCK, :128], res[BLOCK:, :128]))
        sums.append(jnp.where(low, res[:BLOCK, 128:], res[BLOCK:, 128:]))
        tops.append(
            jnp.where(
                low,
                top[pair * 256 : pair * 256 + BLOCK],
                top[pair * 256 + BLOCK : (pair + 1) * 256],
            )
        )
    return tuple(jnp.concatenate(x, axis=1) for x in (outs, sums, tops))


def _attend(query, keys, values, bias):
    return _weigh(_scores(query, keys), values, bias)


def _join(near, far):
    both = jnp.maximum(near[2], far[2])
    a = jnp.exp(near[2] - both)
    b = jnp.exp(far[2] - both)
    return a * near[0] + b * far[0], a * near[1] + b * far[1], both


def _own_kernel(
    rank_ref, len_ref, owner_ref, slot_ref, gpos_ref, own_ref, wq_ref, wk_ref, wv_ref,
    q_ref, k_ref, v_ref, bias_ref,
):
    own = own_ref[...]
    q_ref[...] = _dot(own, wq_ref[...]).astype(jnp.bfloat16) * jnp.bfloat16(0.125)
    k_ref[...] = _dot(own, wk_ref[...]).astype(jnp.bfloat16)
    v_ref[...] = _dot(own, wv_ref[...]).astype(jnp.bfloat16)

    @pl.when(pl.program_id(0) == 0)
    def _():
        live = len_ref[0]
        lane = lax.broadcasted_iota(jnp.int32, (1, 4 * BLOCK), 1)

        def row(parts):
            dead = lane < 0
            for at, block in parts:
                dead = dead | (at & ((block < 0) | (block >= live)))
            return jnp.where(dead, NEG, 0.0)

        def picked(q, j):
            return owner_ref[q, j] * 2 + slot_ref[q, j]

        for q in range(2):
            near = [(lane // BLOCK == i, rank_ref[0] * 2 + q - 1 + i) for i in range(3)]
            bias_ref[q : q + 1, :] = row(near)
        glob = jnp.where(gpos_ref[...] < live * BLOCK, 0.0, NEG)
        rows = lane // SUB
        for q in range(2):
            far = row([((rows % PICKS == j), picked(q, j)) for j in range(PICKS)])
            parts = [far[:, : PICKS * BLOCK], glob]
            bias_ref[2 + q : 3 + q, :] = jnp.concatenate(parts if q == 0 else parts[::-1], axis=1)
        bias_ref[4:8, :] = jnp.zeros((4, 4 * BLOCK), jnp.float32)


def _halo_kernel(lo_ref, hi_ref, bias_ref, q_ref, k_ref, v_ref, wk_ref, wv_ref, o_ref, l_ref, m_ref):
    rim = jnp.concatenate([lo_ref[...], hi_ref[...]], axis=0)

    def widen(own_ref, w_ref):
        far = _dot(rim, w_ref[...]).astype(jnp.bfloat16)
        return jnp.concatenate([far[:BLOCK], own_ref[...], far[BLOCK:]], axis=0)

    keys = widen(k_ref, wk_ref)
    values = widen(v_ref, wv_ref)
    for b in range(2):
        at = slice(b * BLOCK, b * BLOCK + 3 * BLOCK)
        res = _attend(
            q_ref[b * BLOCK : (b + 1) * BLOCK], keys[at], values[at], bias_ref[b : b + 1, : 3 * BLOCK]
        )
        for ref, val in zip((o_ref, l_ref, m_ref), res):
            ref[b * BLOCK : (b + 1) * BLOCK, :] = val


def _whole(shape):
    return pl.BlockSpec(shape, lambda p: (0,) * len(shape))


def _cols(rows, shift=0):
    return pl.BlockSpec((rows, TILE), lambda p: (0, p + shift))


def own_part(rank, length, owner, slot, gpos, own, w_query, w_kv):
    half = jax.ShapeDtypeStruct((ROWS, D), jnp.bfloat16)
    return pl.pallas_call(
        _own_kernel,
        grid=(STEPS,),
        out_shape=(half, half, half, jax.ShapeDtypeStruct((8, 4 * BLOCK), jnp.float32)),
        in_specs=[pl.BlockSpec(memory_space=SM)] * 4
        + [_whole((1, BLOCK)), _whole((ROWS, D)), _cols(D), _cols(D), _cols(D, STEPS)],
        out_specs=(_cols(ROWS),) * 3 + (_whole((8, 4 * BLOCK)),),
        name="own",
    )(rank, length, owner, slot, gpos, own, w_query, w_kv, w_kv)


def halo_part(lo, hi, bias, q, k, v, w_kv):
    f32 = jax.ShapeDtypeStruct((ROWS, D), jnp.float32)
    lo = pltpu.with_memory_space_constraint(lo, VM)
    hi = pltpu.with_memory_space_constraint(hi, VM)
    return pl.pallas_call(
        _halo_kernel,
        grid=(STEPS,),
        out_shape=(f32, f32, f32),
        in_specs=[
            pl.BlockSpec(memory_space=VM),
            pl.BlockSpec(memory_space=VM),
            _whole((8, 4 * BLOCK)),
            *[_cols(ROWS)] * 3,
            _cols(D),
            _cols(D, STEPS),
        ],
        out_specs=(_cols(ROWS),) * 3,
        name="halo",
    )(lo, hi, bias, q, k, v, w_kv, w_kv)


def _finish(projected, acc, gain_ref, live):
    tiles = []
    for c in range(LT):
        acc[c] = projected[:, c * 128 : (c + 1) * 128]
    for c in range(LT):
        total = acc[c, pl.ds(0, 32, stride=POOL), :]
        for i in range(1, POOL):
            total = total + acc[c, pl.ds(i, 32, stride=POOL), :]
        tiles.append(total)
    pooled = jnp.concatenate(tiles, axis=1) * (1.0 / POOL)
    mean = jnp.mean(pooled, axis=1, keepdims=True)
    centered = pooled - mean
    var = jnp.mean(centered * centered, axis=1, keepdims=True)
    normed = centered * lax.rsqrt(var + 1e-05) * gain_ref[...]
    return jnp.where(live, normed, 0.0).astype(jnp.bfloat16)


def _tile(p, base=0):
    return slice(base + p * TILE, base + (p + 1) * TILE)


def _stage(query, keys_ref, values_ref, scores_ref, weight_ref, bias):
    width = keys_ref.shape[0]
    scores_ref[:, :width] = _scores(query, keys_ref[...])
    tops = []
    for r in range(0, 4 * BLOCK, 64):
        piece = scores_ref[r : r + 64, :width] + bias
        top = jnp.max(piece, axis=1, keepdims=True)
        weight_ref[r : r + 64, :width] = jnp.exp(piece - top).astype(jnp.bfloat16)
        tops.append(top)
    top = jnp.concatenate(tops, axis=0)
    ones = jnp.ones((width, 128), jnp.bfloat16)
    low = lax.broadcasted_iota(jnp.int32, (BLOCK, 128), 1) < HD
    outs, sums, maxes = [], [], []
    for pair in range(2):
        base = pair * 256
        ext = jnp.concatenate([values_ref[:, pair * 128 : (pair + 1) * 128], ones], axis=1)
        res = _dot(weight_ref[base : base + 256, :width], ext)
        outs.append(jnp.where(low, res[:BLOCK, :128], res[BLOCK:, :128]))
        sums.append(jnp.where(low, res[:BLOCK, 128:], res[BLOCK:, 128:]))
        maxes.append(jnp.where(low, top[base : base + BLOCK], top[base + BLOCK : base + 256]))
    return tuple(jnp.concatenate(x, axis=1) for x in (outs, sums, maxes))


class _Fetch:
    def __init__(self, q_ref, o_ref, l_ref, m_ref, wkv_ref, wo_ref, bufs, sem):
        q, o, l, m, wkv, wo = bufs
        self.copies = {}
        count = 0

        def start(key, src, dst):
            nonlocal count
            copy = pltpu.make_async_copy(src, dst, sem.at[count])
            copy.start()
            self.copies[key] = copy
            count += 1

        def weights(p, base):
            at = _tile(p, base)
            start(("w", base, p), wkv_ref.at[:, at], wkv.at[:, at])

        weights(0, 0)
        start("q", q_ref, q)
        weights(0, D)
        weights(1, 0)
        for key, src, dst in (("o", o_ref, o), ("l", l_ref, l), ("m", m_ref, m)):
            start(key, src, dst)
        for p in range(1, STEPS):
            weights(p, D)
            if p + 1 < STEPS:
                weights(p + 1, 0)
        start("wo", wo_ref, wo)

    def wait(self, *keys):
        for key in keys:
            self.copies.pop(key).wait()


def _late_kernel(
    rank_ref, len_ref, rows_ref, bias_ref, q_hbm, o_hbm, l_hbm, m_hbm, wkv_hbm, wo_hbm, gain_ref,
    out_ref, acc, q_ref, o_ref, l_ref, m_ref, wkv_ref, wo_ref, sem,
    keys_ref, values_ref, scores_ref, weight_ref, context_ref,
):
    fetch = _Fetch(
        q_hbm, o_hbm, l_hbm, m_hbm, wkv_hbm, wo_hbm, (q_ref, o_ref, l_ref, m_ref, wkv_ref, wo_ref), sem
    )
    near = PICKS * BLOCK

    def project(p):
        fetch.wait(("w", 0, p), ("w", D, p))
        both = [_dot(rows_ref[...], wkv_ref[:, _tile(p, base)]) for base in (0, D)]
        for full, ref in zip(both, (keys_ref, values_ref)):
            full = full.reshape(SHARDS, SUBS, SUB, TILE)
            ref[p % 2, :near] = full[:, :PICKS].reshape(near, TILE).astype(jnp.bfloat16)
            ref[p % 2, near : near + BLOCK] = full[:, 2 * PICKS].reshape(BLOCK, TILE).astype(jnp.bfloat16)
            ref[p % 2, near + BLOCK :] = full[:, PICKS : 2 * PICKS].reshape(near, TILE).astype(jnp.bfloat16)

    project(0)
    fetch.wait("q")
    for p in range(STEPS):
        at = _tile(p)
        if p + 1 < STEPS:
            project(p + 1)
        if p == 0:
            fetch.wait("o", "l", "m")
        for b in range(2):
            rows = slice(b * BLOCK, (b + 1) * BLOCK)
            used = pl.ds(b * near, near + BLOCK)
            far = _stage(
                q_ref[rows, at], keys_ref.at[p % 2, used], values_ref.at[p % 2, used],
                scores_ref.at[b], weight_ref.at[b], bias_ref[2 + b : 3 + b, :],
            )
            out, total, _ = _join((o_ref[rows, at], l_ref[rows, at], m_ref[rows, at]), far)
            context_ref[rows, at] = (out / total).astype(jnp.bfloat16)
    fetch.wait("wo")
    projected = _dot(context_ref[...], wo_ref[...])
    for b in range(2):
        live = rank_ref[0] * 2 + b < len_ref[0]
        part = projected[b * BLOCK : (b + 1) * BLOCK]
        out_ref[b * 32 : (b + 1) * 32, :] = _finish(part, acc.at[b], gain_ref, live)


def late(rank, length, rows, bias, q, o, l, m, w_kv, w_out, gain):
    rows = pltpu.with_memory_space_constraint(rows, VM)
    return pl.pallas_call(
        _late_kernel,
        out_shape=jax.ShapeDtypeStruct((64, D), jnp.bfloat16),
        in_specs=[
            *[pl.BlockSpec(memory_space=SM)] * 2,
            *[pl.BlockSpec(memory_space=VM)] * 2,
            *[pl.BlockSpec(memory_space=pl.ANY)] * 6,
            pl.BlockSpec(memory_space=VM),
        ],
        out_specs=pl.BlockSpec(memory_space=VM),
        scratch_shapes=[
            VM((2, LT, BLOCK, 128), jnp.float32),
            VM((ROWS, D), jnp.bfloat16),
            *[VM((ROWS, D), jnp.float32)] * 3,
            VM((D, 2 * D), jnp.bfloat16),
            VM((D, D), jnp.bfloat16),
            pltpu.SemaphoreType.DMA((2 * STEPS + 5,)),
            VM((2, SUBS * BLOCK, TILE), jnp.bfloat16),
            VM((2, SUBS * BLOCK, TILE), jnp.bfloat16),
            VM((2, 4 * BLOCK, 4 * BLOCK), jnp.float32),
            VM((2, 4 * BLOCK, 4 * BLOCK), jnp.bfloat16),
            VM((ROWS, D), jnp.bfloat16),
        ],
        name="late",
    )(rank, length, rows, bias, q, o, l, m, w_kv, w_out, gain)


def exchange(value):
    return lax.all_to_all(value, "tm", split_axis=0, concat_axis=0, tiled=True)


def program(frames, w_query, w_kv, w_out, norm_gain, rand_owner, rand_slot, global_pos, length):
    shards = lax.axis_size("tm")
    rank = lax.axis_index("tm").astype(jnp.int32).reshape(1)
    gpos = global_pos.reshape(1, BLOCK)
    gain = norm_gain.reshape(1, D)
    up = [(i, i + 1) for i in range(shards - 1)]
    down = [(j, i) for i, j in up]
    packed = pack(rank, rand_owner, rand_slot, frames, gpos)
    held = exchange(packed)
    q, k, v, bias = own_part(rank, length, rand_owner, rand_slot, gpos, frames, w_query, w_kv)
    lo = lax.ppermute(frames[BLOCK:], "tm", up)
    hi = lax.ppermute(frames[:BLOCK], "tm", down)
    reply = select(held)
    got = exchange(reply).reshape(SUBS * BLOCK, D)
    o, l, m = halo_part(lo, hi, bias, q, k, v, w_kv)
    return late(rank, length, got, bias, q, o, l, m, w_kv, w_out, gain)


def solution(mesh):
    placed = (
        P(("rec", "tm"), None),
        P(),
        P(),
        P(),
        P(),
        P(("rec", "tm"), None),
        P(("rec", "tm"), None),
        P("rec"),
        P("rec"),
    )
    return jax.shard_map(
        program, mesh=mesh, in_specs=placed, out_specs=P(("rec", "tm"), None), check_vma=False
    )
```

```python
import jax
import jax.numpy as jnp
from jax import lax
from jax.experimental import pallas as pl
from jax.experimental.pallas import tpu as pltpu
from jax.sharding import PartitionSpec as P


BLOCK = 128
POOL = 4
PICKS = 3
D = 1280
HD = 64
TILE = 256
STEPS = D // TILE
SHARDS = 16
SUB = BLOCK // SHARDS
ROWS = 256
SUBS_A = PICKS + 2
SUBS_B = PICKS - 1
LT = D // 128
NEG = -1e30

VM = pltpu.VMEM
SM = pltpu.SMEM


def _pack_kernel(rank_ref, owner_ref, slot_ref, frames_ref, gpos_ref, out_ref):
    frames = frames_ref[...]
    for blk in range(2):
        for c in range(LT):
            piece = frames_ref[blk * BLOCK : (blk + 1) * BLOCK, c * 128 : (c + 1) * 128]
            out_ref[:, blk * LT + c] = piece.reshape(SHARDS, SUB, 128)
    local = (gpos_ref[...] - rank_ref[0] * ROWS).astype(jnp.float32)
    local = jnp.broadcast_to(local, (8, BLOCK)).T[:, :1]
    cols = lax.broadcasted_iota(jnp.int32, (BLOCK, ROWS), 1).astype(jnp.float32)
    onehot = jnp.where(cols == local, 1.0, 0.0).astype(jnp.bfloat16)
    picked = jnp.dot(onehot, frames, preferred_element_type=jnp.float32)
    for c in range(LT):
        piece = picked[:, c * 128 : (c + 1) * 128].reshape(SHARDS, SUB, 128)
        out_ref[:, 2 * LT + c] = piece.astype(jnp.bfloat16)
    lane = lax.broadcasted_iota(jnp.int32, (SUB, 128), 1)
    codes = jnp.zeros((SUB, 128), jnp.int32)
    for q in range(2):
        for j in range(PICKS):
            code = (slot_ref[q, j] * SHARDS + owner_ref[q, j]) * SUB
            codes = jnp.where(lane == q * PICKS + j, code, codes)
    codes = codes + lax.broadcasted_iota(jnp.int32, (SUB, 128), 0)
    codes = codes.astype(jnp.float32).astype(jnp.bfloat16)
    for s in range(SHARDS):
        out_ref[s, 3 * LT] = codes


def pack(rank, owner, slot, frames, gpos):
    return pl.pallas_call(
        _pack_kernel,
        out_shape=VM((SHARDS, 3 * LT + 1, SUB, 128), jnp.bfloat16),
        in_specs=[pl.BlockSpec(memory_space=SM)] * 3 + [pl.BlockSpec(memory_space=VM)] * 2,
        out_specs=pl.BlockSpec(memory_space=VM),
        name="pack",
    )(rank, owner, slot, frames, gpos)


def _select_kernel(held_ref, a_ref, b_ref, buf, sem):
    copies = []

    def send(k, dest):
        copy = pltpu.make_async_copy(buf.at[k], dest, sem.at[k])
        copy.start()
        copies.append(copy)

    codes = held_ref[:, 3 * LT].astype(jnp.float32).reshape(BLOCK, 128)
    blocks = []
    for slot in range(2):
        tiles = [
            held_ref[:, slot * LT + c].astype(jnp.float32).reshape(BLOCK, 128).astype(jnp.bfloat16)
            for c in range(LT)
        ]
        blocks.append(jnp.concatenate(tiles, axis=1))
    rows = jnp.concatenate(blocks, axis=0)
    cols = lax.broadcasted_iota(jnp.int32, (BLOCK, ROWS), 1).astype(jnp.float32)
    for c in range(LT):
        total = held_ref[0, 2 * LT + c].astype(jnp.float32)
        for i in range(1, SHARDS):
            total = total + held_ref[i, 2 * LT + c].astype(jnp.float32)
        total = total.astype(jnp.bfloat16)
        for r in range(SHARDS):
            buf[2 * PICKS, r, :, c * 128 : (c + 1) * 128] = total
    send(2 * PICKS, a_ref.at[:, SUBS_A - 1])
    for k in range(2 * PICKS):
        onehot = jnp.where(cols == codes[:, k : k + 1], 1.0, 0.0).astype(jnp.bfloat16)
        got = jnp.dot(onehot, rows, preferred_element_type=jnp.float32)
        buf[k] = got.reshape(SHARDS, SUB, D).astype(jnp.bfloat16)
        send(k, a_ref.at[:, k] if k < SUBS_A - 1 else b_ref.at[:, k - SUBS_A + 1])
    for copy in copies:
        copy.wait()


def select(held):
    return pl.pallas_call(
        _select_kernel,
        out_shape=(
            jax.ShapeDtypeStruct((SHARDS, SUBS_A, SUB, D), jnp.bfloat16),
            jax.ShapeDtypeStruct((SHARDS, SUBS_B, SUB, D), jnp.bfloat16),
        ),
        in_specs=[pl.BlockSpec(memory_space=VM)],
        out_specs=(pl.BlockSpec(memory_space=pl.ANY), pl.BlockSpec(memory_space=pl.ANY)),
        scratch_shapes=[
            pltpu.VMEM((2 * PICKS + 1, SHARDS, SUB, D), jnp.bfloat16),
            pltpu.SemaphoreType.DMA((2 * PICKS + 1,)),
        ],
        name="select",
    )(pltpu.with_memory_space_constraint(held, VM))


def _dot(a, b):
    return jnp.dot(a, b, preferred_element_type=jnp.float32)


def _scores(query, keys):
    lanes = lax.broadcasted_iota(jnp.int32, (BLOCK, TILE), 1) // HD
    zero = jnp.zeros_like(query)
    stacked = jnp.concatenate([jnp.where(lanes == i, query, zero) for i in range(4)], axis=0)
    return lax.dot_general(
        stacked, keys, (((1,), (1,)), ((), ())), preferred_element_type=jnp.float32
    )


def _weigh(scores, values, bias):
    scores = scores + bias
    top = jnp.max(scores, axis=1, keepdims=True)
    weight = jnp.exp(scores - top).astype(jnp.bfloat16)
    ones = jnp.ones((values.shape[0], 128), jnp.bfloat16)
    low = lax.broadcasted_iota(jnp.int32, (BLOCK, 128), 1) < HD
    outs, sums, tops = [], [], []
    for pair in range(2):
        ext = jnp.concatenate([values[:, pair * 128 : (pair + 1) * 128], ones], axis=1)
        res = _dot(weight[pair * 256 : (pair + 1) * 256], ext)
        outs.append(jnp.where(low, res[:BLOCK, :128], res[BLOCK:, :128]))
        sums.append(jnp.where(low, res[:BLOCK, 128:], res[BLOCK:, 128:]))
        tops.append(
            jnp.where(
                low,
                top[pair * 256 : pair * 256 + BLOCK],
                top[pair * 256 + BLOCK : (pair + 1) * 256],
            )
        )
    return tuple(jnp.concatenate(x, axis=1) for x in (outs, sums, tops))


def _attend(query, keys, values, bias):
    return _weigh(_scores(query, keys), values, bias)


def _join(near, far):
    both = jnp.maximum(near[2], far[2])
    a = jnp.exp(near[2] - both)
    b = jnp.exp(far[2] - both)
    return a * near[0] + b * far[0], a * near[1] + b * far[1], both


def _own_kernel(
    rank_ref, len_ref, owner_ref, slot_ref, gpos_ref, own_ref, gain_ref, wq_ref, wk_ref, wv_ref,
    q_ref, k_ref, v_ref, bias_ref, keep_ref,
):
    keep_ref[...] = gain_ref[...]
    own = own_ref[...]
    q_ref[...] = _dot(own, wq_ref[...]).astype(jnp.bfloat16) * jnp.bfloat16(0.125)
    k_ref[...] = _dot(own, wk_ref[...]).astype(jnp.bfloat16)
    v_ref[...] = _dot(own, wv_ref[...]).astype(jnp.bfloat16)

    @pl.when(pl.program_id(0) == 0)
    def _():
        live = len_ref[0]
        lane = lax.broadcasted_iota(jnp.int32, (1, 4 * BLOCK), 1)

        def row(parts):
            dead = lane < 0
            for at, block in parts:
                dead = dead | (at & ((block < 0) | (block >= live)))
            return jnp.where(dead, NEG, 0.0)

        def picked(q, j):
            return owner_ref[q, j] * 2 + slot_ref[q, j]

        for q in range(2):
            near = [(lane // BLOCK == i, rank_ref[0] * 2 + q - 1 + i) for i in range(3)]
            bias_ref[q : q + 1, :] = row(near)
        glob = jnp.where(gpos_ref[...] < live * BLOCK, 0.0, NEG)
        rows = lane // SUB
        far = row([(rows % PICKS == j, picked(0, j)) for j in range(PICKS)])
        bias_ref[2:3, :] = jnp.concatenate([far[:, : PICKS * BLOCK], glob], axis=1)
        one = row([(lane >= 0, picked(1, 0))])
        far = row([(rows % SUBS_B == j, picked(1, j + 1)) for j in range(SUBS_B)])
        parts = [glob, one[:, :BLOCK], far[:, : SUBS_B * BLOCK]]
        bias_ref[3:4, :] = jnp.concatenate(parts, axis=1)
        bias_ref[4:8, :] = jnp.zeros((4, 4 * BLOCK), jnp.float32)


def _halo_kernel(lo_ref, hi_ref, bias_ref, q_ref, k_ref, v_ref, wk_ref, wv_ref, o_ref, l_ref, m_ref):
    rim = jnp.concatenate([lo_ref[...], hi_ref[...]], axis=0)

    def widen(own_ref, w_ref):
        far = _dot(rim, w_ref[...]).astype(jnp.bfloat16)
        return jnp.concatenate([far[:BLOCK], own_ref[...], far[BLOCK:]], axis=0)

    keys = widen(k_ref, wk_ref)
    values = widen(v_ref, wv_ref)
    for b in range(2):
        at = slice(b * BLOCK, b * BLOCK + 3 * BLOCK)
        res = _attend(
            q_ref[b * BLOCK : (b + 1) * BLOCK], keys[at], values[at], bias_ref[b : b + 1, : 3 * BLOCK]
        )
        for ref, val in zip((o_ref, l_ref, m_ref), res):
            ref[b * BLOCK : (b + 1) * BLOCK, :] = val


def _whole(shape):
    return pl.BlockSpec(shape, lambda p: (0,) * len(shape))


def _cols(rows, shift=0):
    return pl.BlockSpec((rows, TILE), lambda p: (0, p + shift))


def own_part(rank, length, owner, slot, gpos, own, gain, w_query, w_kv):
    half = jax.ShapeDtypeStruct((ROWS, D), jnp.bfloat16)
    return pl.pallas_call(
        _own_kernel,
        grid=(STEPS,),
        out_shape=(
            half, half, half,
            jax.ShapeDtypeStruct((8, 4 * BLOCK), jnp.float32),
            jax.ShapeDtypeStruct((1, D), jnp.float32),
        ),
        in_specs=[pl.BlockSpec(memory_space=SM)] * 4
        + [_whole((1, BLOCK)), _whole((ROWS, D)), _whole((1, D)), _cols(D), _cols(D), _cols(D, STEPS)],
        out_specs=(_cols(ROWS),) * 3 + (_whole((8, 4 * BLOCK)), _whole((1, D))),
        name="own",
    )(rank, length, owner, slot, gpos, own, gain, w_query, w_kv, w_kv)


def halo_part(lo, hi, bias, q, k, v, w_kv):
    f32 = jax.ShapeDtypeStruct((ROWS, D), jnp.float32)
    lo = pltpu.with_memory_space_constraint(lo, VM)
    hi = pltpu.with_memory_space_constraint(hi, VM)
    return pl.pallas_call(
        _halo_kernel,
        grid=(STEPS,),
        out_shape=(f32, f32, f32),
        in_specs=[
            pl.BlockSpec(memory_space=VM),
            pl.BlockSpec(memory_space=VM),
            _whole((8, 4 * BLOCK)),
            *[_cols(ROWS)] * 3,
            _cols(D),
            _cols(D, STEPS),
        ],
        out_specs=(_cols(ROWS),) * 3,
        name="halo",
    )(lo, hi, bias, q, k, v, w_kv, w_kv)


def _finish(projected, acc, gain_ref, live):
    tiles = []
    for c in range(LT):
        acc[c] = projected[:, c * 128 : (c + 1) * 128]
    for c in range(LT):
        total = acc[c, pl.ds(0, 32, stride=POOL), :]
        for i in range(1, POOL):
            total = total + acc[c, pl.ds(i, 32, stride=POOL), :]
        tiles.append(total)
    pooled = jnp.concatenate(tiles, axis=1) * (1.0 / POOL)
    mean = jnp.mean(pooled, axis=1, keepdims=True)
    centered = pooled - mean
    var = jnp.mean(centered * centered, axis=1, keepdims=True)
    normed = centered * lax.rsqrt(var + 1e-05) * gain_ref[...]
    return jnp.where(live, normed, 0.0).astype(jnp.bfloat16)


def _tile(p, base=0):
    return slice(base + p * TILE, base + (p + 1) * TILE)


def _stage(query, keys_ref, values_ref, scores_ref, weight_ref, bias):
    width = keys_ref.shape[0]
    scores_ref[:, :width] = _scores(query, keys_ref[...])
    tops = []
    for r in range(0, 4 * BLOCK, 64):
        piece = scores_ref[r : r + 64, :width] + bias
        top = jnp.max(piece, axis=1, keepdims=True)
        weight_ref[r : r + 64, :width] = jnp.exp(piece - top).astype(jnp.bfloat16)
        tops.append(top)
    top = jnp.concatenate(tops, axis=0)
    ones = jnp.ones((width, 128), jnp.bfloat16)
    low = lax.broadcasted_iota(jnp.int32, (BLOCK, 128), 1) < HD
    outs, sums, maxes = [], [], []
    for pair in range(2):
        base = pair * 256
        ext = jnp.concatenate([values_ref[:, pair * 128 : (pair + 1) * 128], ones], axis=1)
        res = _dot(weight_ref[base : base + 256, :width], ext)
        outs.append(jnp.where(low, res[:BLOCK, :128], res[BLOCK:, :128]))
        sums.append(jnp.where(low, res[:BLOCK, 128:], res[BLOCK:, 128:]))
        maxes.append(jnp.where(low, top[base : base + BLOCK], top[base + BLOCK : base + 256]))
    return tuple(jnp.concatenate(x, axis=1) for x in (outs, sums, maxes))


class _Fetch:
    def __init__(self, q_ref, o_ref, l_ref, m_ref, wkv_ref, wo_ref, bufs, sem):
        q, o, l, m, wkv, wo = bufs
        self.copies = {}
        count = 0

        def start(key, src, dst):
            nonlocal count
            copy = pltpu.make_async_copy(src, dst, sem.at[count])
            copy.start()
            self.copies[key] = copy
            count += 1

        def weights(p, base):
            at = _tile(p, base)
            start(("w", base, p), wkv_ref.at[:, at], wkv.at[:, at])

        weights(0, 0)
        start("q", q_ref, q)
        weights(0, D)
        weights(1, 0)
        for key, src, dst in (("o", o_ref, o), ("l", l_ref, l), ("m", m_ref, m)):
            start(key, src, dst)
        for p in range(1, STEPS):
            weights(p, D)
            if p + 1 < STEPS:
                weights(p + 1, 0)
        start("wo", wo_ref, wo)

    def wait(self, *keys):
        for key in keys:
            self.copies.pop(key).wait()


def _first_kernel(
    rank_ref, len_ref, rows_ref, bias_ref, q_hbm, o_hbm, l_hbm, m_hbm, wkv_hbm, wo_hbm, gain_ref,
    out_ref, o1_ref, l1_ref, m1_ref, acc, q_ref, o_ref, l_ref, m_ref, wkv_ref, wo_ref, sem,
    keys_ref, values_ref, context_ref, scores_ref, weight_ref, scores1_ref, weight1_ref,
):
    fetch = _Fetch(
        q_hbm, o_hbm, l_hbm, m_hbm, wkv_hbm, wo_hbm, (q_ref, o_ref, l_ref, m_ref, wkv_ref, wo_ref), sem
    )
    near = PICKS * BLOCK

    def project(p):
        fetch.wait(("w", 0, p), ("w", D, p))
        both = [_dot(rows_ref[...], wkv_ref[:, _tile(p, base)]) for base in (0, D)]
        for full, ref in zip(both, (keys_ref, values_ref)):
            full = full.reshape(SHARDS, SUBS_A, SUB, TILE)
            ref[p % 2, :near] = full[:, :PICKS].reshape(near, TILE).astype(jnp.bfloat16)
            ref[p % 2, near : near + BLOCK] = full[:, PICKS + 1].reshape(BLOCK, TILE).astype(jnp.bfloat16)
            ref[p % 2, near + BLOCK :] = full[:, PICKS].reshape(BLOCK, TILE).astype(jnp.bfloat16)

    project(0)
    fetch.wait("q")
    for p in range(STEPS):
        at = _tile(p)
        if p + 1 < STEPS:
            project(p + 1)
        if p == 0:
            fetch.wait("o", "l", "m")
        rows = slice(0, BLOCK)
        used = pl.ds(0, near + BLOCK)
        far = _stage(
            q_ref[rows, at], keys_ref.at[p % 2, used], values_ref.at[p % 2, used],
            scores_ref.at[p % 2], weight_ref.at[p % 2], bias_ref[2:3, :],
        )
        out, total, _ = _join((o_ref[rows, at], l_ref[rows, at], m_ref[rows, at]), far)
        context_ref[:, at] = (out / total).astype(jnp.bfloat16)
        rows = slice(BLOCK, ROWS)
        used = pl.ds(near, 2 * BLOCK)
        far = _stage(
            q_ref[rows, at], keys_ref.at[p % 2, used], values_ref.at[p % 2, used],
            scores1_ref.at[p % 2], weight1_ref.at[p % 2], bias_ref[3:4, : 2 * BLOCK],
        )
        joined = _join((o_ref[rows, at], l_ref[rows, at], m_ref[rows, at]), far)
        for ref, val in zip((o1_ref, l1_ref, m1_ref), joined):
            ref[:, at] = val
    fetch.wait("wo")
    projected = _dot(context_ref[...], wo_ref[...])
    out_ref[...] = _finish(projected, acc, gain_ref, rank_ref[0] * 2 < len_ref[0])


def _second_kernel(
    rank_ref, len_ref, rows_ref, bias_ref, q_hbm, o_hbm, l_hbm, m_hbm, wkv_hbm, wo_hbm, gain_ref,
    prev_ref, out_ref, acc, q_ref, o_ref, l_ref, m_ref, wkv_ref, wo_ref, sem,
    keys_ref, values_ref, context_ref, scores_ref, weight_ref,
):
    fetch = _Fetch(
        q_hbm.at[pl.ds(BLOCK, BLOCK)], o_hbm, l_hbm, m_hbm, wkv_hbm, wo_hbm,
        (q_ref, o_ref, l_ref, m_ref, wkv_ref, wo_ref), sem,
    )

    def project(p):
        fetch.wait(("w", 0, p), ("w", D, p))
        both = [_dot(rows_ref[...], wkv_ref[:, _tile(p, base)]) for base in (0, D)]
        for full, ref in zip(both, (keys_ref, values_ref)):
            ref[p % 2] = full.astype(jnp.bfloat16)

    project(0)
    fetch.wait("q")
    for p in range(STEPS):
        at = _tile(p)
        if p + 1 < STEPS:
            project(p + 1)
        if p == 0:
            fetch.wait("o", "l", "m")
        far = _stage(
            q_ref[:, at], keys_ref.at[p % 2], values_ref.at[p % 2], scores_ref.at[p % 2],
            weight_ref.at[p % 2], bias_ref[3:4, 2 * BLOCK :],
        )
        out, total, _ = _join((o_ref[:, at], l_ref[:, at], m_ref[:, at]), far)
        context_ref[:, at] = (out / total).astype(jnp.bfloat16)
    fetch.wait("wo")
    projected = _dot(context_ref[...], wo_ref[...])
    out_ref[...] = _finish(projected, acc, gain_ref, rank_ref[0] * 2 + 1 < len_ref[0])


def _late(rows, wide, *widths):
    scratch = [
        VM((LT, BLOCK, 128), jnp.float32),
        VM((rows, D), jnp.bfloat16),
        *[VM((rows, D), jnp.float32)] * 3,
        VM((D, 2 * D), jnp.bfloat16),
        VM((D, D), jnp.bfloat16),
        pltpu.SemaphoreType.DMA((2 * STEPS + 5,)),
        VM((2, wide, TILE), jnp.bfloat16),
        VM((2, wide, TILE), jnp.bfloat16),
        VM((BLOCK, D), jnp.bfloat16),
    ]
    for width in widths:
        scratch += [VM((2, 4 * BLOCK, width), jnp.float32), VM((2, 4 * BLOCK, width), jnp.bfloat16)]
    return dict(grid=(1,), scratch_shapes=scratch)


LATE_SPECS = [
    *[pl.BlockSpec(memory_space=SM)] * 2,
    *[pl.BlockSpec(memory_space=VM)] * 2,
    *[pl.BlockSpec(memory_space=pl.ANY)] * 6,
    pl.BlockSpec(memory_space=VM),
]


def first(rank, length, rows, bias, q, o, l, m, w_kv, w_out, gain):
    f32 = jax.ShapeDtypeStruct((BLOCK, D), jnp.float32)
    rows = pltpu.with_memory_space_constraint(rows, VM)
    return pl.pallas_call(
        _first_kernel,
        out_shape=(jax.ShapeDtypeStruct((64, D), jnp.bfloat16), f32, f32, f32),
        in_specs=LATE_SPECS,
        out_specs=(pl.BlockSpec((32, D), lambda p: (0, 0)),) + (_whole((BLOCK, D)),) * 3,
        name="first",
        **_late(ROWS, SUBS_A * BLOCK, 4 * BLOCK, 2 * BLOCK),
    )(rank, length, rows, bias, q, o, l, m, w_kv, w_out, gain)


def second(rank, length, rows, bias, q, o, l, m, w_kv, w_out, gain, prev):
    rows = pltpu.with_memory_space_constraint(rows, VM)
    return pl.pallas_call(
        _second_kernel,
        out_shape=jax.ShapeDtypeStruct((64, D), jnp.bfloat16),
        in_specs=LATE_SPECS + [pl.BlockSpec(memory_space=pl.ANY)],
        out_specs=pl.BlockSpec((32, D), lambda p: (1, 0)),
        input_output_aliases={11: 0},
        name="second",
        **_late(BLOCK, SUBS_B * BLOCK, SUBS_B * BLOCK),
    )(rank, length, rows, bias, q, o, l, m, w_kv, w_out, gain, prev)


def exchange(value):
    return lax.all_to_all(value, "tm", split_axis=0, concat_axis=0, tiled=True)


def program(frames, w_query, w_kv, w_out, norm_gain, rand_owner, rand_slot, global_pos, length):
    shards = lax.axis_size("tm")
    rank = lax.axis_index("tm").astype(jnp.int32).reshape(1)
    gpos = global_pos.reshape(1, BLOCK)
    gain = norm_gain.reshape(1, D)
    up = [(i, i + 1) for i in range(shards - 1)]
    down = [(j, i) for i, j in up]
    packed = pack(rank, rand_owner, rand_slot, frames, gpos)
    held = exchange(packed)
    q, k, v, bias, gain = own_part(
        rank, length, rand_owner, rand_slot, gpos, frames, gain, w_query, w_kv
    )
    lo = lax.ppermute(frames[BLOCK:], "tm", up)
    hi = lax.ppermute(frames[:BLOCK], "tm", down)
    send_a, send_b = select(held)
    got_a = exchange(send_a).reshape(SUBS_A * BLOCK, D)
    got_b = exchange(send_b).reshape(SUBS_B * BLOCK, D)
    o, l, m = halo_part(lo, hi, bias, q, k, v, w_kv)
    half, o1, l1, m1 = first(rank, length, got_a, bias, q, o, l, m, w_kv, w_out, gain)
    return second(rank, length, got_b, bias, q, o1, l1, m1, w_kv, w_out, gain, half)


def solution(mesh):
    placed = (
        P(("rec", "tm"), None),
        P(),
        P(),
        P(),
        P(),
        P(("rec", "tm"), None),
        P(("rec", "tm"), None),
        P("rec"),
        P("rec"),
    )
    return jax.shard_map(
        program, mesh=mesh, in_specs=placed, out_specs=P(("rec", "tm"), None), check_vma=False
    )
```

```python
import jax
import jax.numpy as jnp
from jax import lax
from jax.experimental import pallas as pl
from jax.experimental.pallas import tpu as pltpu
from jax.sharding import PartitionSpec as P


BLOCK = 128
POOL = 4
PICKS = 3
D = 1280
HD = 64
TILE = 256
STEPS = D // TILE
SHARDS = 16
SUB = BLOCK // SHARDS
ROWS = 256
SUBS = 2 * PICKS + 1
LT = D // 128
NEG = -1e30

VM = pltpu.VMEM
SM = pltpu.SMEM


def _pack_kernel(rank_ref, owner_ref, slot_ref, gpos_ref, frames_hbm, out_hbm, frames_ref, more_ref, sem):
    load = pltpu.make_async_copy(frames_hbm, frames_ref, sem.at[0])
    load.start()
    copies = []
    for blk in range(2):
        for c in range(LT):
            src = frames_hbm.at[blk, :, :, c * 128 : (c + 1) * 128]
            k = blk * LT + c
            copies.append(pltpu.make_async_copy(src, out_hbm.at[:, k], sem.at[1 + k]))
            copies[-1].start()
    local = (gpos_ref[...] - rank_ref[0] * ROWS).astype(jnp.float32)
    local = jnp.broadcast_to(local, (8, BLOCK)).T[:, :1]
    cols = lax.broadcasted_iota(jnp.int32, (BLOCK, ROWS), 1).astype(jnp.float32)
    onehot = jnp.where(cols == local, 1.0, 0.0).astype(jnp.bfloat16)
    lane = lax.broadcasted_iota(jnp.int32, (SUB, 128), 1)
    codes = jnp.zeros((SUB, 128), jnp.int32)
    for q in range(2):
        for j in range(PICKS):
            code = (slot_ref[q, j] * SHARDS + owner_ref[q, j]) * SUB
            codes = jnp.where(lane == q * PICKS + j, code, codes)
    codes = codes + lax.broadcasted_iota(jnp.int32, (SUB, 128), 0)
    codes = codes.astype(jnp.float32).astype(jnp.bfloat16)
    for s in range(SHARDS):
        more_ref[s, LT] = codes
    load.wait()
    frames = frames_ref[...].astype(jnp.float32).reshape(ROWS, D).astype(jnp.bfloat16)
    picked = jnp.dot(onehot, frames, preferred_element_type=jnp.float32)
    for c in range(LT):
        piece = picked[:, c * 128 : (c + 1) * 128].reshape(SHARDS, SUB, 128)
        more_ref[:, c] = piece.astype(jnp.bfloat16)
    last = pltpu.make_async_copy(more_ref, out_hbm.at[:, 2 * LT : 3 * LT + 1], sem.at[1 + 2 * LT])
    last.start()
    for copy in copies:
        copy.wait()
    last.wait()


def pack(rank, owner, slot, frames, gpos):
    return pl.pallas_call(
        _pack_kernel,
        out_shape=jax.ShapeDtypeStruct((SHARDS, 3 * LT + 1, SUB, 128), jnp.bfloat16),
        in_specs=[pl.BlockSpec(memory_space=SM)] * 3
        + [pl.BlockSpec(memory_space=VM), pl.BlockSpec(memory_space=pl.ANY)],
        out_specs=pl.BlockSpec(memory_space=pl.ANY),
        scratch_shapes=[
            VM((2, SHARDS, SUB, D), jnp.bfloat16),
            VM((SHARDS, LT + 1, SUB, 128), jnp.bfloat16),
            pltpu.SemaphoreType.DMA((2 * LT + 2,)),
        ],
        name="pack",
    )(rank, owner, slot, gpos, frames.reshape(2, SHARDS, SUB, D))


def _select_kernel(held_ref, out_ref, buf, sem):
    copies = []

    def send(k, dest):
        copy = pltpu.make_async_copy(buf.at[k], dest, sem.at[k])
        copy.start()
        copies.append(copy)

    codes = held_ref[:, 3 * LT].astype(jnp.float32).reshape(BLOCK, 128)
    blocks = []
    for slot in range(2):
        tiles = [
            held_ref[:, slot * LT + c].astype(jnp.float32).reshape(BLOCK, 128).astype(jnp.bfloat16)
            for c in range(LT)
        ]
        blocks.append(jnp.concatenate(tiles, axis=1))
    rows = jnp.concatenate(blocks, axis=0)
    cols = lax.broadcasted_iota(jnp.int32, (BLOCK, ROWS), 1).astype(jnp.float32)
    for c in range(LT):
        total = held_ref[0, 2 * LT + c].astype(jnp.float32)
        for i in range(1, SHARDS):
            total = total + held_ref[i, 2 * LT + c].astype(jnp.float32)
        total = total.astype(jnp.bfloat16)
        for r in range(SHARDS):
            buf[2 * PICKS, r, :, c * 128 : (c + 1) * 128] = total
    send(2 * PICKS, out_ref.at[:, 2 * PICKS])
    for k in range(2 * PICKS):
        onehot = jnp.where(cols == codes[:, k : k + 1], 1.0, 0.0).astype(jnp.bfloat16)
        got = jnp.dot(onehot, rows, preferred_element_type=jnp.float32)
        buf[k] = got.reshape(SHARDS, SUB, D).astype(jnp.bfloat16)
        send(k, out_ref.at[:, k])
    for copy in copies:
        copy.wait()


def select(held):
    return pl.pallas_call(
        _select_kernel,
        out_shape=jax.ShapeDtypeStruct((SHARDS, SUBS, SUB, D), jnp.bfloat16),
        in_specs=[pl.BlockSpec(memory_space=VM)],
        out_specs=pl.BlockSpec(memory_space=pl.ANY),
        scratch_shapes=[
            pltpu.VMEM((2 * PICKS + 1, SHARDS, SUB, D), jnp.bfloat16),
            pltpu.SemaphoreType.DMA((2 * PICKS + 1,)),
        ],
        name="select",
    )(pltpu.with_memory_space_constraint(held, VM))


def _dot(a, b):
    return jnp.dot(a, b, preferred_element_type=jnp.float32)


def _scores(query, keys):
    lanes = lax.broadcasted_iota(jnp.int32, (BLOCK, TILE), 1) // HD
    zero = jnp.zeros_like(query)
    stacked = jnp.concatenate([jnp.where(lanes == i, query, zero) for i in range(4)], axis=0)
    return lax.dot_general(
        stacked, keys, (((1,), (1,)), ((), ())), preferred_element_type=jnp.float32
    )


def _weigh(scores, values, bias):
    scores = scores + bias
    top = jnp.max(scores, axis=1, keepdims=True)
    weight = jnp.exp(scores - top).astype(jnp.bfloat16)
    ones = jnp.ones((values.shape[0], 128), jnp.bfloat16)
    low = lax.broadcasted_iota(jnp.int32, (BLOCK, 128), 1) < HD
    outs, sums, tops = [], [], []
    for pair in range(2):
        ext = jnp.concatenate([values[:, pair * 128 : (pair + 1) * 128], ones], axis=1)
        res = _dot(weight[pair * 256 : (pair + 1) * 256], ext)
        outs.append(jnp.where(low, res[:BLOCK, :128], res[BLOCK:, :128]))
        sums.append(jnp.where(low, res[:BLOCK, 128:], res[BLOCK:, 128:]))
        tops.append(
            jnp.where(
                low,
                top[pair * 256 : pair * 256 + BLOCK],
                top[pair * 256 + BLOCK : (pair + 1) * 256],
            )
        )
    return tuple(jnp.concatenate(x, axis=1) for x in (outs, sums, tops))


def _attend(query, keys, values, bias):
    return _weigh(_scores(query, keys), values, bias)


def _join(near, far):
    both = jnp.maximum(near[2], far[2])
    a = jnp.exp(near[2] - both)
    b = jnp.exp(far[2] - both)
    return a * near[0] + b * far[0], a * near[1] + b * far[1], both


def _own_kernel(
    rank_ref, len_ref, owner_ref, slot_ref, gpos_ref, own_ref, wq_ref, wk_ref, wv_ref,
    q_ref, k_ref, v_ref, bias_ref,
):
    own = own_ref[...]
    q_ref[...] = _dot(own, wq_ref[...]).astype(jnp.bfloat16) * jnp.bfloat16(0.125)
    k_ref[...] = _dot(own, wk_ref[...]).astype(jnp.bfloat16)
    v_ref[...] = _dot(own, wv_ref[...]).astype(jnp.bfloat16)

    @pl.when(pl.program_id(0) == 0)
    def _():
        live = len_ref[0]
        lane = lax.broadcasted_iota(jnp.int32, (1, 4 * BLOCK), 1)

        def row(parts):
            dead = lane < 0
            for at, block in parts:
                dead = dead | (at & ((block < 0) | (block >= live)))
            return jnp.where(dead, NEG, 0.0)

        def picked(q, j):
            return owner_ref[q, j] * 2 + slot_ref[q, j]

        for q in range(2):
            near = [(lane // BLOCK == i, rank_ref[0] * 2 + q - 1 + i) for i in range(3)]
            bias_ref[q : q + 1, :] = row(near)
        glob = jnp.where(gpos_ref[...] < live * BLOCK, 0.0, NEG)
        rows = lane // SUB
        for q in range(2):
            far = row([((rows % PICKS == j), picked(q, j)) for j in range(PICKS)])
            parts = [far[:, : PICKS * BLOCK], glob]
            bias_ref[2 + q : 3 + q, :] = jnp.concatenate(parts if q == 0 else parts[::-1], axis=1)
        bias_ref[4:8, :] = jnp.zeros((4, 4 * BLOCK), jnp.float32)


def _halo_kernel(lo_ref, hi_ref, bias_ref, q_ref, k_ref, v_ref, wk_ref, wv_ref, o_ref, l_ref, m_ref):
    rim = jnp.concatenate([lo_ref[...], hi_ref[...]], axis=0)

    def widen(own_ref, w_ref):
        far = _dot(rim, w_ref[...]).astype(jnp.bfloat16)
        return jnp.concatenate([far[:BLOCK], own_ref[...], far[BLOCK:]], axis=0)

    keys = widen(k_ref, wk_ref)
    values = widen(v_ref, wv_ref)
    for b in range(2):
        at = slice(b * BLOCK, b * BLOCK + 3 * BLOCK)
        res = _attend(
            q_ref[b * BLOCK : (b + 1) * BLOCK], keys[at], values[at], bias_ref[b : b + 1, : 3 * BLOCK]
        )
        for ref, val in zip((o_ref, l_ref, m_ref), res):
            ref[b * BLOCK : (b + 1) * BLOCK, :] = val


def _whole(shape):
    return pl.BlockSpec(shape, lambda p: (0,) * len(shape))


def _cols(rows, shift=0):
    return pl.BlockSpec((rows, TILE), lambda p: (0, p + shift))


def own_part(rank, length, owner, slot, gpos, own, w_query, w_kv):
    half = jax.ShapeDtypeStruct((ROWS, D), jnp.bfloat16)
    return pl.pallas_call(
        _own_kernel,
        grid=(STEPS,),
        out_shape=(half, half, half, jax.ShapeDtypeStruct((8, 4 * BLOCK), jnp.float32)),
        in_specs=[pl.BlockSpec(memory_space=SM)] * 4
        + [_whole((1, BLOCK)), _whole((ROWS, D)), _cols(D), _cols(D), _cols(D, STEPS)],
        out_specs=(_cols(ROWS),) * 3 + (_whole((8, 4 * BLOCK)),),
        name="own",
    )(rank, length, owner, slot, gpos, own, w_query, w_kv, w_kv)


def halo_part(lo, hi, bias, q, k, v, w_kv):
    f32 = jax.ShapeDtypeStruct((ROWS, D), jnp.float32)
    lo = pltpu.with_memory_space_constraint(lo, VM)
    hi = pltpu.with_memory_space_constraint(hi, VM)
    return pl.pallas_call(
        _halo_kernel,
        grid=(STEPS,),
        out_shape=(f32, f32, f32),
        in_specs=[
            pl.BlockSpec(memory_space=VM),
            pl.BlockSpec(memory_space=VM),
            _whole((8, 4 * BLOCK)),
            *[_cols(ROWS)] * 3,
            _cols(D),
            _cols(D, STEPS),
        ],
        out_specs=(_cols(ROWS),) * 3,
        name="halo",
    )(lo, hi, bias, q, k, v, w_kv, w_kv)


def _finish(projected, acc, gain_ref, live):
    tiles = []
    for c in range(LT):
        acc[c] = projected[:, c * 128 : (c + 1) * 128]
    for c in range(LT):
        total = acc[c, pl.ds(0, 32, stride=POOL), :]
        for i in range(1, POOL):
            total = total + acc[c, pl.ds(i, 32, stride=POOL), :]
        tiles.append(total)
    pooled = jnp.concatenate(tiles, axis=1) * (1.0 / POOL)
    mean = jnp.mean(pooled, axis=1, keepdims=True)
    centered = pooled - mean
    var = jnp.mean(centered * centered, axis=1, keepdims=True)
    normed = centered * lax.rsqrt(var + 1e-05) * gain_ref[...]
    return jnp.where(live, normed, 0.0).astype(jnp.bfloat16)


def _tile(p, base=0):
    return slice(base + p * TILE, base + (p + 1) * TILE)


def _stage(query, keys_ref, values_ref, scores_ref, weight_ref, bias):
    width = keys_ref.shape[0]
    scores_ref[:, :width] = _scores(query, keys_ref[...])
    tops = []
    for r in range(0, 4 * BLOCK, 64):
        piece = scores_ref[r : r + 64, :width] + bias
        top = jnp.max(piece, axis=1, keepdims=True)
        weight_ref[r : r + 64, :width] = jnp.exp(piece - top).astype(jnp.bfloat16)
        tops.append(top)
    top = jnp.concatenate(tops, axis=0)
    ones = jnp.ones((width, 128), jnp.bfloat16)
    low = lax.broadcasted_iota(jnp.int32, (BLOCK, 128), 1) < HD
    outs, sums, maxes = [], [], []
    for pair in range(2):
        base = pair * 256
        ext = jnp.concatenate([values_ref[:, pair * 128 : (pair + 1) * 128], ones], axis=1)
        res = _dot(weight_ref[base : base + 256, :width], ext)
        outs.append(jnp.where(low, res[:BLOCK, :128], res[BLOCK:, :128]))
        sums.append(jnp.where(low, res[:BLOCK, 128:], res[BLOCK:, 128:]))
        maxes.append(jnp.where(low, top[base : base + BLOCK], top[base + BLOCK : base + 256]))
    return tuple(jnp.concatenate(x, axis=1) for x in (outs, sums, maxes))


class _Fetch:
    def __init__(self, q_ref, o_ref, l_ref, m_ref, wkv_ref, wo_ref, bufs, sem):
        q, o, l, m, wkv, wo = bufs
        self.copies = {}
        count = 0

        def start(key, src, dst):
            nonlocal count
            copy = pltpu.make_async_copy(src, dst, sem.at[count])
            copy.start()
            self.copies[key] = copy
            count += 1

        def weights(p, base):
            at = _tile(p, base)
            start(("w", base, p), wkv_ref.at[:, at], wkv.at[:, at])

        weights(0, 0)
        start("q", q_ref, q)
        weights(0, D)
        weights(1, 0)
        for key, src, dst in (("o", o_ref, o), ("l", l_ref, l), ("m", m_ref, m)):
            start(key, src, dst)
        for p in range(1, STEPS):
            weights(p, D)
            if p + 1 < STEPS:
                weights(p + 1, 0)
        start("wo", wo_ref, wo)

    def wait(self, *keys):
        for key in keys:
            self.copies.pop(key).wait()


def _late_kernel(
    rank_ref, len_ref, rows_ref, bias_ref, q_hbm, o_hbm, l_hbm, m_hbm, wkv_hbm, wo_hbm, gain_ref,
    out_ref, acc, q_ref, o_ref, l_ref, m_ref, wkv_ref, wo_ref, sem,
    keys_ref, values_ref, scores_ref, weight_ref, context_ref,
):
    fetch = _Fetch(
        q_hbm, o_hbm, l_hbm, m_hbm, wkv_hbm, wo_hbm, (q_ref, o_ref, l_ref, m_ref, wkv_ref, wo_ref), sem
    )
    near = PICKS * BLOCK

    def project(p):
        fetch.wait(("w", 0, p), ("w", D, p))
        both = [_dot(rows_ref[...], wkv_ref[:, _tile(p, base)]) for base in (0, D)]
        for full, ref in zip(both, (keys_ref, values_ref)):
            full = full.reshape(SHARDS, SUBS, SUB, TILE)
            ref[p % 2, :near] = full[:, :PICKS].reshape(near, TILE).astype(jnp.bfloat16)
            ref[p % 2, near : near + BLOCK] = full[:, 2 * PICKS].reshape(BLOCK, TILE).astype(jnp.bfloat16)
            ref[p % 2, near + BLOCK :] = full[:, PICKS : 2 * PICKS].reshape(near, TILE).astype(jnp.bfloat16)

    project(0)
    fetch.wait("q")
    for p in range(STEPS):
        at = _tile(p)
        if p + 1 < STEPS:
            project(p + 1)
        if p == 0:
            fetch.wait("o", "l", "m")
        for b in range(2):
            rows = slice(b * BLOCK, (b + 1) * BLOCK)
            used = pl.ds(b * near, near + BLOCK)
            far = _stage(
                q_ref[rows, at], keys_ref.at[p % 2, used], values_ref.at[p % 2, used],
                scores_ref.at[b], weight_ref.at[b], bias_ref[2 + b : 3 + b, :],
            )
            out, total, _ = _join((o_ref[rows, at], l_ref[rows, at], m_ref[rows, at]), far)
            context_ref[rows, at] = (out / total).astype(jnp.bfloat16)
    fetch.wait("wo")
    projected = _dot(context_ref[...], wo_ref[...])
    for b in range(2):
        live = rank_ref[0] * 2 + b < len_ref[0]
        part = projected[b * BLOCK : (b + 1) * BLOCK]
        out_ref[b * 32 : (b + 1) * 32, :] = _finish(part, acc.at[b], gain_ref, live)


def late(rank, length, rows, bias, q, o, l, m, w_kv, w_out, gain):
    rows = pltpu.with_memory_space_constraint(rows, VM)
    return pl.pallas_call(
        _late_kernel,
        out_shape=jax.ShapeDtypeStruct((64, D), jnp.bfloat16),
        in_specs=[
            *[pl.BlockSpec(memory_space=SM)] * 2,
            *[pl.BlockSpec(memory_space=VM)] * 2,
            *[pl.BlockSpec(memory_space=pl.ANY)] * 6,
            pl.BlockSpec(memory_space=VM),
        ],
        out_specs=pl.BlockSpec(memory_space=VM),
        scratch_shapes=[
            VM((2, LT, BLOCK, 128), jnp.float32),
            VM((ROWS, D), jnp.bfloat16),
            *[VM((ROWS, D), jnp.float32)] * 3,
            VM((D, 2 * D), jnp.bfloat16),
            VM((D, D), jnp.bfloat16),
            pltpu.SemaphoreType.DMA((2 * STEPS + 5,)),
            VM((2, SUBS * BLOCK, TILE), jnp.bfloat16),
            VM((2, SUBS * BLOCK, TILE), jnp.bfloat16),
            VM((2, 4 * BLOCK, 4 * BLOCK), jnp.float32),
            VM((2, 4 * BLOCK, 4 * BLOCK), jnp.bfloat16),
            VM((ROWS, D), jnp.bfloat16),
        ],
        name="late",
    )(rank, length, rows, bias, q, o, l, m, w_kv, w_out, gain)


def exchange(value):
    return lax.all_to_all(value, "tm", split_axis=0, concat_axis=0, tiled=True)


def program(frames, w_query, w_kv, w_out, norm_gain, rand_owner, rand_slot, global_pos, length):
    shards = lax.axis_size("tm")
    rank = lax.axis_index("tm").astype(jnp.int32).reshape(1)
    gpos = global_pos.reshape(1, BLOCK)
    gain = norm_gain.reshape(1, D)
    up = [(i, i + 1) for i in range(shards - 1)]
    down = [(j, i) for i, j in up]
    packed = pack(rank, rand_owner, rand_slot, frames, gpos)
    held = exchange(packed)
    q, k, v, bias = own_part(rank, length, rand_owner, rand_slot, gpos, frames, w_query, w_kv)
    lo = lax.ppermute(frames[BLOCK:], "tm", up)
    hi = lax.ppermute(frames[:BLOCK], "tm", down)
    reply = select(held)
    got = exchange(reply).reshape(SUBS * BLOCK, D)
    o, l, m = halo_part(lo, hi, bias, q, k, v, w_kv)
    return late(rank, length, got, bias, q, o, l, m, w_kv, w_out, gain)


def solution(mesh):
    placed = (
        P(("rec", "tm"), None),
        P(),
        P(),
        P(),
        P(),
        P(("rec", "tm"), None),
        P(("rec", "tm"), None),
        P("rec"),
        P("rec"),
    )
    return jax.shard_map(
        program, mesh=mesh, in_specs=placed, out_specs=P(("rec", "tm"), None), check_vma=False
    )
```

```python
import jax
import jax.numpy as jnp
from jax import lax
from jax.experimental import pallas as pl
from jax.experimental.pallas import tpu as pltpu
from jax.sharding import PartitionSpec as P


BLOCK = 128
POOL = 4
PICKS = 3
D = 1280
HD = 64
TILE = 256
STEPS = D // TILE
SHARDS = 16
SUB = BLOCK // SHARDS
ROWS = 256
SUBS = 2 * PICKS
LT = D // 128
NEG = -1e30

VM = pltpu.VMEM
SM = pltpu.SMEM


def _pack_kernel(rank_ref, owner_ref, slot_ref, frames_ref, gpos_ref, out_ref, picked_ref):
    frames = frames_ref[...]
    for blk in range(2):
        for c in range(LT):
            piece = frames_ref[blk * BLOCK : (blk + 1) * BLOCK, c * 128 : (c + 1) * 128]
            out_ref[:, blk * LT + c] = piece.reshape(SHARDS, SUB, 128)
    local = (gpos_ref[...] - rank_ref[0] * ROWS).astype(jnp.float32)
    local = jnp.broadcast_to(local, (8, BLOCK)).T[:, :1]
    cols = lax.broadcasted_iota(jnp.int32, (BLOCK, ROWS), 1).astype(jnp.float32)
    onehot = jnp.where(cols == local, 1.0, 0.0).astype(jnp.bfloat16)
    picked = jnp.dot(onehot, frames, preferred_element_type=jnp.float32)
    picked_ref[...] = picked.astype(jnp.bfloat16)
    lane = lax.broadcasted_iota(jnp.int32, (SUB, 128), 1)
    codes = jnp.zeros((SUB, 128), jnp.int32)
    for q in range(2):
        for j in range(PICKS):
            code = (slot_ref[q, j] * SHARDS + owner_ref[q, j]) * SUB
            codes = jnp.where(lane == q * PICKS + j, code, codes)
    codes = codes + lax.broadcasted_iota(jnp.int32, (SUB, 128), 0)
    codes = codes.astype(jnp.float32).astype(jnp.bfloat16)
    for s in range(SHARDS):
        out_ref[s, 2 * LT] = codes


def pack(rank, owner, slot, frames, gpos):
    return pl.pallas_call(
        _pack_kernel,
        out_shape=(
            jax.ShapeDtypeStruct((SHARDS, 2 * LT + 1, SUB, 128), jnp.bfloat16),
            jax.ShapeDtypeStruct((BLOCK, D), jnp.bfloat16),
        ),
        in_specs=[pl.BlockSpec(memory_space=SM)] * 3 + [pl.BlockSpec(memory_space=VM)] * 2,
        out_specs=(pl.BlockSpec(memory_space=VM),) * 2,
        name="pack",
    )(rank, owner, slot, frames, gpos)


def _select_kernel(held_ref, out_ref, buf, sem):
    copies = []

    def send(k, dest):
        copy = pltpu.make_async_copy(buf.at[k], dest, sem.at[k])
        copy.start()
        copies.append(copy)

    codes = held_ref[:, 2 * LT].astype(jnp.float32).reshape(BLOCK, 128)
    blocks = []
    for slot in range(2):
        tiles = [
            held_ref[:, slot * LT + c].astype(jnp.float32).reshape(BLOCK, 128).astype(jnp.bfloat16)
            for c in range(LT)
        ]
        blocks.append(jnp.concatenate(tiles, axis=1))
    rows = jnp.concatenate(blocks, axis=0)
    cols = lax.broadcasted_iota(jnp.int32, (BLOCK, ROWS), 1).astype(jnp.float32)
    for k in range(2 * PICKS):
        onehot = jnp.where(cols == codes[:, k : k + 1], 1.0, 0.0).astype(jnp.bfloat16)
        got = jnp.dot(onehot, rows, preferred_element_type=jnp.float32)
        buf[k] = got.reshape(SHARDS, SUB, D).astype(jnp.bfloat16)
        send(k, out_ref.at[:, k])
    for copy in copies:
        copy.wait()


def select(held):
    return pl.pallas_call(
        _select_kernel,
        out_shape=jax.ShapeDtypeStruct((SHARDS, SUBS, SUB, D), jnp.bfloat16),
        in_specs=[pl.BlockSpec(memory_space=VM)],
        out_specs=pl.BlockSpec(memory_space=pl.ANY),
        scratch_shapes=[
            pltpu.VMEM((2 * PICKS + 1, SHARDS, SUB, D), jnp.bfloat16),
            pltpu.SemaphoreType.DMA((SUBS,)),
        ],
        name="select",
    )(pltpu.with_memory_space_constraint(held, VM))


def _dot(a, b):
    return jnp.dot(a, b, preferred_element_type=jnp.float32)


def _scores(query, keys):
    lanes = lax.broadcasted_iota(jnp.int32, (BLOCK, TILE), 1) // HD
    zero = jnp.zeros_like(query)
    stacked = jnp.concatenate([jnp.where(lanes == i, query, zero) for i in range(4)], axis=0)
    return lax.dot_general(
        stacked, keys, (((1,), (1,)), ((), ())), preferred_element_type=jnp.float32
    )


def _weigh(scores, values, bias):
    scores = scores + bias
    top = jnp.max(scores, axis=1, keepdims=True)
    weight = jnp.exp(scores - top).astype(jnp.bfloat16)
    ones = jnp.ones((values.shape[0], 128), jnp.bfloat16)
    low = lax.broadcasted_iota(jnp.int32, (BLOCK, 128), 1) < HD
    outs, sums, tops = [], [], []
    for pair in range(2):
        ext = jnp.concatenate([values[:, pair * 128 : (pair + 1) * 128], ones], axis=1)
        res = _dot(weight[pair * 256 : (pair + 1) * 256], ext)
        outs.append(jnp.where(low, res[:BLOCK, :128], res[BLOCK:, :128]))
        sums.append(jnp.where(low, res[:BLOCK, 128:], res[BLOCK:, 128:]))
        tops.append(
            jnp.where(
                low,
                top[pair * 256 : pair * 256 + BLOCK],
                top[pair * 256 + BLOCK : (pair + 1) * 256],
            )
        )
    return tuple(jnp.concatenate(x, axis=1) for x in (outs, sums, tops))


def _attend(query, keys, values, bias):
    return _weigh(_scores(query, keys), values, bias)


def _join(near, far):
    both = jnp.maximum(near[2], far[2])
    a = jnp.exp(near[2] - both)
    b = jnp.exp(far[2] - both)
    return a * near[0] + b * far[0], a * near[1] + b * far[1], both


def _own_kernel(
    rank_ref, len_ref, owner_ref, slot_ref, gpos_ref, own_ref, wq_ref, wk_ref, wv_ref,
    q_ref, k_ref, v_ref, bias_ref,
):
    own = own_ref[...]
    q_ref[...] = _dot(own, wq_ref[...]).astype(jnp.bfloat16) * jnp.bfloat16(0.125)
    k_ref[...] = _dot(own, wk_ref[...]).astype(jnp.bfloat16)
    v_ref[...] = _dot(own, wv_ref[...]).astype(jnp.bfloat16)

    @pl.when(pl.program_id(0) == 0)
    def _():
        live = len_ref[0]
        lane = lax.broadcasted_iota(jnp.int32, (1, 4 * BLOCK), 1)

        def row(parts):
            dead = lane < 0
            for at, block in parts:
                dead = dead | (at & ((block < 0) | (block >= live)))
            return jnp.where(dead, NEG, 0.0)

        def picked(q, j):
            return owner_ref[q, j] * 2 + slot_ref[q, j]

        glob = jnp.where(gpos_ref[...] < live * BLOCK, 0.0, NEG)
        rows = lane // SUB
        for q in range(2):
            near = row([(lane // BLOCK == i, rank_ref[0] * 2 + q - 1 + i) for i in range(3)])
            bias_ref[q : q + 1, :] = jnp.concatenate([near[:, : 3 * BLOCK], glob], axis=1)
            far = row([(rows % PICKS == j, picked(q, j)) for j in range(PICKS)])
            bias_ref[2 + q : 3 + q, :] = far
        bias_ref[4:8, :] = jnp.zeros((4, 4 * BLOCK), jnp.float32)


def _halo_kernel(
    lo_ref, hi_ref, glob_ref, bias_ref, q_ref, k_ref, v_ref, wk_ref, wv_ref, o_ref, l_ref, m_ref
):
    rim = jnp.concatenate([lo_ref[...], hi_ref[...], glob_ref[...]], axis=0)

    def widen(own_ref, w_ref):
        far = _dot(rim, w_ref[...]).astype(jnp.bfloat16)
        lo, hi, glob = (far[i * BLOCK : (i + 1) * BLOCK] for i in range(3))
        own = own_ref[...]
        return [jnp.concatenate([lo, own, glob], axis=0), jnp.concatenate([own, hi, glob], axis=0)]

    keys = widen(k_ref, wk_ref)
    values = widen(v_ref, wv_ref)
    for b in range(2):
        res = _attend(
            q_ref[b * BLOCK : (b + 1) * BLOCK], keys[b], values[b], bias_ref[b : b + 1, :]
        )
        for ref, val in zip((o_ref, l_ref, m_ref), res):
            ref[b * BLOCK : (b + 1) * BLOCK, :] = val


def _whole(shape):
    return pl.BlockSpec(shape, lambda p: (0,) * len(shape))


def _cols(rows, shift=0):
    return pl.BlockSpec((rows, TILE), lambda p: (0, p + shift))


def own_part(rank, length, owner, slot, gpos, own, w_query, w_kv):
    half = jax.ShapeDtypeStruct((ROWS, D), jnp.bfloat16)
    return pl.pallas_call(
        _own_kernel,
        grid=(STEPS,),
        out_shape=(half, half, half, jax.ShapeDtypeStruct((8, 4 * BLOCK), jnp.float32)),
        in_specs=[pl.BlockSpec(memory_space=SM)] * 4
        + [_whole((1, BLOCK)), _whole((ROWS, D)), _cols(D), _cols(D), _cols(D, STEPS)],
        out_specs=(_cols(ROWS),) * 3 + (_whole((8, 4 * BLOCK)),),
        name="own",
    )(rank, length, owner, slot, gpos, own, w_query, w_kv, w_kv)


def halo_part(lo, hi, glob, bias, q, k, v, w_kv):
    f32 = jax.ShapeDtypeStruct((ROWS, D), jnp.float32)
    lo = pltpu.with_memory_space_constraint(lo, VM)
    hi = pltpu.with_memory_space_constraint(hi, VM)
    return pl.pallas_call(
        _halo_kernel,
        grid=(STEPS,),
        out_shape=(f32, f32, f32),
        in_specs=[
            pl.BlockSpec(memory_space=VM),
            pl.BlockSpec(memory_space=VM),
            _whole((BLOCK, D)),
            _whole((8, 4 * BLOCK)),
            *[_cols(ROWS)] * 3,
            _cols(D),
            _cols(D, STEPS),
        ],
        out_specs=(_cols(ROWS),) * 3,
        name="halo",
    )(lo, hi, glob, bias, q, k, v, w_kv, w_kv)


def _finish(projected, acc, gain_ref, live):
    tiles = []
    for c in range(LT):
        acc[c] = projected[:, c * 128 : (c + 1) * 128]
    for c in range(LT):
        total = acc[c, pl.ds(0, 32, stride=POOL), :]
        for i in range(1, POOL):
            total = total + acc[c, pl.ds(i, 32, stride=POOL), :]
        tiles.append(total)
    pooled = jnp.concatenate(tiles, axis=1) * (1.0 / POOL)
    mean = jnp.mean(pooled, axis=1, keepdims=True)
    centered = pooled - mean
    var = jnp.mean(centered * centered, axis=1, keepdims=True)
    normed = centered * lax.rsqrt(var + 1e-05) * gain_ref[...]
    return jnp.where(live, normed, 0.0).astype(jnp.bfloat16)


def _tile(p, base=0):
    return slice(base + p * TILE, base + (p + 1) * TILE)


def _stage(query, keys_ref, values_ref, scores_ref, weight_ref, bias):
    width = keys_ref.shape[0]
    scores_ref[:, :width] = _scores(query, keys_ref[...])
    tops = []
    for r in range(0, 4 * BLOCK, 64):
        piece = scores_ref[r : r + 64, :width] + bias
        top = jnp.max(piece, axis=1, keepdims=True)
        weight_ref[r : r + 64, :width] = jnp.exp(piece - top).astype(jnp.bfloat16)
        tops.append(top)
    top = jnp.concatenate(tops, axis=0)
    ones = jnp.ones((width, 128), jnp.bfloat16)
    low = lax.broadcasted_iota(jnp.int32, (BLOCK, 128), 1) < HD
    outs, sums, maxes = [], [], []
    for pair in range(2):
        base = pair * 256
        ext = jnp.concatenate([values_ref[:, pair * 128 : (pair + 1) * 128], ones], axis=1)
        res = _dot(weight_ref[base : base + 256, :width], ext)
        outs.append(jnp.where(low, res[:BLOCK, :128], res[BLOCK:, :128]))
        sums.append(jnp.where(low, res[:BLOCK, 128:], res[BLOCK:, 128:]))
        maxes.append(jnp.where(low, top[base : base + BLOCK], top[base + BLOCK : base + 256]))
    return tuple(jnp.concatenate(x, axis=1) for x in (outs, sums, maxes))


class _Fetch:
    def __init__(self, q_ref, o_ref, l_ref, m_ref, wkv_ref, wo_ref, bufs, sem):
        q, o, l, m, wkv, wo = bufs
        self.copies = {}
        count = 0

        def start(key, src, dst):
            nonlocal count
            copy = pltpu.make_async_copy(src, dst, sem.at[count])
            copy.start()
            self.copies[key] = copy
            count += 1

        def weights(p, base):
            at = _tile(p, base)
            start(("w", base, p), wkv_ref.at[:, at], wkv.at[:, at])

        weights(0, 0)
        start("q", q_ref, q)
        weights(0, D)
        weights(1, 0)
        for key, src, dst in (("o", o_ref, o), ("l", l_ref, l), ("m", m_ref, m)):
            start(key, src, dst)
        for p in range(1, STEPS):
            weights(p, D)
            if p + 1 < STEPS:
                weights(p + 1, 0)
        start("wo", wo_ref, wo)

    def wait(self, *keys):
        for key in keys:
            self.copies.pop(key).wait()


def _late_kernel(
    rank_ref, len_ref, rows_ref, bias_ref, q_hbm, o_hbm, l_hbm, m_hbm, wkv_hbm, wo_hbm, gain_ref,
    out_ref, acc, q_ref, o_ref, l_ref, m_ref, wkv_ref, wo_ref, sem,
    keys_ref, values_ref, scores_ref, weight_ref, context_ref,
):
    fetch = _Fetch(
        q_hbm, o_hbm, l_hbm, m_hbm, wkv_hbm, wo_hbm, (q_ref, o_ref, l_ref, m_ref, wkv_ref, wo_ref), sem
    )
    near = PICKS * BLOCK

    def project(p):
        fetch.wait(("w", 0, p), ("w", D, p))
        both = [_dot(rows_ref[...], wkv_ref[:, _tile(p, base)]) for base in (0, D)]
        for full, ref in zip(both, (keys_ref, values_ref)):
            full = full.reshape(SHARDS, SUBS, SUB, TILE)
            ref[p % 2, :near] = full[:, :PICKS].reshape(near, TILE).astype(jnp.bfloat16)
            ref[p % 2, near:] = full[:, PICKS:].reshape(near, TILE).astype(jnp.bfloat16)

    project(0)
    fetch.wait("q")
    for p in range(STEPS):
        at = _tile(p)
        if p + 1 < STEPS:
            project(p + 1)
        if p == 0:
            fetch.wait("o", "l", "m")
        for b in range(2):
            rows = slice(b * BLOCK, (b + 1) * BLOCK)
            used = pl.ds(b * near, near)
            far = _stage(
                q_ref[rows, at], keys_ref.at[p % 2, used], values_ref.at[p % 2, used],
                scores_ref.at[b], weight_ref.at[b], bias_ref[2 + b : 3 + b, :near],
            )
            out, total, _ = _join((o_ref[rows, at], l_ref[rows, at], m_ref[rows, at]), far)
            context_ref[rows, at] = (out / total).astype(jnp.bfloat16)
    fetch.wait("wo")
    projected = _dot(context_ref[...], wo_ref[...])
    for b in range(2):
        live = rank_ref[0] * 2 + b < len_ref[0]
        part = projected[b * BLOCK : (b + 1) * BLOCK]
        out_ref[b * 32 : (b + 1) * 32, :] = _finish(part, acc.at[b], gain_ref, live)


def late(rank, length, rows, bias, q, o, l, m, w_kv, w_out, gain):
    rows = pltpu.with_memory_space_constraint(rows, VM)
    return pl.pallas_call(
        _late_kernel,
        out_shape=jax.ShapeDtypeStruct((64, D), jnp.bfloat16),
        in_specs=[
            *[pl.BlockSpec(memory_space=SM)] * 2,
            *[pl.BlockSpec(memory_space=VM)] * 2,
            *[pl.BlockSpec(memory_space=pl.ANY)] * 6,
            pl.BlockSpec(memory_space=VM),
        ],
        out_specs=pl.BlockSpec(memory_space=VM),
        scratch_shapes=[
            VM((2, LT, BLOCK, 128), jnp.float32),
            VM((ROWS, D), jnp.bfloat16),
            *[VM((ROWS, D), jnp.float32)] * 3,
            VM((D, 2 * D), jnp.bfloat16),
            VM((D, D), jnp.bfloat16),
            pltpu.SemaphoreType.DMA((2 * STEPS + 5,)),
            VM((2, SUBS * BLOCK, TILE), jnp.bfloat16),
            VM((2, SUBS * BLOCK, TILE), jnp.bfloat16),
            VM((2, 4 * BLOCK, PICKS * BLOCK), jnp.float32),
            VM((2, 4 * BLOCK, PICKS * BLOCK), jnp.bfloat16),
            VM((ROWS, D), jnp.bfloat16),
        ],
        name="late",
    )(rank, length, rows, bias, q, o, l, m, w_kv, w_out, gain)


def exchange(value):
    return lax.all_to_all(value, "tm", split_axis=0, concat_axis=0, tiled=True)


def program(frames, w_query, w_kv, w_out, norm_gain, rand_owner, rand_slot, global_pos, length):
    shards = lax.axis_size("tm")
    rank = lax.axis_index("tm").astype(jnp.int32).reshape(1)
    gpos = global_pos.reshape(1, BLOCK)
    gain = norm_gain.reshape(1, D)
    up = [(i, i + 1) for i in range(shards - 1)]
    down = [(j, i) for i, j in up]
    packed, glob = pack(rank, rand_owner, rand_slot, frames, gpos)
    held = exchange(packed)
    q, k, v, bias = own_part(rank, length, rand_owner, rand_slot, gpos, frames, w_query, w_kv)
    lo = lax.ppermute(frames[BLOCK:], "tm", up)
    hi = lax.ppermute(frames[:BLOCK], "tm", down)
    for k_step in range(4):
        other = lax.ppermute(glob, "tm", [(i, i ^ (1 << k_step)) for i in range(shards)])
        glob = glob + other
    reply = select(held)
    got = exchange(reply).reshape(SUBS * BLOCK, D)
    o, l, m = halo_part(lo, hi, glob, bias, q, k, v, w_kv)
    return late(rank, length, got, bias, q, o, l, m, w_kv, w_out, gain)


def solution(mesh):
    placed = (
        P(("rec", "tm"), None),
        P(),
        P(),
        P(),
        P(),
        P(("rec", "tm"), None),
        P(("rec", "tm"), None),
        P("rec"),
        P("rec"),
    )
    return jax.shard_map(
        program, mesh=mesh, in_specs=placed, out_specs=P(("rec", "tm"), None), check_vma=False
    )
```

```python
import jax
import jax.numpy as jnp
from jax import lax
from jax.experimental import pallas as pl
from jax.experimental.pallas import tpu as pltpu
from jax.sharding import PartitionSpec as P


BLOCK = 128
POOL = 4
PICKS = 3
D = 1280
HD = 64
TILE = 256
STEPS = D // TILE
SHARDS = 16
SUB = BLOCK // SHARDS
ROWS = 256
SUBS = 2 * PICKS + 1
LT = D // 128
NEG = -1e30

VM = pltpu.VMEM
SM = pltpu.SMEM


def _pack_kernel(rank_ref, owner_ref, slot_ref, gpos_ref, frames_hbm, out_hbm, frames_ref, buf, sem):
    loads, stores = [], []
    for blk in range(2):
        at = pl.ds(blk * BLOCK, BLOCK)
        loads.append(pltpu.make_async_copy(frames_hbm.at[at], frames_ref.at[at], sem.at[blk]))
        loads[-1].start()

    def send(k, start, count):
        at = pl.ds(start, count)
        stores.append(pltpu.make_async_copy(buf.at[:, at], out_hbm.at[:, at], sem.at[k]))
        stores[-1].start()

    lane = lax.broadcasted_iota(jnp.int32, (SUB, 128), 1)
    codes = jnp.zeros((SUB, 128), jnp.int32)
    for q in range(2):
        for j in range(PICKS):
            code = (slot_ref[q, j] * SHARDS + owner_ref[q, j]) * SUB
            codes = jnp.where(lane == q * PICKS + j, code, codes)
    codes = codes + lax.broadcasted_iota(jnp.int32, (SUB, 128), 0)
    codes = codes.astype(jnp.float32).astype(jnp.bfloat16)
    for s in range(SHARDS):
        buf[s, 3 * LT] = codes
    local = (gpos_ref[...] - rank_ref[0] * ROWS).astype(jnp.float32)
    local = jnp.broadcast_to(local, (8, BLOCK)).T[:, :1]
    cols = lax.broadcasted_iota(jnp.int32, (BLOCK, ROWS), 1).astype(jnp.float32)
    onehot = jnp.where(cols == local, 1.0, 0.0).astype(jnp.bfloat16)
    for blk in range(2):
        loads[blk].wait()
        for c in range(LT):
            piece = frames_ref[blk * BLOCK : (blk + 1) * BLOCK, c * 128 : (c + 1) * 128]
            buf[:, blk * LT + c] = piece.reshape(SHARDS, SUB, 128)
        send(2 + blk, blk * LT, LT)
    picked = jnp.dot(onehot, frames_ref[...], preferred_element_type=jnp.float32)
    for c in range(LT):
        piece = picked[:, c * 128 : (c + 1) * 128].reshape(SHARDS, SUB, 128)
        buf[:, 2 * LT + c] = piece.astype(jnp.bfloat16)
    send(4, 2 * LT, LT + 1)
    for copy in stores:
        copy.wait()


def pack(rank, owner, slot, frames, gpos):
    shape = (SHARDS, 3 * LT + 1, SUB, 128)
    return pl.pallas_call(
        _pack_kernel,
        out_shape=jax.ShapeDtypeStruct(shape, jnp.bfloat16),
        in_specs=[pl.BlockSpec(memory_space=SM)] * 3
        + [pl.BlockSpec(memory_space=VM), pl.BlockSpec(memory_space=pl.ANY)],
        out_specs=pl.BlockSpec(memory_space=pl.ANY),
        scratch_shapes=[
            VM((ROWS, D), jnp.bfloat16),
            VM(shape, jnp.bfloat16),
            pltpu.SemaphoreType.DMA((5,)),
        ],
        name="pack",
    )(rank, owner, slot, gpos, frames)


def _select_kernel(held_ref, out_ref, buf, sem):
    copies = []

    def send(k, dest):
        copy = pltpu.make_async_copy(buf.at[k], dest, sem.at[k])
        copy.start()
        copies.append(copy)

    codes = held_ref[:, 3 * LT].astype(jnp.float32).reshape(BLOCK, 128)
    blocks = []
    for slot in range(2):
        tiles = [
            held_ref[:, slot * LT + c].astype(jnp.float32).reshape(BLOCK, 128).astype(jnp.bfloat16)
            for c in range(LT)
        ]
        blocks.append(jnp.concatenate(tiles, axis=1))
    rows = jnp.concatenate(blocks, axis=0)
    cols = lax.broadcasted_iota(jnp.int32, (BLOCK, ROWS), 1).astype(jnp.float32)
    for c in range(LT):
        total = held_ref[0, 2 * LT + c].astype(jnp.float32)
        for i in range(1, SHARDS):
            total = total + held_ref[i, 2 * LT + c].astype(jnp.float32)
        total = total.astype(jnp.bfloat16)
        for r in range(SHARDS):
            buf[2 * PICKS, r, :, c * 128 : (c + 1) * 128] = total
    send(2 * PICKS, out_ref.at[:, 2 * PICKS])
    for k in range(2 * PICKS):
        onehot = jnp.where(cols == codes[:, k : k + 1], 1.0, 0.0).astype(jnp.bfloat16)
        got = jnp.dot(onehot, rows, preferred_element_type=jnp.float32)
        buf[k] = got.reshape(SHARDS, SUB, D).astype(jnp.bfloat16)
        send(k, out_ref.at[:, k])
    for copy in copies:
        copy.wait()


def select(held):
    return pl.pallas_call(
        _select_kernel,
        out_shape=jax.ShapeDtypeStruct((SHARDS, SUBS, SUB, D), jnp.bfloat16),
        in_specs=[pl.BlockSpec(memory_space=VM)],
        out_specs=pl.BlockSpec(memory_space=pl.ANY),
        scratch_shapes=[
            pltpu.VMEM((2 * PICKS + 1, SHARDS, SUB, D), jnp.bfloat16),
            pltpu.SemaphoreType.DMA((2 * PICKS + 1,)),
        ],
        name="select",
    )(pltpu.with_memory_space_constraint(held, VM))


def _dot(a, b):
    return jnp.dot(a, b, preferred_element_type=jnp.float32)


def _scores(query, keys):
    lanes = lax.broadcasted_iota(jnp.int32, (BLOCK, TILE), 1) // HD
    zero = jnp.zeros_like(query)
    stacked = jnp.concatenate([jnp.where(lanes == i, query, zero) for i in range(4)], axis=0)
    return lax.dot_general(
        stacked, keys, (((1,), (1,)), ((), ())), preferred_element_type=jnp.float32
    )


def _weigh(scores, values, bias):
    scores = scores + bias
    top = jnp.max(scores, axis=1, keepdims=True)
    weight = jnp.exp(scores - top).astype(jnp.bfloat16)
    ones = jnp.ones((values.shape[0], 128), jnp.bfloat16)
    low = lax.broadcasted_iota(jnp.int32, (BLOCK, 128), 1) < HD
    outs, sums, tops = [], [], []
    for pair in range(2):
        ext = jnp.concatenate([values[:, pair * 128 : (pair + 1) * 128], ones], axis=1)
        res = _dot(weight[pair * 256 : (pair + 1) * 256], ext)
        outs.append(jnp.where(low, res[:BLOCK, :128], res[BLOCK:, :128]))
        sums.append(jnp.where(low, res[:BLOCK, 128:], res[BLOCK:, 128:]))
        tops.append(
            jnp.where(
                low,
                top[pair * 256 : pair * 256 + BLOCK],
                top[pair * 256 + BLOCK : (pair + 1) * 256],
            )
        )
    return tuple(jnp.concatenate(x, axis=1) for x in (outs, sums, tops))


def _attend(query, keys, values, bias):
    return _weigh(_scores(query, keys), values, bias)


def _join(near, far):
    both = jnp.maximum(near[2], far[2])
    a = jnp.exp(near[2] - both)
    b = jnp.exp(far[2] - both)
    return a * near[0] + b * far[0], a * near[1] + b * far[1], both


def _own_kernel(
    rank_ref, len_ref, owner_ref, slot_ref, gpos_ref, own_ref, wq_ref, wk_ref, wv_ref,
    q_ref, k_ref, v_ref, bias_ref,
):
    own = own_ref[...]
    q_ref[...] = _dot(own, wq_ref[...]).astype(jnp.bfloat16) * jnp.bfloat16(0.125)
    k_ref[...] = _dot(own, wk_ref[...]).astype(jnp.bfloat16)
    v_ref[...] = _dot(own, wv_ref[...]).astype(jnp.bfloat16)

    @pl.when(pl.program_id(0) == 0)
    def _():
        live = len_ref[0]
        lane = lax.broadcasted_iota(jnp.int32, (1, 4 * BLOCK), 1)

        def row(parts):
            dead = lane < 0
            for at, block in parts:
                dead = dead | (at & ((block < 0) | (block >= live)))
            return jnp.where(dead, NEG, 0.0)

        def picked(q, j):
            return owner_ref[q, j] * 2 + slot_ref[q, j]

        for q in range(2):
            near = [(lane // BLOCK == i, rank_ref[0] * 2 + q - 1 + i) for i in range(3)]
            bias_ref[q : q + 1, :] = row(near)
        glob = jnp.where(gpos_ref[...] < live * BLOCK, 0.0, NEG)
        rows = lane // SUB
        for q in range(2):
            far = row([((rows % PICKS == j), picked(q, j)) for j in range(PICKS)])
            parts = [far[:, : PICKS * BLOCK], glob]
            bias_ref[2 + q : 3 + q, :] = jnp.concatenate(parts if q == 0 else parts[::-1], axis=1)
        bias_ref[4:8, :] = jnp.zeros((4, 4 * BLOCK), jnp.float32)


def _halo_kernel(lo_ref, hi_ref, bias_ref, q_ref, k_ref, v_ref, wk_ref, wv_ref, o_ref, l_ref, m_ref):
    rim = jnp.concatenate([lo_ref[...], hi_ref[...]], axis=0)

    def widen(own_ref, w_ref):
        far = _dot(rim, w_ref[...]).astype(jnp.bfloat16)
        return jnp.concatenate([far[:BLOCK], own_ref[...], far[BLOCK:]], axis=0)

    keys = widen(k_ref, wk_ref)
    values = widen(v_ref, wv_ref)
    for b in range(2):
        at = slice(b * BLOCK, b * BLOCK + 3 * BLOCK)
        res = _attend(
            q_ref[b * BLOCK : (b + 1) * BLOCK], keys[at], values[at], bias_ref[b : b + 1, : 3 * BLOCK]
        )
        for ref, val in zip((o_ref, l_ref, m_ref), res):
            ref[b * BLOCK : (b + 1) * BLOCK, :] = val


def _whole(shape):
    return pl.BlockSpec(shape, lambda p: (0,) * len(shape))


def _cols(rows, shift=0):
    return pl.BlockSpec((rows, TILE), lambda p: (0, p + shift))


def own_part(rank, length, owner, slot, gpos, own, w_query, w_kv):
    half = jax.ShapeDtypeStruct((ROWS, D), jnp.bfloat16)
    return pl.pallas_call(
        _own_kernel,
        grid=(STEPS,),
        out_shape=(half, half, half, jax.ShapeDtypeStruct((8, 4 * BLOCK), jnp.float32)),
        in_specs=[pl.BlockSpec(memory_space=SM)] * 4
        + [_whole((1, BLOCK)), _whole((ROWS, D)), _cols(D), _cols(D), _cols(D, STEPS)],
        out_specs=(_cols(ROWS),) * 3 + (_whole((8, 4 * BLOCK)),),
        name="own",
    )(rank, length, owner, slot, gpos, own, w_query, w_kv, w_kv)


def halo_part(lo, hi, bias, q, k, v, w_kv):
    f32 = jax.ShapeDtypeStruct((ROWS, D), jnp.float32)
    lo = pltpu.with_memory_space_constraint(lo, VM)
    hi = pltpu.with_memory_space_constraint(hi, VM)
    return pl.pallas_call(
        _halo_kernel,
        grid=(STEPS,),
        out_shape=(f32, f32, f32),
        in_specs=[
            pl.BlockSpec(memory_space=VM),
            pl.BlockSpec(memory_space=VM),
            _whole((8, 4 * BLOCK)),
            *[_cols(ROWS)] * 3,
            _cols(D),
            _cols(D, STEPS),
        ],
        out_specs=(_cols(ROWS),) * 3,
        name="halo",
    )(lo, hi, bias, q, k, v, w_kv, w_kv)


def _finish(projected, acc, gain_ref, live):
    tiles = []
    for c in range(LT):
        acc[c] = projected[:, c * 128 : (c + 1) * 128]
    for c in range(LT):
        total = acc[c, pl.ds(0, 32, stride=POOL), :]
        for i in range(1, POOL):
            total = total + acc[c, pl.ds(i, 32, stride=POOL), :]
        tiles.append(total)
    pooled = jnp.concatenate(tiles, axis=1) * (1.0 / POOL)
    mean = jnp.mean(pooled, axis=1, keepdims=True)
    centered = pooled - mean
    var = jnp.mean(centered * centered, axis=1, keepdims=True)
    normed = centered * lax.rsqrt(var + 1e-05) * gain_ref[...]
    return jnp.where(live, normed, 0.0).astype(jnp.bfloat16)


def _tile(p, base=0):
    return slice(base + p * TILE, base + (p + 1) * TILE)


def _soften(scores_ref, weight_ref, bias):
    tops = []
    for r in range(0, 4 * BLOCK, 64):
        piece = scores_ref[r : r + 64, :] + bias
        top = jnp.max(piece, axis=1, keepdims=True)
        weight_ref[r : r + 64, :] = jnp.exp(piece - top).astype(jnp.bfloat16)
        tops.append(top)
    return jnp.concatenate(tops, axis=0)


def _mix(weight_ref, values_ref, top):
    ones = jnp.ones((weight_ref.shape[1], 128), jnp.bfloat16)
    low = lax.broadcasted_iota(jnp.int32, (BLOCK, 128), 1) < HD
    outs, sums, maxes = [], [], []
    for pair in range(2):
        base = pair * 256
        ext = jnp.concatenate([values_ref[:, pair * 128 : (pair + 1) * 128], ones], axis=1)
        res = _dot(weight_ref[base : base + 256, :], ext)
        outs.append(jnp.where(low, res[:BLOCK, :128], res[BLOCK:, :128]))
        sums.append(jnp.where(low, res[:BLOCK, 128:], res[BLOCK:, 128:]))
        maxes.append(jnp.where(low, top[base : base + BLOCK], top[base + BLOCK : base + 256]))
    return tuple(jnp.concatenate(x, axis=1) for x in (outs, sums, maxes))


class _Fetch:
    def __init__(self, q_ref, o_ref, l_ref, m_ref, wkv_ref, wo_ref, bufs, sem):
        q, o, l, m, wkv, wo = bufs
        self.copies = {}
        count = 0

        def start(key, src, dst):
            nonlocal count
            copy = pltpu.make_async_copy(src, dst, sem.at[count])
            copy.start()
            self.copies[key] = copy
            count += 1

        def weights(p, base):
            at = _tile(p, base)
            start(("w", base, p), wkv_ref.at[:, at], wkv.at[:, at])

        weights(0, 0)
        start("q", q_ref, q)
        weights(0, D)
        weights(1, 0)
        for key, src, dst in (("o", o_ref, o), ("l", l_ref, l), ("m", m_ref, m)):
            start(key, src, dst)
        for p in range(1, STEPS):
            weights(p, D)
            if p + 1 < STEPS:
                weights(p + 1, 0)
        start("wo", wo_ref, wo)

    def wait(self, *keys):
        for key in keys:
            self.copies.pop(key).wait()


def _late_kernel(
    rank_ref, len_ref, rows_ref, bias_ref, q_hbm, o_hbm, l_hbm, m_hbm, wkv_hbm, wo_hbm, gain_ref,
    out_ref, acc, q_ref, o_ref, l_ref, m_ref, wkv_ref, wo_ref, sem,
    keys_ref, values_ref, scores_ref, weight_ref, context_ref,
):
    fetch = _Fetch(
        q_hbm, o_hbm, l_hbm, m_hbm, wkv_hbm, wo_hbm, (q_ref, o_ref, l_ref, m_ref, wkv_ref, wo_ref), sem
    )
    near = PICKS * BLOCK

    def keep(full, ref, p):
        full = full.reshape(SHARDS, SUBS, SUB, TILE)
        ref[p % 2, :near] = full[:, :PICKS].reshape(near, TILE).astype(jnp.bfloat16)
        ref[p % 2, near : near + BLOCK] = full[:, 2 * PICKS].reshape(BLOCK, TILE).astype(jnp.bfloat16)
        ref[p % 2, near + BLOCK :] = full[:, PICKS : 2 * PICKS].reshape(near, TILE).astype(jnp.bfloat16)

    def project(p, base):
        return _dot(rows_ref[...], wkv_ref[:, _tile(p, base)])

    fetch.wait(("w", 0, 0), ("w", D, 0))
    both = [project(0, 0), project(0, D)]
    keep(both[0], keys_ref, 0)
    keep(both[1], values_ref, 0)
    fetch.wait("q", "o", "l", "m")
    halves = [(slice(b * BLOCK, (b + 1) * BLOCK), pl.ds(b * near, near + BLOCK)) for b in range(2)]
    for p in range(STEPS):
        at = _tile(p)
        more = p + 1 < STEPS
        if more:
            fetch.wait(("w", 0, p + 1), ("w", D, p + 1))
        for b, (rows, used) in enumerate(halves):
            scores_ref[b] = _scores(q_ref[rows, at], keys_ref[p % 2, used])
        if more:
            both = [project(p + 1, 0), project(p + 1, D)]
            keep(both[0], keys_ref, p + 1)
            keep(both[1], values_ref, p + 1)
        tops = []
        for b in range(2):
            tops.append(_soften(scores_ref.at[b], weight_ref.at[b], bias_ref[2 + b : 3 + b, :]))
        for b, (rows, used) in enumerate(halves):
            far = _mix(weight_ref.at[b], values_ref.at[p % 2, used], tops[b])
            out, total, _ = _join((o_ref[rows, at], l_ref[rows, at], m_ref[rows, at]), far)
            context_ref[rows, at] = (out / total).astype(jnp.bfloat16)
    fetch.wait("wo")
    projected = _dot(context_ref[...], wo_ref[...])
    for b in range(2):
        live = rank_ref[0] * 2 + b < len_ref[0]
        part = projected[b * BLOCK : (b + 1) * BLOCK]
        out_ref[b * 32 : (b + 1) * 32, :] = _finish(part, acc.at[b], gain_ref, live)


def late(rank, length, rows, bias, q, o, l, m, w_kv, w_out, gain):
    rows = pltpu.with_memory_space_constraint(rows, VM)
    return pl.pallas_call(
        _late_kernel,
        out_shape=jax.ShapeDtypeStruct((64, D), jnp.bfloat16),
        in_specs=[
            *[pl.BlockSpec(memory_space=SM)] * 2,
            *[pl.BlockSpec(memory_space=VM)] * 2,
            *[pl.BlockSpec(memory_space=pl.ANY)] * 6,
            pl.BlockSpec(memory_space=VM),
        ],
        out_specs=pl.BlockSpec(memory_space=VM),
        scratch_shapes=[
            VM((2, LT, BLOCK, 128), jnp.float32),
            VM((ROWS, D), jnp.bfloat16),
            *[VM((ROWS, D), jnp.float32)] * 3,
            VM((D, 2 * D), jnp.bfloat16),
            VM((D, D), jnp.bfloat16),
            pltpu.SemaphoreType.DMA((2 * STEPS + 5,)),
            VM((2, SUBS * BLOCK, TILE), jnp.bfloat16),
            VM((2, SUBS * BLOCK, TILE), jnp.bfloat16),
            VM((2, 4 * BLOCK, 4 * BLOCK), jnp.float32),
            VM((2, 4 * BLOCK, 4 * BLOCK), jnp.bfloat16),
            VM((ROWS, D), jnp.bfloat16),
        ],
        name="late",
    )(rank, length, rows, bias, q, o, l, m, w_kv, w_out, gain)


def exchange(value):
    return lax.all_to_all(value, "tm", split_axis=0, concat_axis=0, tiled=True)


def program(frames, w_query, w_kv, w_out, norm_gain, rand_owner, rand_slot, global_pos, length):
    shards = lax.axis_size("tm")
    rank = lax.axis_index("tm").astype(jnp.int32).reshape(1)
    gpos = global_pos.reshape(1, BLOCK)
    gain = norm_gain.reshape(1, D)
    up = [(i, i + 1) for i in range(shards - 1)]
    down = [(j, i) for i, j in up]
    packed = pack(rank, rand_owner, rand_slot, frames, gpos)
    held = exchange(packed)
    q, k, v, bias = own_part(rank, length, rand_owner, rand_slot, gpos, frames, w_query, w_kv)
    lo = lax.ppermute(frames[BLOCK:], "tm", up)
    hi = lax.ppermute(frames[:BLOCK], "tm", down)
    reply = select(held)
    got = exchange(reply).reshape(SUBS * BLOCK, D)
    o, l, m = halo_part(lo, hi, bias, q, k, v, w_kv)
    return late(rank, length, got, bias, q, o, l, m, w_kv, w_out, gain)


def solution(mesh):
    placed = (
        P(("rec", "tm"), None),
        P(),
        P(),
        P(),
        P(),
        P(("rec", "tm"), None),
        P(("rec", "tm"), None),
        P("rec"),
        P("rec"),
    )
    return jax.shard_map(
        program, mesh=mesh, in_specs=placed, out_specs=P(("rec", "tm"), None), check_vma=False
    )
```

```python
import jax
import jax.numpy as jnp
from jax import lax
from jax.experimental import pallas as pl
from jax.experimental.pallas import tpu as pltpu
from jax.sharding import PartitionSpec as P


BLOCK = 128
POOL = 4
PICKS = 3
D = 1280
HD = 64
TILE = 256
STEPS = D // TILE
SHARDS = 16
SUB = BLOCK // SHARDS
ROWS = 256
SUBS = 2 * PICKS + 1
LT = D // 128
NEG = -1e30

VM = pltpu.VMEM
SM = pltpu.SMEM


def _pack_kernel(rank_ref, owner_ref, slot_ref, frames_ref, gpos_ref, out_ref):
    frames = frames_ref[...]
    for blk in range(2):
        for c in range(LT):
            piece = frames_ref[blk * BLOCK : (blk + 1) * BLOCK, c * 128 : (c + 1) * 128]
            out_ref[:, blk * LT + c] = piece.reshape(SHARDS, SUB, 128)
    local = (gpos_ref[...] - rank_ref[0] * ROWS).astype(jnp.float32)
    local = jnp.broadcast_to(local, (8, BLOCK)).T[:, :1]
    cols = lax.broadcasted_iota(jnp.int32, (BLOCK, ROWS), 1).astype(jnp.float32)
    onehot = jnp.where(cols == local, 1.0, 0.0).astype(jnp.bfloat16)
    picked = jnp.dot(onehot, frames, preferred_element_type=jnp.float32)
    for c in range(LT):
        piece = picked[:, c * 128 : (c + 1) * 128].reshape(SHARDS, SUB, 128)
        out_ref[:, 2 * LT + c] = piece.astype(jnp.bfloat16)
    lane = lax.broadcasted_iota(jnp.int32, (SUB, 128), 1)
    codes = jnp.zeros((SUB, 128), jnp.int32)
    for q in range(2):
        for j in range(PICKS):
            code = (slot_ref[q, j] * SHARDS + owner_ref[q, j]) * SUB
            codes = jnp.where(lane == q * PICKS + j, code, codes)
    codes = codes + lax.broadcasted_iota(jnp.int32, (SUB, 128), 0)
    codes = codes.astype(jnp.float32).astype(jnp.bfloat16)
    for s in range(SHARDS):
        out_ref[s, 3 * LT] = codes


def pack(rank, owner, slot, frames, gpos):
    return pl.pallas_call(
        _pack_kernel,
        out_shape=VM((SHARDS, 3 * LT + 1, SUB, 128), jnp.bfloat16),
        in_specs=[pl.BlockSpec(memory_space=SM)] * 3 + [pl.BlockSpec(memory_space=VM)] * 2,
        out_specs=pl.BlockSpec(memory_space=VM),
        name="pack",
    )(rank, owner, slot, frames, gpos)


def _select_kernel(held_ref, out_ref, buf, sem):
    copies = []

    def send(k, dest):
        copy = pltpu.make_async_copy(buf.at[k], dest, sem.at[k])
        copy.start()
        copies.append(copy)

    codes = held_ref[:, 3 * LT].astype(jnp.float32).reshape(BLOCK, 128)
    blocks = []
    for slot in range(2):
        tiles = [
            held_ref[:, slot * LT + c].astype(jnp.float32).reshape(BLOCK, 128).astype(jnp.bfloat16)
            for c in range(LT)
        ]
        blocks.append(jnp.concatenate(tiles, axis=1))
    rows = jnp.concatenate(blocks, axis=0)
    cols = lax.broadcasted_iota(jnp.int32, (BLOCK, ROWS), 1).astype(jnp.float32)
    for c in range(LT):
        total = held_ref[0, 2 * LT + c].astype(jnp.float32)
        for i in range(1, SHARDS):
            total = total + held_ref[i, 2 * LT + c].astype(jnp.float32)
        total = total.astype(jnp.bfloat16)
        for r in range(SHARDS):
            buf[2 * PICKS, r, :, c * 128 : (c + 1) * 128] = total
    send(2 * PICKS, out_ref.at[:, 2 * PICKS])
    for k in range(2 * PICKS):
        onehot = jnp.where(cols == codes[:, k : k + 1], 1.0, 0.0).astype(jnp.bfloat16)
        got = jnp.dot(onehot, rows, preferred_element_type=jnp.float32)
        buf[k] = got.reshape(SHARDS, SUB, D).astype(jnp.bfloat16)
        send(k, out_ref.at[:, k])
    for copy in copies:
        copy.wait()


def select(held):
    return pl.pallas_call(
        _select_kernel,
        out_shape=jax.ShapeDtypeStruct((SHARDS, SUBS, SUB, D), jnp.bfloat16),
        in_specs=[pl.BlockSpec(memory_space=VM)],
        out_specs=pl.BlockSpec(memory_space=pl.ANY),
        scratch_shapes=[
            pltpu.VMEM((2 * PICKS + 1, SHARDS, SUB, D), jnp.bfloat16),
            pltpu.SemaphoreType.DMA((2 * PICKS + 1,)),
        ],
        name="select",
    )(pltpu.with_memory_space_constraint(held, VM))


def _dot(a, b):
    return jnp.dot(a, b, preferred_element_type=jnp.float32)


def _scores(query, keys):
    lanes = lax.broadcasted_iota(jnp.int32, (BLOCK, TILE), 1) // HD
    zero = jnp.zeros_like(query)
    stacked = jnp.concatenate([jnp.where(lanes == i, query, zero) for i in range(4)], axis=0)
    return lax.dot_general(
        stacked, keys, (((1,), (1,)), ((), ())), preferred_element_type=jnp.float32
    )


def _weigh(scores, values, bias):
    scores = scores + bias
    top = jnp.max(scores, axis=1, keepdims=True)
    weight = jnp.exp(scores - top).astype(jnp.bfloat16)
    ones = jnp.ones((values.shape[0], 128), jnp.bfloat16)
    low = lax.broadcasted_iota(jnp.int32, (BLOCK, 128), 1) < HD
    outs, sums, tops = [], [], []
    for pair in range(2):
        ext = jnp.concatenate([values[:, pair * 128 : (pair + 1) * 128], ones], axis=1)
        res = _dot(weight[pair * 256 : (pair + 1) * 256], ext)
        outs.append(jnp.where(low, res[:BLOCK, :128], res[BLOCK:, :128]))
        sums.append(jnp.where(low, res[:BLOCK, 128:], res[BLOCK:, 128:]))
        tops.append(
            jnp.where(
                low,
                top[pair * 256 : pair * 256 + BLOCK],
                top[pair * 256 + BLOCK : (pair + 1) * 256],
            )
        )
    return tuple(jnp.concatenate(x, axis=1) for x in (outs, sums, tops))


def _attend(query, keys, values, bias):
    return _weigh(_scores(query, keys), values, bias)


def _join(near, far):
    both = jnp.maximum(near[2], far[2])
    a = jnp.exp(near[2] - both)
    b = jnp.exp(far[2] - both)
    return a * near[0] + b * far[0], a * near[1] + b * far[1], both


def _own_kernel(
    rank_ref, len_ref, owner_ref, slot_ref, gpos_ref, own_ref, wq_ref, wk_ref, wv_ref,
    q_ref, k_ref, v_ref, bias_ref,
):
    own = own_ref[...]
    q_ref[...] = _dot(own, wq_ref[...]).astype(jnp.bfloat16) * jnp.bfloat16(0.125)
    k_ref[...] = _dot(own, wk_ref[...]).astype(jnp.bfloat16)
    v_ref[...] = _dot(own, wv_ref[...]).astype(jnp.bfloat16)

    @pl.when(pl.program_id(0) == 0)
    def _():
        live = len_ref[0]
        lane = lax.broadcasted_iota(jnp.int32, (1, 4 * BLOCK), 1)

        def row(parts):
            dead = lane < 0
            for at, block in parts:
                dead = dead | (at & ((block < 0) | (block >= live)))
            return jnp.where(dead, NEG, 0.0)

        def picked(q, j):
            return owner_ref[q, j] * 2 + slot_ref[q, j]

        for q in range(2):
            near = [(lane // BLOCK == i, rank_ref[0] * 2 + q - 1 + i) for i in range(3)]
            bias_ref[q : q + 1, :] = row(near)
        glob = jnp.where(gpos_ref[...] < live * BLOCK, 0.0, NEG)
        rows = lane // SUB
        for q in range(2):
            far = row([((rows % PICKS == j), picked(q, j)) for j in range(PICKS)])
            parts = [far[:, : PICKS * BLOCK], glob]
            bias_ref[2 + q : 3 + q, :] = jnp.concatenate(parts if q == 0 else parts[::-1], axis=1)
        bias_ref[4:8, :] = jnp.zeros((4, 4 * BLOCK), jnp.float32)


def _halo_kernel(lo_ref, hi_ref, bias_ref, q_ref, k_ref, v_ref, wk_ref, wv_ref, o_ref, l_ref, m_ref):
    rim = jnp.concatenate([lo_ref[...], hi_ref[...]], axis=0)

    def widen(own_ref, w_ref):
        far = _dot(rim, w_ref[...]).astype(jnp.bfloat16)
        return jnp.concatenate([far[:BLOCK], own_ref[...], far[BLOCK:]], axis=0)

    keys = widen(k_ref, wk_ref)
    values = widen(v_ref, wv_ref)
    for b in range(2):
        at = slice(b * BLOCK, b * BLOCK + 3 * BLOCK)
        res = _attend(
            q_ref[b * BLOCK : (b + 1) * BLOCK], keys[at], values[at], bias_ref[b : b + 1, : 3 * BLOCK]
        )
        for ref, val in zip((o_ref, l_ref, m_ref), res):
            ref[b * BLOCK : (b + 1) * BLOCK, :] = val


def _whole(shape):
    return pl.BlockSpec(shape, lambda p: (0,) * len(shape))


def _cols(rows, shift=0):
    return pl.BlockSpec((rows, TILE), lambda p: (0, p + shift))


def own_part(rank, length, owner, slot, gpos, own, w_query, w_kv):
    half = jax.ShapeDtypeStruct((ROWS, D), jnp.bfloat16)
    return pl.pallas_call(
        _own_kernel,
        grid=(STEPS,),
        out_shape=(half, half, half, jax.ShapeDtypeStruct((8, 4 * BLOCK), jnp.float32)),
        in_specs=[pl.BlockSpec(memory_space=SM)] * 4
        + [_whole((1, BLOCK)), _whole((ROWS, D)), _cols(D), _cols(D), _cols(D, STEPS)],
        out_specs=(_cols(ROWS),) * 3 + (_whole((8, 4 * BLOCK)),),
        name="own",
    )(rank, length, owner, slot, gpos, own, w_query, w_kv, w_kv)


def halo_part(lo, hi, bias, q, k, v, w_kv):
    f32 = jax.ShapeDtypeStruct((ROWS, D), jnp.float32)
    lo = pltpu.with_memory_space_constraint(lo, VM)
    hi = pltpu.with_memory_space_constraint(hi, VM)
    return pl.pallas_call(
        _halo_kernel,
        grid=(STEPS,),
        out_shape=(f32, f32, f32),
        in_specs=[
            pl.BlockSpec(memory_space=VM),
            pl.BlockSpec(memory_space=VM),
            _whole((8, 4 * BLOCK)),
            *[_cols(ROWS)] * 3,
            _cols(D),
            _cols(D, STEPS),
        ],
        out_specs=(_cols(ROWS),) * 3,
        name="halo",
    )(lo, hi, bias, q, k, v, w_kv, w_kv)


def _finish(projected, acc, gain_ref, live):
    tiles = []
    for c in range(LT):
        acc[c] = projected[:, c * 128 : (c + 1) * 128]
    for c in range(LT):
        total = acc[c, pl.ds(0, 32, stride=POOL), :]
        for i in range(1, POOL):
            total = total + acc[c, pl.ds(i, 32, stride=POOL), :]
        tiles.append(total)
    pooled = jnp.concatenate(tiles, axis=1) * (1.0 / POOL)
    mean = jnp.mean(pooled, axis=1, keepdims=True)
    centered = pooled - mean
    var = jnp.mean(centered * centered, axis=1, keepdims=True)
    normed = centered * lax.rsqrt(var + 1e-05) * gain_ref[...]
    return jnp.where(live, normed, 0.0).astype(jnp.bfloat16)


def _tile(p, base=0):
    return slice(base + p * TILE, base + (p + 1) * TILE)


def _soften(scores_ref, weight_ref, bias):
    tops = []
    for r in range(0, 4 * BLOCK, 64):
        piece = scores_ref[r : r + 64, :] + bias
        top = jnp.max(piece, axis=1, keepdims=True)
        weight_ref[r : r + 64, :] = jnp.exp(piece - top).astype(jnp.bfloat16)
        tops.append(top)
    return jnp.concatenate(tops, axis=0)


def _mix(weight_ref, values_ref, top):
    ones = jnp.ones((weight_ref.shape[1], 128), jnp.bfloat16)
    low = lax.broadcasted_iota(jnp.int32, (BLOCK, 128), 1) < HD
    outs, sums, maxes = [], [], []
    for pair in range(2):
        base = pair * 256
        ext = jnp.concatenate([values_ref[:, pair * 128 : (pair + 1) * 128], ones], axis=1)
        res = _dot(weight_ref[base : base + 256, :], ext)
        outs.append(jnp.where(low, res[:BLOCK, :128], res[BLOCK:, :128]))
        sums.append(jnp.where(low, res[:BLOCK, 128:], res[BLOCK:, 128:]))
        maxes.append(jnp.where(low, top[base : base + BLOCK], top[base + BLOCK : base + 256]))
    return tuple(jnp.concatenate(x, axis=1) for x in (outs, sums, maxes))


class _Fetch:
    def __init__(self, q_ref, o_ref, l_ref, m_ref, wkv_ref, wo_ref, bufs, sem):
        q, o, l, m, wkv, wo = bufs
        self.copies = {}
        count = 0

        def start(key, src, dst):
            nonlocal count
            copy = pltpu.make_async_copy(src, dst, sem.at[count])
            copy.start()
            self.copies[key] = copy
            count += 1

        def weights(p, base):
            at = _tile(p, base)
            start(("w", base, p), wkv_ref.at[:, at], wkv.at[:, at])

        weights(0, 0)
        weights(0, D)
        start("q", q_ref, q)
        weights(1, 0)
        for key, src, dst in (("o", o_ref, o), ("l", l_ref, l), ("m", m_ref, m)):
            start(key, src, dst)
        for p in range(1, STEPS):
            weights(p, D)
            if p + 1 < STEPS:
                weights(p + 1, 0)
        start("wo", wo_ref, wo)

    def wait(self, *keys):
        for key in keys:
            self.copies.pop(key).wait()


def _late_kernel(
    rank_ref, len_ref, rows_ref, bias_ref, q_hbm, o_hbm, l_hbm, m_hbm, wkv_hbm, wo_hbm, gain_ref,
    out_ref, acc, q_ref, o_ref, l_ref, m_ref, wkv_ref, wo_ref, sem,
    keys_ref, values_ref, scores_ref, weight_ref, context_ref,
):
    fetch = _Fetch(
        q_hbm, o_hbm, l_hbm, m_hbm, wkv_hbm, wo_hbm, (q_ref, o_ref, l_ref, m_ref, wkv_ref, wo_ref), sem
    )
    near = PICKS * BLOCK

    def keep(full, ref, p):
        full = full.reshape(SHARDS, SUBS, SUB, TILE)
        ref[p % 2, :near] = full[:, :PICKS].reshape(near, TILE).astype(jnp.bfloat16)
        ref[p % 2, near : near + BLOCK] = full[:, 2 * PICKS].reshape(BLOCK, TILE).astype(jnp.bfloat16)
        ref[p % 2, near + BLOCK :] = full[:, PICKS : 2 * PICKS].reshape(near, TILE).astype(jnp.bfloat16)

    def project(p, base):
        return _dot(rows_ref[...], wkv_ref[:, _tile(p, base)])

    fetch.wait(("w", 0, 0), ("w", D, 0))
    both = [project(0, 0), project(0, D)]
    keep(both[0], keys_ref, 0)
    keep(both[1], values_ref, 0)
    fetch.wait("q", "o", "l", "m")
    halves = [(slice(b * BLOCK, (b + 1) * BLOCK), pl.ds(b * near, near + BLOCK)) for b in range(2)]
    for p in range(STEPS):
        at = _tile(p)
        more = p + 1 < STEPS
        if more:
            fetch.wait(("w", 0, p + 1), ("w", D, p + 1))
        for b, (rows, used) in enumerate(halves):
            scores_ref[b] = _scores(q_ref[rows, at], keys_ref[p % 2, used])
        if more:
            both = [project(p + 1, 0), project(p + 1, D)]
            keep(both[0], keys_ref, p + 1)
            keep(both[1], values_ref, p + 1)
        tops = []
        for b in range(2):
            tops.append(_soften(scores_ref.at[b], weight_ref.at[b], bias_ref[2 + b : 3 + b, :]))
        for b, (rows, used) in enumerate(halves):
            far = _mix(weight_ref.at[b], values_ref.at[p % 2, used], tops[b])
            out, total, _ = _join((o_ref[rows, at], l_ref[rows, at], m_ref[rows, at]), far)
            context_ref[rows, at] = (out / total).astype(jnp.bfloat16)
    fetch.wait("wo")
    projected = _dot(context_ref[...], wo_ref[...])
    for b in range(2):
        live = rank_ref[0] * 2 + b < len_ref[0]
        part = projected[b * BLOCK : (b + 1) * BLOCK]
        out_ref[b * 32 : (b + 1) * 32, :] = _finish(part, acc.at[b], gain_ref, live)


def late(rank, length, rows, bias, q, o, l, m, w_kv, w_out, gain):
    rows = pltpu.with_memory_space_constraint(rows, VM)
    return pl.pallas_call(
        _late_kernel,
        out_shape=jax.ShapeDtypeStruct((64, D), jnp.bfloat16),
        in_specs=[
            *[pl.BlockSpec(memory_space=SM)] * 2,
            *[pl.BlockSpec(memory_space=VM)] * 2,
            *[pl.BlockSpec(memory_space=pl.ANY)] * 6,
            pl.BlockSpec(memory_space=VM),
        ],
        out_specs=pl.BlockSpec(memory_space=VM),
        scratch_shapes=[
            VM((2, LT, BLOCK, 128), jnp.float32),
            VM((ROWS, D), jnp.bfloat16),
            *[VM((ROWS, D), jnp.float32)] * 3,
            VM((D, 2 * D), jnp.bfloat16),
            VM((D, D), jnp.bfloat16),
            pltpu.SemaphoreType.DMA((2 * STEPS + 5,)),
            VM((2, SUBS * BLOCK, TILE), jnp.bfloat16),
            VM((2, SUBS * BLOCK, TILE), jnp.bfloat16),
            VM((2, 4 * BLOCK, 4 * BLOCK), jnp.float32),
            VM((2, 4 * BLOCK, 4 * BLOCK), jnp.bfloat16),
            VM((ROWS, D), jnp.bfloat16),
        ],
        name="late",
    )(rank, length, rows, bias, q, o, l, m, w_kv, w_out, gain)


def exchange(value):
    return lax.all_to_all(value, "tm", split_axis=0, concat_axis=0, tiled=True)


def program(frames, w_query, w_kv, w_out, norm_gain, rand_owner, rand_slot, global_pos, length):
    shards = lax.axis_size("tm")
    rank = lax.axis_index("tm").astype(jnp.int32).reshape(1)
    gpos = global_pos.reshape(1, BLOCK)
    gain = norm_gain.reshape(1, D)
    up = [(i, i + 1) for i in range(shards - 1)]
    down = [(j, i) for i, j in up]
    packed = pack(rank, rand_owner, rand_slot, frames, gpos)
    held = exchange(packed)
    q, k, v, bias = own_part(rank, length, rand_owner, rand_slot, gpos, frames, w_query, w_kv)
    lo = lax.ppermute(frames[BLOCK:], "tm", up)
    hi = lax.ppermute(frames[:BLOCK], "tm", down)
    reply = select(held)
    got = exchange(reply).reshape(SUBS * BLOCK, D)
    o, l, m = halo_part(lo, hi, bias, q, k, v, w_kv)
    return late(rank, length, got, bias, q, o, l, m, w_kv, w_out, gain)


def solution(mesh):
    placed = (
        P(("rec", "tm"), None),
        P(),
        P(),
        P(),
        P(),
        P(("rec", "tm"), None),
        P(("rec", "tm"), None),
        P("rec"),
        P("rec"),
    )
    return jax.shard_map(
        program, mesh=mesh, in_specs=placed, out_specs=P(("rec", "tm"), None), check_vma=False
    )
```
